32 devices in a mesh: rep: 4 (over x, core), fsdp: 2 (over y), tp: 4 (over z).
Axes of the slice: x: 2, y: 2, z: 4, core: 2. Of those that a mesh axis runs over, the one named last changes fastest.
Arguments:
- image_input: bfloat16 [8, 896, 1536], P(('rep', 'fsdp'), 'tp'), may hold values from -6 to 6
- text_input: bfloat16 [8, 128, 1536], P(('rep', 'fsdp'), 'tp'), may hold values from -6 to 6
- cond: float32 [8, 1536], P(('rep', 'fsdp')), may hold values from -6 to 6
- image_cotangent: bfloat16 [8, 896, 1536], P(('rep', 'fsdp'), 'tp'), may hold values from -6 to 6
- text_cotangent: bfloat16 [8, 128, 1536], P(('rep', 'fsdp'), 'tp'), may hold values from -6 to 6
- live: int32 [8], P(('rep', 'fsdp')), may hold values from 0 to 1, as said below
- slot_adapter_index: int32 [8], P(('rep', 'fsdp')), may hold values from 0 to 7
- modulation_weight: bfloat16 [2, 1536, 6, 1536], P(None, 'fsdp', None, 'tp'), may hold values from -0.15625 to 0.15625
- query_key_value_weight: bfloat16 [2, 1536, 3, 1536], P(None, 'fsdp', None, 'tp'), may hold values from -0.15625 to 0.15625
- output_weight: bfloat16 [2, 1536, 1536], P(None, 'tp', 'fsdp'), may hold values from -0.625 to 0.625
- first_feed_weight: bfloat16 [2, 1536, 6144], P(None, 'fsdp', 'tp'), may hold values from -0.15625 to 0.15625
- second_feed_weight: bfloat16 [2, 6144, 1536], P(None, 'tp', 'fsdp'), may hold values from -0.078125 to 0.078125
- adapter_down_table: bfloat16 [3, 2, 128, 1536], P(None, None, ('fsdp', 'tp')), may hold values from -0.15625 to 0.15625
- adapter_up_table: bfloat16 [2, 2, 128, 1536], P(None, None, ('fsdp', 'tp')), may hold values from -1.5 to 1.5
- modulation_up_factor: bfloat16 [2, 128, 6, 1536], P(None, 'fsdp', None, 'tp'), may hold values from -1.5 to 1.5
- query_key_value_up: bfloat16 [2, 128, 3, 1536], P(None, 'fsdp', None, 'tp'), may hold values from -1.5 to 1.5
- first_feed_up: bfloat16 [2, 128, 6144], P(None, 'fsdp', 'tp'), may hold values from -1.5 to 1.5
- output_down_factor: bfloat16 [2, 128, 1536], P(None, 'fsdp', 'tp'), may hold values from -0.625 to 0.625
- second_feed_down: bfloat16 [2, 128, 6144], P(None, 'fsdp', 'tp'), may hold values from -0.078125 to 0.078125
Outputs:
- out_img: bfloat16 [8, 896, 1536], P(('rep', 'fsdp'), 'tp')
- out_txt: bfloat16 [8, 128, 1536], P(('rep', 'fsdp'), 'tp')
- dx_img: bfloat16 [8, 896, 1536], P(('rep', 'fsdp'), 'tp')
- dx_txt: bfloat16 [8, 128, 1536], P(('rep', 'fsdp'), 'tp')
- dcond: float32 [8, 1536], P(('rep', 'fsdp'))
- grad_lora_in: float32 [3, 2, 128, 1536], P(None, None, ('fsdp', 'tp'))
- grad_lora_back: float32 [2, 2, 128, 1536], P(None, None, ('fsdp', 'tp'))
- grad_b_ada: float32 [2, 128, 6, 1536], P(None, 'fsdp', None, 'tp')
- grad_b_qkv: float32 [2, 128, 3, 1536], P(None, 'fsdp', None, 'tp')
- grad_b_fc1: float32 [2, 128, 6144], P(None, 'fsdp', 'tp')
- output_down_gradient: float32 [2, 128, 1536], P(None, 'fsdp', 'tp')
- grad_a_fc2: float32 [2, 128, 6144], P(None, 'fsdp', 'tp')
The draws below stay inside these ranges and needn't reach their ends.
Inputs may be any that keep to these rules, and one draw needn't show every extreme that they name: `live`: slot 0 of each aligned block of 1 slots always holds a sequence; the others may be empty.
All inputs are finite; a program needn't handle non-finite values.
Results may differ from the reference program's by a relative error of at most 0.025.
The reference program's roundings to bfloat16 on the way count: a program that leaves them out, or rounds other values in their place, can miss the bound.
Values may be sent and summed in bfloat16 or wider, within the bound.
No kernel may reach another device: no remote copies, remote signals or barrier semaphores. Data moves between devices by JAX's collectives and lax.ppermute only.
A program may use at most 320 MiB of HBM per device.

```python
import jax
import jax.numpy as jnp
from jax import lax

MODEL_WIDTH = 1536
HEADS = 24
HD = 64
FF = 6144
ADAPTER_RANK = 16
ADAPTER_COUNT = 8
LI = 896
LT = 128
SLOTS = 1
SLOTS_ALL = 8


def draw_live(key, part):
    coin_flips = jax.random.randint(key, (SLOTS_ALL,), 0, 2)
    first_slot = jnp.arange(SLOTS_ALL) % SLOTS == 0
    return jnp.where(first_slot, 1, coin_flips).astype(jnp.int32)


def set_ends(drawn, key, low, largest):
    spot = [jax.random.randint(jax.random.fold_in(key, axis), (), 0, length) for axis, length in enumerate(drawn.shape)]
    widest = drawn.shape.index(max(drawn.shape))
    neighbour = spot[:widest] + [(spot[widest] + 1) % drawn.shape[widest]] + spot[widest + 1:]
    return drawn.at[tuple(spot)].set(low).at[tuple(neighbour)].set(largest)


def shard_levels(own_key, extent, cuts, least, largest):
    loudness, own = 1.0, jax.random.fold_in(own_key, 6)
    for position, shards_of in cuts:
        steps = jnp.exp(jax.random.uniform(jax.random.fold_in(own, position), (shards_of,), jnp.float32, least / len(cuts), largest / len(cuts)))
        loudness = loudness * jnp.repeat(steps, extent[position] // shards_of).reshape([-1 if axis == position else 1 for axis in range(len(extent))])
    return loudness


def bell_draw(stream_key, shape, width, bound, cuts=(), kind=jnp.bfloat16):
    drawn = jax.random.normal(stream_key, shape, jnp.float32) * width
    if len(cuts) > 0:
        drawn = shard_levels(stream_key, shape, cuts, -0.22, 0.18) * drawn
    return jnp.clip(drawn, min=-bound, max=bound).astype(kind)


def setup_inputs(seed: int = 0) -> dict:
    key_of = jax.random.split(jax.random.key(seed), 20)
    return {
        "image_input": bell_draw(key_of[0], (SLOTS_ALL, LI, MODEL_WIDTH), 1.0, 6.0, ((0, 8), (1, 4))),
        "text_input": bell_draw(key_of[1], (SLOTS_ALL, LT, MODEL_WIDTH), 1.0, 6.0, ((0, 8), (1, 4))),
        "cond": bell_draw(key_of[2], (SLOTS_ALL, MODEL_WIDTH), 1.0, 6.0, ((0, 8),), jnp.float32),
        "image_cotangent": bell_draw(key_of[3], (SLOTS_ALL, LI, MODEL_WIDTH), 1.0, 6.0, ((0, 8), (1, 4))),
        "text_cotangent": bell_draw(key_of[4], (SLOTS_ALL, LT, MODEL_WIDTH), 1.0, 6.0, ((0, 8), (1, 4))),
        "live": draw_live(jax.random.fold_in(key_of[19], 71), 0),
        "slot_adapter_index": set_ends(jax.random.randint(key_of[6], (SLOTS_ALL,), 0, ADAPTER_COUNT), jax.random.fold_in(key_of[6], 1), 0, ADAPTER_COUNT - 1).astype(jnp.int32),
        "modulation_weight": bell_draw(key_of[7], (2, MODEL_WIDTH, 6, MODEL_WIDTH), MODEL_WIDTH ** -0.5, 0.15625, ((1, 2), (3, 4))),
        "query_key_value_weight": bell_draw(key_of[8], (2, MODEL_WIDTH, 3, MODEL_WIDTH), MODEL_WIDTH ** -0.5, 0.15625, ((1, 2), (3, 4))),
        "output_weight": bell_draw(key_of[9], (2, MODEL_WIDTH, MODEL_WIDTH), (MODEL_WIDTH // 16) ** -0.5, 0.625, ((1, 4), (2, 2))),
        "first_feed_weight": bell_draw(key_of[10], (2, MODEL_WIDTH, FF), MODEL_WIDTH ** -0.5, 0.15625, ((1, 2), (2, 4))),
        "second_feed_weight": bell_draw(key_of[11], (2, FF, MODEL_WIDTH), FF ** -0.5, 0.078125, ((1, 4), (2, 2))),
        "adapter_down_table": bell_draw(key_of[12], (3, 2, ADAPTER_COUNT * ADAPTER_RANK, MODEL_WIDTH), MODEL_WIDTH ** -0.5, 0.15625, ((2, 8),)),
        "adapter_up_table": bell_draw(key_of[13], (2, 2, ADAPTER_COUNT * ADAPTER_RANK, MODEL_WIDTH), ADAPTER_RANK ** -0.5, 1.5, ((2, 8),)),
        "modulation_up_factor": bell_draw(key_of[14], (2, ADAPTER_COUNT * ADAPTER_RANK, 6, MODEL_WIDTH), ADAPTER_RANK ** -0.5, 1.5, ((1, 2), (3, 4))),
        "query_key_value_up": bell_draw(key_of[15], (2, ADAPTER_COUNT * ADAPTER_RANK, 3, MODEL_WIDTH), ADAPTER_RANK ** -0.5, 1.5, ((1, 2), (3, 4))),
        "first_feed_up": bell_draw(key_of[16], (2, ADAPTER_COUNT * ADAPTER_RANK, FF), ADAPTER_RANK ** -0.5, 1.5, ((1, 2), (2, 4))),
        "output_down_factor": bell_draw(key_of[17], (2, ADAPTER_COUNT * ADAPTER_RANK, MODEL_WIDTH), (MODEL_WIDTH // 16) ** -0.5, 0.625, ((1, 2), (2, 4))),
        "second_feed_down": bell_draw(key_of[18], (2, ADAPTER_COUNT * ADAPTER_RANK, FF), FF ** -0.5, 0.078125, ((1, 2), (2, 4))),
    }


highest = lax.Precision.HIGHEST

@jax.custom_vjp
def lowrank_value(v):
    return lax.optimization_barrier(v.astype(jnp.bfloat16)).astype(jnp.float32)

@jax.custom_vjp
def lowrank_backward(v):
    return v

def low_keep(v):
    return (lowrank_value(v), None)

def low_pass(kept, grad):
    return (grad,)

def back_keep(v):
    return (v, None)

def back_low(kept, grad):
    return (lowrank_value(grad),)
lowrank_value.defvjp(low_keep, low_pass)
lowrank_backward.defvjp(back_keep, back_low)

def norm_rows(values):
    centred = values - lax.optimization_barrier(jnp.mean(values, axis=-1, keepdims=True))
    variance = lax.optimization_barrier(jnp.mean(centred * centred, axis=-1, keepdims=True))
    return centred * lax.rsqrt(variance + 1e-06)

def matrix_product(left, right):
    return jnp.dot(left, right, precision=highest)

def block_forward(image_token_rows, text_token_rows, condition_vector, adapter_down_table, adapter_up_table, modulation_up_factor, query_key_value_up, first_feed_up, output_down_factor, second_feed_down, frozen_weights):
    modulation_weight, query_key_value_weight, output_weight, first_feed_weight, second_feed_weight = frozen_weights
    condition_lowrank = lowrank_value(jax.nn.silu(condition_vector))
    streams = (image_token_rows, text_token_rows)
    mod_list = []
    joint_list = []
    for stream_index in range(2):
        condition_ranked = lowrank_value(matrix_product(adapter_down_table[0, stream_index], condition_lowrank))
        mod_rows = jnp.einsum('d,dcj->cj', condition_lowrank, modulation_weight[stream_index], precision=highest)
        mod_rows = mod_rows + jnp.einsum('r,rcj->cj', condition_ranked, modulation_up_factor[stream_index], precision=highest)
        mod_rows = lowrank_backward(mod_rows)
        mod_list.append(mod_rows)
        normed_tokens = lowrank_value(norm_rows(streams[stream_index]) * (1.0 + mod_rows[1]) + mod_rows[0])
        query_key_value_ranked = lowrank_backward(lowrank_value(matrix_product(normed_tokens, adapter_down_table[1, stream_index].T)))
        combined_rows = jnp.einsum('ld,dcj->lcj', normed_tokens, query_key_value_weight[stream_index], precision=highest)
        combined_rows = combined_rows + jnp.einsum('lr,rcj->lcj', query_key_value_ranked, query_key_value_up[stream_index], precision=highest)
        joint_list.append(lowrank_backward(lowrank_value(combined_rows)))
    joint_all = jnp.concatenate([joint_list[1], joint_list[0]], axis=0)
    length = joint_all.shape[0]
    queries = joint_all[:, 0].reshape(length, HEADS, HD)
    key_rows = joint_all[:, 1].reshape(length, HEADS, HD)
    values = joint_all[:, 2].reshape(length, HEADS, HD)
    scores = lowrank_backward(jnp.einsum('qhd,khd->hqk', queries, key_rows, precision=highest) * HD ** (-0.5))
    probabilities = lowrank_value(jax.nn.softmax(scores, axis=-1))
    attended = jnp.einsum('hqk,khd->qhd', probabilities, values, precision=highest).reshape(length, MODEL_WIDTH)
    attended = lowrank_backward(lowrank_value(attended))
    text_len = text_token_rows.shape[0]
    split_rows = (attended[text_len:], attended[:text_len])
    results = []
    for stream_index in range(2):
        mod_rows = mod_list[stream_index]
        segment_rows = split_rows[stream_index]
        output_ranked = lowrank_backward(lowrank_value(matrix_product(segment_rows, output_down_factor[stream_index].T)))
        attention_branch = lowrank_backward(matrix_product(segment_rows, output_weight[stream_index]) + matrix_product(output_ranked, adapter_up_table[0, stream_index]))
        after_attn = streams[stream_index] + mod_rows[2] * attention_branch
        normed_feedforward = lowrank_value(norm_rows(after_attn) * (1.0 + mod_rows[4]) + mod_rows[3])
        first_feed_ranked = lowrank_backward(lowrank_value(matrix_product(normed_feedforward, adapter_down_table[2, stream_index].T)))
        hidden_state = lowrank_backward(matrix_product(normed_feedforward, first_feed_weight[stream_index]) + matrix_product(first_feed_ranked, first_feed_up[stream_index]))
        activation_rows = lowrank_value(jax.nn.gelu(hidden_state, approximate=True))
        second_feed_ranked = lowrank_backward(lowrank_value(matrix_product(activation_rows, second_feed_down[stream_index].T)))
        feedforward_branch = lowrank_backward(matrix_product(activation_rows, second_feed_weight[stream_index]) + matrix_product(second_feed_ranked, adapter_up_table[1, stream_index]))
        results.append(after_attn + mod_rows[5] * feedforward_branch)
    return (results[0], results[1])

def reference(image_input, text_input, cond, image_cotangent, text_cotangent, live, slot_adapter_index, modulation_weight, query_key_value_weight, output_weight, first_feed_weight, second_feed_weight, adapter_down_table, adapter_up_table, modulation_up_factor, query_key_value_up, first_feed_up, output_down_factor, second_feed_down):
    frozen_weights = tuple((weight_matrix.astype(jnp.float32) for weight_matrix in (modulation_weight, query_key_value_weight, output_weight, first_feed_weight, second_feed_weight)))
    adapter_tables = tuple((weight_matrix.astype(jnp.float32) for weight_matrix in (adapter_down_table, adapter_up_table, modulation_up_factor, query_key_value_up, first_feed_up, output_down_factor, second_feed_down)))
    table_axes = (2, 2, 1, 1, 1, 1, 1)

    def step(totals, slot_data):
        image_token_rows, text_token_rows, condition_vector, cot_image, cot_text, alive_flag, ident = slot_data
        start_row = (ident * ADAPTER_RANK).astype(jnp.int32)
        pieces = tuple((lax.dynamic_slice_in_dim(table, start_row, ADAPTER_RANK, table_axis) for table, table_axis in zip(adapter_tables, table_axes)))

        def forward(image_f, text_f, cond_f, piece_a, piece_b, piece_c, piece_d, piece_e, piece_f, piece_g):
            return block_forward(image_f, text_f, cond_f, piece_a, piece_b, piece_c, piece_d, piece_e, piece_f, piece_g, frozen_weights)
        outputs, pull_back = jax.vjp(forward, image_token_rows.astype(jnp.float32), text_token_rows.astype(jnp.float32), condition_vector, pieces[0], pieces[1], pieces[2], pieces[3], pieces[4], pieces[5], pieces[6])
        weight = alive_flag.astype(jnp.float32)
        gradients = pull_back((cot_image.astype(jnp.float32) * weight, cot_text.astype(jnp.float32) * weight))
        new_totals = tuple((lax.dynamic_update_slice_in_dim(running, lax.dynamic_slice_in_dim(running, start_row, ADAPTER_RANK, table_axis) + grad_piece, start_row, table_axis) for running, grad_piece, table_axis in zip(totals, gradients[3:], table_axes)))
        slot_out = ((outputs[0] * weight).astype(jnp.bfloat16), (outputs[1] * weight).astype(jnp.bfloat16), gradients[0].astype(jnp.bfloat16), gradients[1].astype(jnp.bfloat16), gradients[2])
        return (new_totals, slot_out)
    start_totals = tuple((jnp.zeros_like(table) for table in adapter_tables))
    totals, slot_rows = lax.scan(step, start_totals, (image_input, text_input, cond, image_cotangent, text_cotangent, live, slot_adapter_index))
    return (slot_rows[0], slot_rows[1], slot_rows[2], slot_rows[3], slot_rows[4], totals[0], totals[1], totals[2], totals[3], totals[4], totals[5], totals[6])
```

```python
import functools

import jax
import jax.numpy as jnp
from jax import lax
from jax.experimental import pallas as pl
from jax.experimental.pallas import tpu as pltpu
from jax.sharding import PartitionSpec as P

HD = 64
RANK = 16
EPSILON = 1e-06
BF = jnp.bfloat16
F32 = jnp.float32
CORES = 2


def dot(left, right, dims):
    return lax.dot_general(left, right, (dims, ((), ())), preferred_element_type=F32)


def mm(left, right):
    return dot(left, right, ((left.ndim - 1,), (0,)))


def mm_t(left, right):
    return dot(left, right, ((left.ndim - 1,), (right.ndim - 1,)))


def t_mm(left, right):
    return dot(left, right, ((0,), (0,)))


def norm_rows(values):
    centred = values - jnp.mean(values, axis=-1, keepdims=True)
    inverse = lax.rsqrt(jnp.mean(centred * centred, axis=-1, keepdims=True) + EPSILON)
    return centred * inverse, inverse


def norm_back(grad_hat, hat, inverse):
    first = jnp.mean(grad_hat, axis=-1, keepdims=True)
    second = jnp.mean(grad_hat * hat, axis=-1, keepdims=True)
    return inverse * (grad_hat - first - hat * second)


def gelu_tanh(values):
    return jax.nn.gelu(values, approximate=True)


def head_tiles(width):
    if width % 128 == 0:
        return [(p * 128, 128, 2) for p in range(width // 128)]
    return [(h * HD, HD, 1) for h in range(width // HD)]


def head_masks(rows, count):
    if count == 1:
        return [None]
    lane = lax.broadcasted_iota(jnp.int32, (rows, 128), 1)
    return [lane < HD, lane >= HD]


def pick(mask, values):
    return values if mask is None else jnp.where(mask, values, jnp.zeros_like(values))


def attend_forward_kernel(width, q_ref, kv_ref, out_ref, lse_ref):
    rows = q_ref.shape[0]
    lses = []
    for start, size, count in head_tiles(width):
        queries = q_ref[:, start : start + size] * jnp.asarray(HD ** (-0.5), BF)
        keys = kv_ref[:, width + start : width + start + size]
        values = kv_ref[:, 2 * width + start : 2 * width + start + size]
        total = None
        for mask in head_masks(rows, count):
            scores = mm_t(pick(mask, queries), keys)
            top = jnp.max(scores, axis=-1, keepdims=True)
            weights = jnp.exp(scores - top)
            norm = jnp.sum(weights, axis=-1, keepdims=True)
            part = mm(weights.astype(BF), values) * (1.0 / norm)
            part = pick(mask, part)
            total = part if total is None else total + part
            lses.append(top + jnp.log(norm))
        out_ref[:, start : start + size] = total.astype(BF)
    lse_ref[...] = jnp.concatenate(lses, axis=1)


def attend_backward_kernel(width, blocks, q_ref, kv_ref, grad_ref, lse_ref, out_ref, dk_ref, dv_ref):
    step = pl.program_id(0)
    rows = q_ref.shape[0]

    @pl.when(step == 0)
    def _():
        dk_ref[...] = jnp.zeros_like(dk_ref)
        dv_ref[...] = jnp.zeros_like(dv_ref)

    row0 = pl.multiple_of(step * rows, rows)
    head = 0
    for start, size, count in head_tiles(width):
        queries = q_ref[:, start : start + size] * jnp.asarray(HD ** (-0.5), BF)
        keys = kv_ref[:, width + start : width + start + size]
        values = kv_ref[:, 2 * width + start : 2 * width + start + size]
        grads = grad_ref[:, start : start + size]
        grad_q = None
        for mask in head_masks(rows, count):
            queries_m = pick(mask, queries)
            grads_m = pick(mask, grads)
            scores = mm_t(queries_m, keys)
            probs = jnp.exp(scores - lse_ref[:, head : head + 1])
            grad_probs = mm_t(grads_m, values)
            product = probs * grad_probs
            inner = jnp.sum(product, axis=-1, keepdims=True)
            grad_scores = (product - probs * inner).astype(BF)
            part = pick(mask, mm(grad_scores, keys))
            grad_q = part if grad_q is None else grad_q + part
            dk_ref[:, start : start + size] += t_mm(grad_scores, queries_m)
            dv_ref[:, start : start + size] += t_mm(probs.astype(BF), grads_m)
            head += 1
        out_ref[pl.ds(row0, rows), start : start + size] = (grad_q * HD ** (-0.5)).astype(BF)

    @pl.when(step == blocks - 1)
    def _():
        out_ref[:, width : 2 * width] = dk_ref[...].astype(BF)
        out_ref[:, 2 * width :] = dv_ref[...].astype(BF)


def query_block(length):
    for rows in (256, 128, 64, 32, 16):
        if length % rows == 0:
            return rows
    return length


def attend_forward(joint):
    length, width3 = joint.shape
    width = width3 // 3
    heads = width // HD
    rows = query_block(length)
    return pl.pallas_call(
        functools.partial(attend_forward_kernel, width),
        grid=(length // rows,),
        in_specs=[
            pl.BlockSpec((rows, width3), lambda i: (i, 0)),
            pl.BlockSpec((length, width3), lambda i: (0, 0)),
        ],
        out_specs=[
            pl.BlockSpec((rows, width), lambda i: (i, 0)),
            pl.BlockSpec((rows, heads), lambda i: (i, 0)),
        ],
        out_shape=[
            jax.ShapeDtypeStruct((length, width), BF),
            jax.ShapeDtypeStruct((length, heads), F32),
        ],
        compiler_params=pltpu.CompilerParams(vmem_limit_bytes=40 * 1024 * 1024),
        cost_estimate=pl.CostEstimate(
            flops=4 * length * length * width,
            transcendentals=length * length * heads,
            bytes_accessed=length * width3 * 4,
        ),
        name="attend_forward",
    )(joint, joint)


def attend_backward(joint, grads, lse):
    length, width3 = joint.shape
    width = width3 // 3
    heads = width // HD
    rows = query_block(length)
    blocks = length // rows
    return pl.pallas_call(
        functools.partial(attend_backward_kernel, width, blocks),
        grid=(blocks,),
        in_specs=[
            pl.BlockSpec((rows, width3), lambda i: (i, 0)),
            pl.BlockSpec((length, width3), lambda i: (0, 0)),
            pl.BlockSpec((rows, width), lambda i: (i, 0)),
            pl.BlockSpec((rows, heads), lambda i: (i, 0)),
        ],
        out_specs=pl.BlockSpec((length, width3), lambda i: (0, 0)),
        out_shape=jax.ShapeDtypeStruct((length, width3), BF),
        scratch_shapes=[pltpu.VMEM((length, width), F32), pltpu.VMEM((length, width), F32)],
        compiler_params=pltpu.CompilerParams(vmem_limit_bytes=48 * 1024 * 1024),
        cost_estimate=pl.CostEstimate(
            flops=10 * length * length * width,
            transcendentals=length * length * heads,
            bytes_accessed=length * width3 * 8,
        ),
        name="attend_backward",
    )(joint, joint, grads, lse)


class Stream:
    pass


def powers(size):
    bits, bit = [], 1
    while bit < size:
        bits.append(bit)
        bit *= 2
    return bits


def body(
    mesh_shape,
    image_input,
    text_input,
    cond,
    image_cotangent,
    text_cotangent,
    live,
    slot_adapter_index,
    modulation_weight,
    query_key_value_weight,
    output_weight,
    first_feed_weight,
    second_feed_weight,
    adapter_down_table,
    adapter_up_table,
    modulation_up_factor,
    query_key_value_up,
    first_feed_up,
    output_down_factor,
    second_feed_down,
):
    R, F, T = mesh_shape
    H = T // CORES
    X = R // CORES
    W = image_input.shape[-1]
    wq = W // T
    Rf = modulation_up_factor.shape[1]
    Rq = adapter_down_table.shape[2]
    ffq = first_feed_weight.shape[-1]
    r = lax.axis_index("rep")
    f = lax.axis_index("fsdp")
    z = lax.axis_index("tp")
    core = lax.rem(r, CORES)
    xi = lax.div(r, CORES)
    high = lax.div(z, H)
    native = core == high
    shard = core * H + lax.rem(z, H)

    def xz(v, bit):
        return lax.ppermute(v, "tp", [(i, i ^ bit) for i in range(T)])

    def xf(v, bit):
        return lax.ppermute(v, "fsdp", [(i, i ^ bit) for i in range(F)])

    def xr(v, bit):
        return lax.ppermute(v, "rep", [(i, i ^ bit) for i in range(R)])

    swap_pairs = []
    for a in range(R):
        for b in range(T):
            here = a * T + b
            stays = a % CORES == b // H
            swap_pairs.append((here, here if stays else (a ^ 1) * T + (b ^ H)))

    def exchange(v):
        return lax.ppermute(v, ("rep", "tp"), swap_pairs)

    def gather_by(v, step, bits):
        blocks = v[None]
        for bit in bits:
            blocks = jnp.concatenate([blocks, step(blocks, bit)], axis=0)
        return blocks

    x_bits = [b for b in powers(R) if b > 1]
    h_bits = powers(H)
    t_bits = powers(T)
    f_bits = powers(F)
    arange_t = jnp.arange(T, dtype=jnp.int32)

    def gather_group(v):
        blocks = [v]
        for bit in h_bits:
            blocks = blocks + [xz(b, bit) for b in blocks]
        blocks = blocks + [xr(b, 1) for b in blocks]
        return jnp.concatenate(blocks, axis=0)

    def scatter_group(v):
        half = v.shape[0] // 2
        v = v[:half] + xr(v[half:], 1)
        for bit in reversed(h_bits):
            half = v.shape[0] // 2
            v = v[:half] + xz(v[half:], bit)
        return v

    def gather_text(v):
        for bit in t_bits:
            v = jnp.concatenate([v, xz(v, bit)], axis=0)
        return v

    def scatter_text(v):
        for bit in reversed(t_bits):
            half = v.shape[0] // 2
            v = v[:half] + xz(v[half:], bit)
        return v

    def to_relative(v, index):
        n = v.shape[-1] // T
        blocks = jnp.moveaxis(v.reshape(v.shape[:-1] + (T, n)), -2, 0)
        return jnp.take(blocks, jnp.bitwise_xor(index, arange_t), axis=0)

    silu = jax.nn.silu(cond).astype(BF)
    info = jnp.concatenate(
        [
            silu.astype(F32),
            jnp.broadcast_to(slot_adapter_index.astype(F32)[:, None], (1, 64)),
            jnp.broadcast_to(live.astype(F32)[:, None], (1, 64)),
        ],
        axis=1,
    )
    info_f = gather_by(info[0], xf, f_bits)
    info_all = gather_by(info_f, xr, [1] + x_bits)
    silu_f = info_f[:, :W].astype(BF)
    ids_f = info_f[:, W].astype(jnp.int32)
    ids_all = info_all[:, :, W].astype(jnp.int32)
    silu_all = info_all[:, :, :W].astype(BF)
    my_id = slot_adapter_index[0]
    alive_txt = live.astype(F32)[0]
    alive_img = jnp.where(native, alive_txt, info_all[1, 0, W + 64])

    img = exchange(image_input[0])
    img_cot = exchange(image_cotangent[0])
    txt = text_input[0]
    txt_cot = text_cotangent[0]

    down_ada = adapter_down_table[0]
    down_rel = gather_by(down_ada, xz, t_bits)
    rank_rel = jnp.einsum("fd,tkid->tfki", silu_f, down_rel, preferred_element_type=F32)
    rank_abs = jnp.take(rank_rel, jnp.bitwise_xor(z, arange_t), axis=0)
    rank_rows = jnp.moveaxis(rank_abs, 0, 2).reshape(F, 2, Rf)
    row_ids = f * Rf + jnp.arange(Rf, dtype=jnp.int32)
    row_adapter = lax.div(row_ids, RANK)
    own_rows = (row_adapter[None] == ids_f[:, None])[:, None, :]
    rank_rows = jnp.where(own_rows, rank_rows, 0.0).astype(BF)
    rows_d = modulation_weight.shape[1]
    silu_rows = lax.dynamic_slice_in_dim(silu_f, f * rows_d, rows_d, axis=1)
    parts = []
    for k in range(2):
        parts.append(
            jnp.einsum("fd,dcj->fcj", silu_rows, modulation_weight[k], preferred_element_type=F32)
            + jnp.einsum(
                "fr,rcj->fcj", rank_rows[:, k], modulation_up_factor[k], preferred_element_type=F32
            )
        )
    partial_mod = jnp.stack(parts, axis=1)
    mod_shard = partial_mod[0]
    for d in range(1, F):
        mod_shard = mod_shard + xf(partial_mod[d], d)
    mod_rel = gather_by(mod_shard, xz, t_bits)
    mod_abs = jnp.take(mod_rel, jnp.bitwise_xor(z, arange_t), axis=0)
    mod_all = jnp.moveaxis(mod_abs, 0, 2).reshape(2, 6, W)
    mod_img = jnp.where(native, mod_all[0], xr(mod_all[0], 1))
    mod_txt = mod_all[1]

    tables = jnp.concatenate([adapter_down_table[1:], adapter_up_table], axis=0)
    base_row = f * Rf + z * Rq

    def own_table_rows(ident):
        wanted = ident * RANK + jnp.arange(RANK, dtype=jnp.int32)
        held = base_row + jnp.arange(Rq, dtype=jnp.int32)
        if Rq == RANK:
            return jnp.where(ident * RANK == base_row, tables, jnp.zeros_like(tables))
        match = (wanted[:, None] == held[None, :]).astype(BF)
        return jnp.einsum("ir,ksrw->ksiw", match, tables, preferred_element_type=F32).astype(BF)

    table_rows = own_table_rows(ids_f[0])
    for d in range(1, F):
        table_rows = table_rows + xf(own_table_rows(ids_f[d]), d)
    for bit in t_bits:
        table_rows = table_rows + xz(table_rows, bit)
    rows_txt = table_rows[:, 1]
    rows_img = jnp.where(native, table_rows[:, 0], xr(table_rows[:, 0], 1))

    columns = jnp.concatenate(
        [
            query_key_value_up.reshape(2, Rf, 3 * wq),
            first_feed_up,
            output_down_factor,
            second_feed_down,
        ],
        axis=2,
    )

    def own_columns(ident):
        start = ident * RANK - f * Rf
        inside = (start >= 0) & (start <= Rf - RANK)
        taken = lax.dynamic_slice_in_dim(columns, jnp.clip(start, 0, Rf - RANK), RANK, axis=1)
        return jnp.where(inside, taken, jnp.zeros_like(taken))

    column_rows = own_columns(ids_f[0])
    for d in range(1, F):
        column_rows = column_rows + xf(own_columns(ids_f[d]), d)
    cols_txt = column_rows[1]
    cols_img = exchange(column_rows[0])
    cuts = (0, 3 * wq, 3 * wq + ffq, 4 * wq + ffq, 4 * wq + 2 * ffq)

    def stream(rows, cols, mod, tokens, cotangent, alive, gather, scatter):
        s = Stream()
        s.a_qkv, s.a_fc1, s.b_out, s.b_fc2 = rows[0], rows[1], rows[2], rows[3]
        s.b_qkv = cols[:, cuts[0] : cuts[1]]
        s.b_fc1 = cols[:, cuts[1] : cuts[2]]
        s.a_out = cols[:, cuts[2] : cuts[3]]
        s.a_fc2 = cols[:, cuts[3] : cuts[4]]
        s.mod, s.x, s.cot, s.live = mod, tokens, cotangent, alive
        s.gather, s.scatter = gather, scatter
        return s

    def place(shape, pieces, axis):
        full = jnp.zeros(shape, BF)
        for piece, offset in pieces:
            full = lax.dynamic_update_slice_in_dim(full, piece, offset, axis=axis)
        return full

    def fetch_image(weight, axis, share):
        rows, cols = weight.shape
        part = rows // X
        mine = lax.dynamic_slice_in_dim(weight, xi * part, part, axis=0)
        moved = gather_by(exchange(mine), xr, x_bits)
        held = place((rows, cols), [(moved[e], (xi ^ e) * part) for e in range(X)], 0)
        held = jnp.where(native, weight, held)
        full_shape = (rows * F, cols) if axis == 0 else (rows, cols * F)
        size = weight.shape[axis]
        full = place(full_shape, [(held, f * size)], axis)
        for d in range(1, F):
            if share:
                piece = xf(lax.dynamic_slice_in_dim(held, xi * part, part, axis=0), d)
                pieces = gather_by(piece, xr, x_bits)
                for e in range(X):
                    start = [0, 0]
                    start[axis] = (f ^ d) * size
                    start[0] = start[0] + (xi ^ e) * part
                    full = lax.dynamic_update_slice(full, pieces[e], start)
            else:
                full = lax.dynamic_update_slice_in_dim(full, xf(held, d), (f ^ d) * size, axis=axis)
        return full

    def fetch_text(weight, axis):
        rows, cols = weight.shape
        part = rows // R
        mine = lax.dynamic_slice_in_dim(weight, r * part, part, axis=0)
        full_shape = (rows * F, cols) if axis == 0 else (rows, cols * F)
        size = weight.shape[axis]
        full = place(full_shape, [(weight, f * size)], axis)
        for d in range(1, F):
            pieces = gather_by(xf(mine, d), xr, x_bits + [1])
            order = [0]
            for bit in x_bits + [1]:
                order = order + [o ^ bit for o in order]
            for e in range(R):
                start = [0, 0]
                start[axis] = (f ^ d) * size
                start[0] = start[0] + (r ^ order[e]) * part
                full = lax.dynamic_update_slice(full, pieces[e], start)
        return full

    qkv_native = query_key_value_weight.reshape(2, rows_d, 3 * wq)
    image = stream(rows_img, cols_img, mod_img, img, img_cot, alive_img, gather_group, scatter_group)
    text = stream(rows_txt, cols_txt, mod_txt, txt, txt_cot, alive_txt, gather_text, scatter_text)
    streams = (image, text)
    image.w_qkv = fetch_image(qkv_native[0], 0, False)
    image.w_out = fetch_image(output_weight[0], 1, True)
    image.w_fc1 = fetch_image(first_feed_weight[0], 0, True)
    image.w_fc2 = fetch_image(second_feed_weight[0], 1, True)
    text.w_qkv = fetch_text(qkv_native[1], 0)
    text.w_out = fetch_text(output_weight[1], 1)
    text.w_fc1 = fetch_text(first_feed_weight[1], 0)
    text.w_fc2 = fetch_text(second_feed_weight[1], 1)

    for s in streams:
        mod = s.mod
        s.xf = s.x.astype(F32)
        s.hat1, s.inv1 = norm_rows(s.xf)
        normed = (s.hat1 * (1.0 + mod[1:2]) + mod[0:1]).astype(BF)
        s.n1 = s.gather(normed)
        s.g2 = s.cot.astype(F32) * s.live
        s.gb_mlp = s.gather((mod[5:6] * s.g2).astype(BF))
        s.rank_qkv = mm_t(s.n1, s.a_qkv).astype(BF)
        s.joint = (mm(s.n1, s.w_qkv) + mm(s.rank_qkv, s.b_qkv)).astype(BF)
    img_len = image.joint.shape[0]
    joint = jnp.concatenate([image.joint, exchange(text.joint)], axis=0)
    attended, lse = attend_forward(joint)
    image.att = attended[:img_len]
    text.att = exchange(attended[img_len:])
    for s in streams:
        mod = s.mod
        s.rank_out = mm_t(s.att, s.a_out).astype(BF)
        partial = mm(s.att, s.w_out) + mm(s.rank_out, s.b_out)
        s.br_attn = s.scatter(partial.astype(BF)).astype(F32)
        s.after = s.xf + mod[2:3] * s.br_attn
        s.hat2, s.inv2 = norm_rows(s.after)
        normed = (s.hat2 * (1.0 + mod[4:5]) + mod[3:4]).astype(BF)
        s.n2 = s.gather(normed)
        s.rank_fc1 = mm_t(s.n2, s.a_fc1).astype(BF)
        s.hidden = mm(s.n2, s.w_fc1) + mm(s.rank_fc1, s.b_fc1)
        s.act = gelu_tanh(s.hidden).astype(BF)
        s.rank_fc2 = mm_t(s.act, s.a_fc2).astype(BF)
        partial = mm(s.act, s.w_fc2) + mm(s.rank_fc2, s.b_fc2)
        s.br_mlp = s.scatter(partial.astype(BF)).astype(F32)
        s.out = ((s.after + mod[5:6] * s.br_mlp) * s.live).astype(BF)

    for s in streams:
        mod = s.mod
        s.gg_mlp = jnp.sum(s.g2 * s.br_mlp, axis=0)
        gb = s.gb_mlp
        gr_fc2 = mm_t(gb, s.b_fc2).astype(BF)
        s.t_back1 = t_mm(s.rank_fc2, gb)
        grad_act = mm_t(gb, s.w_fc2) + mm(gr_fc2, s.a_fc2)
        _, pull = jax.vjp(gelu_tanh, s.hidden)
        gh = pull(grad_act)[0].astype(BF)
        s.t_a_fc2 = t_mm(gr_fc2, s.act)
        s.t_b_fc1 = t_mm(s.rank_fc1, gh)
        gr_fc1 = mm_t(gh, s.b_fc1).astype(BF)
        s.t_in2 = t_mm(gr_fc1, s.n2)
        partial = mm_t(gh, s.w_fc1) + mm(gr_fc1, s.a_fc1)
        gn2 = s.scatter(partial.astype(BF)).astype(F32)
        s.gs_mlp = jnp.sum(gn2, axis=0)
        s.gc_mlp = jnp.sum(gn2 * s.hat2, axis=0)
        s.g_after = s.g2 + norm_back(gn2 * (1.0 + mod[4:5]), s.hat2, s.inv2)
        s.gg_attn = jnp.sum(s.g_after * s.br_attn, axis=0)
        gb = s.gather((mod[2:3] * s.g_after).astype(BF))
        gr_out = mm_t(gb, s.b_out).astype(BF)
        s.t_back0 = t_mm(s.rank_out, gb)
        s.g_att = (mm_t(gb, s.w_out) + mm(gr_out, s.a_out)).astype(BF)
        s.t_a_out = t_mm(gr_out, s.att)

    def combine(pieces):
        blocks = gather_by(gather_by(pieces, xf, f_bits), xr, [1] + x_bits)
        flat = blocks.reshape(R * F * RANK, pieces.shape[-1])
        slots = (ids_all[:, :, None] * RANK + jnp.arange(RANK, dtype=jnp.int32)).reshape(1, -1)
        place_rows = (row_ids[:, None] == slots).astype(BF)
        return mm(place_rows, flat)

    def reduce_rows(img_rows, txt_rows):
        def fold(rows, index, scatter):
            blocks = to_relative(rows, index)
            n = blocks.shape[1]
            return scatter(blocks.reshape(T * n, wq)).reshape(n, wq)

        return exchange(fold(img_rows, shard, scatter_group)), fold(txt_rows, z, scatter_text)

    def rows_home(rows):
        kinds = rows.shape[1]
        blocks = rows.astype(BF).reshape(T, Rq, kinds, wq)
        blocks = jnp.take(blocks, jnp.bitwise_xor(z, arange_t), axis=0)
        got = jnp.stack([blocks[0]] + [xz(blocks[d], d) for d in range(1, T)])
        got = jnp.take(got, jnp.bitwise_xor(z, arange_t), axis=0)
        return jnp.moveaxis(got, 0, 2).reshape(Rq, kinds, W).astype(F32)

    early_rows = reduce_rows(
        *[jnp.concatenate([s.t_back1, s.t_in2, s.t_back0], axis=0).astype(BF) for s in streams]
    )
    early_img = exchange(
        jnp.concatenate([image.t_b_fc1, image.t_a_fc2, image.t_a_out], axis=1).astype(BF)
    )
    early_txt = jnp.concatenate([text.t_b_fc1, text.t_a_fc2, text.t_a_out], axis=1).astype(BF)

    def lay(rows, kinds):
        return [rows[i * RANK : (i + 1) * RANK] for i in range(kinds)]

    early = combine(
        jnp.concatenate([early_img, early_txt] + lay(early_rows[0], 3) + lay(early_rows[1], 3), axis=1)
    )
    span = 2 * ffq + wq
    grad_b_fc1 = jnp.stack([early[:, 0:ffq], early[:, span : span + ffq]])
    grad_a_fc2 = jnp.stack([early[:, ffq : 2 * ffq], early[:, span + ffq : span + 2 * ffq]])
    grad_a_out = jnp.stack([early[:, 2 * ffq : span], early[:, span + 2 * ffq : 2 * span]])
    home = rows_home(early[:, 2 * span :].reshape(Rf, 6, wq))

    g_att = jnp.concatenate([image.g_att, exchange(text.g_att)], axis=0)
    g_joint = attend_backward(joint, g_att, lse)
    image.g_joint = g_joint[:img_len]
    text.g_joint = exchange(g_joint[img_len:])
    for s in streams:
        mod = s.mod
        gj = s.g_joint
        gr_qkv = mm_t(gj, s.b_qkv).astype(BF)
        partial = mm_t(gj, s.w_qkv) + mm(gr_qkv, s.a_qkv)
        gn1 = s.scatter(partial.astype(BF)).astype(F32)
        s.t_b_qkv = t_mm(s.rank_qkv, gj)
        s.t_in1 = t_mm(gr_qkv, s.n1)
        s.gs_attn = jnp.sum(gn1, axis=0)
        s.gc_attn = jnp.sum(gn1 * s.hat1, axis=0)
        dx = s.g_after + norm_back(gn1 * (1.0 + mod[1:2]), s.hat1, s.inv1)
        s.dx = dx.astype(BF)
    late_rows = reduce_rows(
        *[
            jnp.concatenate(
                [
                    s.t_in1,
                    jnp.stack(
                        [s.gs_attn, s.gc_attn, s.gg_attn, s.gs_mlp, s.gc_mlp, s.gg_mlp]
                    ),
                ],
                axis=0,
            )
            for s in streams
        ]
    )
    gm = jnp.stack([rows[RANK:] for rows in late_rows]).astype(BF)
    gm_f = gather_by(gm, xf, f_bits)
    gm_all = gather_by(gm_f, xr, [1] + x_bits)

    late = combine(
        jnp.concatenate(
            [exchange(image.t_b_qkv.astype(BF)), text.t_b_qkv.astype(BF)]
            + [rows[:RANK].astype(BF) for rows in late_rows],
            axis=1,
        )
    )
    grad_b_qkv = jnp.stack([late[:, : 3 * wq], late[:, 3 * wq : 6 * wq]]).reshape(2, Rf, 3, wq)
    home_late = rows_home(late[:, 6 * wq :].reshape(Rf, 2, wq))

    seqs = R * F
    match = (row_adapter[None, :] == ids_all.reshape(seqs)[:, None]).astype(F32)
    gm_seq = gm_all.reshape(seqs, 2, 6, wq)
    rank_seq_rel = jnp.einsum(
        "sd,tkid->stki", silu_all.reshape(seqs, W), down_rel, preferred_element_type=F32
    )
    rank_seq = jnp.take(rank_seq_rel, jnp.bitwise_xor(z, arange_t), axis=1)
    rank_seq = jnp.moveaxis(rank_seq, 1, 2).reshape(seqs, 2, Rf)
    rank_seq = (rank_seq * match[:, None, :]).astype(BF)
    grad_b_ada, gcr = [], []
    for k in range(2):
        grad_b_ada.append(
            jnp.einsum("sr,scj->rcj", rank_seq[:, k], gm_seq[:, k], preferred_element_type=F32)
        )
        gcr.append(
            jnp.einsum(
                "scj,rcj->sr", gm_seq[:, k], modulation_up_factor[k], preferred_element_type=F32
            )
            * match
        )
    grad_b_ada = jnp.stack(grad_b_ada)
    gcr = jnp.stack(gcr, axis=1)
    gcr_rel = jnp.take(
        jnp.moveaxis(gcr.reshape(seqs, 2, T, Rq), 2, 0), jnp.bitwise_xor(z, arange_t), axis=0
    )
    gcr_own = gcr_rel[0]
    for d in range(1, T):
        gcr_own = gcr_own + xz(gcr_rel[d], d)
    grad_in0 = jnp.einsum(
        "ski,sd->kid",
        gcr_own,
        silu_all.reshape(seqs, W).astype(F32),
        precision=lax.Precision.HIGHEST,
    )
    gm_pair = gm_f
    dpart = jnp.zeros((F, rows_d), F32)
    for k in range(2):
        dpart = dpart + jnp.einsum(
            "fcj,dcj->fd", gm_pair[:, k], modulation_weight[k], preferred_element_type=F32
        )
    dfull = lax.dynamic_update_slice_in_dim(jnp.zeros((F, W), F32), dpart, f * rows_d, axis=1)
    gcr_pair = gcr.reshape(R, F, 2, T, Rq)[0]
    gcr_pair = jnp.take(gcr_pair, jnp.bitwise_xor(z, arange_t), axis=2)
    dfull = dfull + jnp.einsum(
        "fkti,tkid->fd",
        gcr_pair,
        down_rel.astype(F32),
        precision=lax.Precision.HIGHEST,
    )
    dsum = dfull[0]
    for d in range(1, F):
        dsum = dsum + xf(dfull[d], d)
    for bit in t_bits:
        dsum = dsum + xz(dsum, bit)
    sigmoid = jax.nn.sigmoid(cond)
    dcond = dsum[None] * sigmoid * (1.0 + cond * (1.0 - sigmoid))

    grad_in = jnp.stack(
        [
            grad_in0,
            jnp.moveaxis(home_late, 1, 0),
            jnp.stack([home[:, 1], home[:, 4]]),
        ]
    )
    grad_back = jnp.stack(
        [jnp.stack([home[:, 2], home[:, 5]]), jnp.stack([home[:, 0], home[:, 3]])]
    )
    return (
        exchange(image.out)[None],
        text.out[None],
        exchange(image.dx)[None],
        text.dx[None],
        dcond,
        grad_in,
        grad_back,
        grad_b_ada,
        grad_b_qkv,
        grad_b_fc1,
        grad_a_out,
        grad_a_fc2,
    )


def solution(mesh):
    tokens = P(("rep", "fsdp"), "tp", None)
    table = P(None, None, ("fsdp", "tp"), None)
    columns4 = P(None, "fsdp", None, "tp")
    columns3 = P(None, "fsdp", "tp")
    rows3 = P(None, "tp", "fsdp")
    slot = P(("rep", "fsdp"))
    in_specs = (
        tokens, tokens, P(("rep", "fsdp"), None), tokens, tokens, slot, slot,
        columns4, columns4, rows3, columns3, rows3, table, table,
        columns4, columns4, columns3, columns3, columns3,
    )
    out_specs = (
        tokens, tokens, tokens, tokens, P(("rep", "fsdp"), None),
        table, table, columns4, columns4, columns3, columns3, columns3,
    )
    sizes = (mesh.shape["rep"], mesh.shape["fsdp"], mesh.shape["tp"])
    return jax.shard_map(
        functools.partial(body, sizes), mesh=mesh, in_specs=in_specs, out_specs=out_specs, check_vma=False
    )
```

```python
import functools

import jax
import jax.numpy as jnp
from jax import lax
from jax.experimental import pallas as pl
from jax.experimental.pallas import tpu as pltpu
from jax.sharding import PartitionSpec as P

HD = 64
RANK = 16
EPSILON = 1e-06
BF = jnp.bfloat16
F32 = jnp.float32
CORES = 2


def dot(left, right, dims):
    return lax.dot_general(left, right, (dims, ((), ())), preferred_element_type=F32)


def mm(left, right):
    return dot(left, right, ((left.ndim - 1,), (0,)))


def mm_t(left, right):
    return dot(left, right, ((left.ndim - 1,), (right.ndim - 1,)))


def t_mm(left, right):
    return dot(left, right, ((0,), (0,)))


def norm_rows(values):
    centred = values - jnp.mean(values, axis=-1, keepdims=True)
    inverse = lax.rsqrt(jnp.mean(centred * centred, axis=-1, keepdims=True) + EPSILON)
    return centred * inverse, inverse


def norm_back(grad_hat, hat, inverse):
    first = jnp.mean(grad_hat, axis=-1, keepdims=True)
    second = jnp.mean(grad_hat * hat, axis=-1, keepdims=True)
    return inverse * (grad_hat - first - hat * second)


def gelu_tanh(values):
    return jax.nn.gelu(values, approximate=True)


class Slot(int):
    pass


def spot(offs, where, step):
    if isinstance(where, Slot):
        return pl.multiple_of(offs[int(where)], step)
    return where


def copies(offs, plan, sources, targets, sems):
    def make(i):
        source, lead, rows, cols, target, row, col, _ = plan[i]
        ref = sources[source] if lead is None else sources[source].at[lead]
        dst = targets[target].at[pl.ds(spot(offs, row, 16), rows), pl.ds(spot(offs, col, 128), cols)]
        return pltpu.make_async_copy(ref, dst, sems.at[i])

    def each(action, chosen):
        for i in range(len(plan)):
            if chosen is not None and plan[i][4] not in chosen:
                continue
            case = plan[i][7]
            if case is None:
                action(make(i))
            else:

                @pl.when(offs[0] == case)
                def _(i=i):
                    action(make(i))

    return (
        lambda chosen=None: each(lambda c: c.start(), chosen),
        lambda chosen=None: each(lambda c: c.wait(), chosen),
    )


ANY = pl.BlockSpec(memory_space=pl.ANY)
SCALARS = pl.BlockSpec(memory_space=pltpu.SMEM)


def head_tiles(width):
    if width % 128 == 0:
        return [(p * 128, 128, 2) for p in range(width // 128)]
    return [(h * HD, HD, 1) for h in range(width // HD)]


def head_masks(rows, count):
    if count == 1:
        return [None]
    lane = lax.broadcasted_iota(jnp.int32, (rows, 128), 1)
    return [lane < HD, lane >= HD]


def pick(mask, values):
    return values if mask is None else jnp.where(mask, values, jnp.zeros_like(values))


def attend_forward_kernel(width, plan, offs, *refs):
    *sources, out_ref, lse_ref, kv_ref, sems = refs
    start_all, wait_all = copies(offs, plan, sources, [kv_ref], sems)
    step = pl.program_id(0)

    @pl.when(step == 0)
    def _():
        start_all()
        wait_all()

    rows = out_ref.shape[0]
    here = pl.ds(pl.multiple_of(step * rows, rows), rows)
    lses = []
    for start, size, count in head_tiles(width):
        queries = kv_ref[here, start : start + size] * jnp.asarray(HD ** (-0.5), BF)
        keys = kv_ref[:, width + start : width + start + size]
        values = kv_ref[:, 2 * width + start : 2 * width + start + size]
        total = None
        for mask in head_masks(rows, count):
            scores = mm_t(pick(mask, queries), keys)
            top = jnp.max(scores, axis=-1, keepdims=True)
            weights = jnp.exp(scores - top)
            norm = jnp.sum(weights, axis=-1, keepdims=True)
            part = mm(weights.astype(BF), values) * (1.0 / norm)
            part = pick(mask, part)
            total = part if total is None else total + part
            lses.append(top + jnp.log(norm))
        out_ref[:, start : start + size] = total.astype(BF)
    lse_ref[...] = jnp.concatenate(lses, axis=1)


def attend_backward_kernel(width, blocks, plan, offs, lse_ref, *refs):
    *sources, out_ref, kv_ref, grad_ref, dk_ref, dv_ref, sems = refs
    start_all, wait_all = copies(offs, plan, sources, [kv_ref, grad_ref], sems)
    step = pl.program_id(0)

    @pl.when(step == 0)
    def _():
        start_all()
        dk_ref[...] = jnp.zeros_like(dk_ref)
        dv_ref[...] = jnp.zeros_like(dv_ref)
        wait_all()

    rows = lse_ref.shape[0]
    here = pl.ds(pl.multiple_of(step * rows, rows), rows)
    head = 0
    for start, size, count in head_tiles(width):
        queries = kv_ref[here, start : start + size] * jnp.asarray(HD ** (-0.5), BF)
        keys = kv_ref[:, width + start : width + start + size]
        values = kv_ref[:, 2 * width + start : 2 * width + start + size]
        grads = grad_ref[here, start : start + size]
        grad_q = None
        for mask in head_masks(rows, count):
            queries_m = pick(mask, queries)
            grads_m = pick(mask, grads)
            scores = mm_t(queries_m, keys)
            probs = jnp.exp(scores - lse_ref[:, head : head + 1])
            grad_probs = mm_t(grads_m, values)
            product = probs * grad_probs
            inner = jnp.sum(product, axis=-1, keepdims=True)
            grad_scores = (product - probs * inner).astype(BF)
            part = pick(mask, mm(grad_scores, keys))
            grad_q = part if grad_q is None else grad_q + part
            dk_ref[:, start : start + size] += t_mm(grad_scores, queries_m)
            dv_ref[:, start : start + size] += t_mm(probs.astype(BF), grads_m)
            head += 1
        out_ref[here, start : start + size] = (grad_q * HD ** (-0.5)).astype(BF)

    @pl.when(step == blocks - 1)
    def _():
        out_ref[:, width : 2 * width] = dk_ref[...].astype(BF)
        out_ref[:, 2 * width :] = dv_ref[...].astype(BF)


def query_block(length):
    for rows in (256, 128, 64, 32, 16):
        if length % rows == 0:
            return rows
    return length


def stack_plan(arrays, target, first):
    plan, row = [], 0
    for i, (array, case) in enumerate(arrays):
        plan.append((first + i, None, array.shape[0], array.shape[1], target, row, 0, case))
        if case != 1:
            row += array.shape[0]
    return plan, row


def attend_forward(offs, joints):
    plan, length = stack_plan(joints, 0, 0)
    width3 = joints[0][0].shape[1]
    width = width3 // 3
    heads = width // HD
    rows = query_block(length)
    return pl.pallas_call(
        functools.partial(attend_forward_kernel, width, plan),
        grid=(length // rows,),
        in_specs=[SCALARS] + [ANY] * len(joints),
        out_specs=[
            pl.BlockSpec((rows, width), lambda i: (i, 0)),
            pl.BlockSpec((rows, heads), lambda i: (i, 0)),
        ],
        out_shape=[
            jax.ShapeDtypeStruct((length, width), BF),
            jax.ShapeDtypeStruct((length, heads), F32),
        ],
        scratch_shapes=[pltpu.VMEM((length, width3), BF), pltpu.SemaphoreType.DMA((len(plan),))],
        compiler_params=pltpu.CompilerParams(vmem_limit_bytes=40 * 1024 * 1024),
        cost_estimate=pl.CostEstimate(
            flops=16 * length * length * width,
            transcendentals=length * length * heads,
            bytes_accessed=length * width3 * 4,
        ),
        name="attend_forward",
    )(offs, *[a for a, _ in joints])


def attend_backward(offs, joints, grads, lse):
    plan, length = stack_plan(joints, 0, 0)
    more, _ = stack_plan(grads, 1, len(joints))
    plan = plan + more
    width3 = joints[0][0].shape[1]
    width = width3 // 3
    heads = width // HD
    rows = query_block(length)
    blocks = length // rows
    return pl.pallas_call(
        functools.partial(attend_backward_kernel, width, blocks, plan),
        grid=(blocks,),
        in_specs=[SCALARS, pl.BlockSpec((rows, heads), lambda i: (i, 0))] + [ANY] * len(plan),
        out_specs=pl.BlockSpec((length, width3), lambda i: (0, 0)),
        out_shape=jax.ShapeDtypeStruct((length, width3), BF),
        scratch_shapes=[
            pltpu.VMEM((length, width3), BF),
            pltpu.VMEM((length, width), BF),
            pltpu.VMEM((length, width), F32),
            pltpu.VMEM((length, width), F32),
            pltpu.SemaphoreType.DMA((len(plan),)),
        ],
        compiler_params=pltpu.CompilerParams(vmem_limit_bytes=48 * 1024 * 1024),
        cost_estimate=pl.CostEstimate(
            flops=32 * length * length * width,
            transcendentals=length * length * heads,
            bytes_accessed=length * width3 * 8,
        ),
        name="attend_backward",
    )(offs, lse, *[a for a, _ in joints], *[a for a, _ in grads])


class Matrix:
    def __init__(self, shape, sources, plan):
        self.shape, self.sources, self.plan = shape, sources, plan


def join(refs):
    if len(refs) == 1:
        return refs[0][...]
    return jnp.concatenate([r[...] for r in refs], axis=0)


def split(value, refs):
    row = 0
    for ref in refs:
        ref[...] = value[row : row + ref.shape[0]].astype(ref.dtype)
        row += ref.shape[0]


def qkv_forward_kernel(ws, ins, outs, need):
    (x_refs, (a,), (b,)), ((out,), (rank_out,)) = ins, outs
    x = join(x_refs)
    rank = mm_t(x, a[...]).astype(BF)
    rank_out[...] = rank
    low = mm(rank, b[...])
    need(0)
    out[...] = (mm(x, ws[0][...]) + low).astype(BF)


def qkv_backward_kernel(ws, ins, outs, need):
    ((g,), x_refs, ranks, (a,), (b,)), (out, (t_b,), (t_a,)) = ins, outs
    grad = g[...]
    low = mm_t(grad, b[...]).astype(BF)
    t_b[...] = t_mm(join(ranks), grad)
    t_a[...] = t_mm(low, join(x_refs))
    need(0)
    split(mm_t(grad, ws[0][...]) + mm(low, a[...]), out)


def out_forward_kernel(ws, ins, outs, need):
    ((att,), (a,), (b,)), (out, (rank_out,)) = ins, outs
    act = att[...]
    rank = mm_t(act, a[...]).astype(BF)
    rank_out[...] = rank
    need(0)
    split(mm(act, ws[0][...]) + mm(rank, b[...]), out)


def out_backward_kernel(ws, ins, outs, need):
    (g_refs, (att,), (rank,), (a,), (b,)), ((out,), (t_b,), (t_a,)) = ins, outs
    grad = join(g_refs)
    low = mm_t(grad, b[...]).astype(BF)
    t_b[...] = t_mm(rank[...], grad)
    t_a[...] = t_mm(low, att[...])
    need(0)
    out[...] = (mm_t(grad, ws[0][...]) + mm(low, a[...])).astype(BF)


def mlp_forward_kernel(ws, ins, outs, need):
    x_refs, (a1,), (b1,), (a2,), (b2,) = ins
    out, (act_out,), (slope_out,), (rank1_out,), (rank2_out,) = outs
    x = join(x_refs)
    rank1 = mm_t(x, a1[...]).astype(BF)
    rank1_out[...] = rank1
    low1 = mm(rank1, b1[...])
    need(0)
    hidden = mm(x, ws[0][...]) + low1
    square = hidden * hidden
    bend = jnp.tanh(0.7978845608028654 * hidden * (1.0 + 0.044715 * square))
    half = 0.5 * (1.0 + bend)
    act = (hidden * half).astype(BF)
    act_out[...] = act
    slope = half + 0.5 * hidden * (1.0 - bend * bend) * (
        0.7978845608028654 * (1.0 + 0.134145 * square)
    )
    slope_out[...] = slope.astype(BF)
    rank2 = mm_t(act, a2[...]).astype(BF)
    rank2_out[...] = rank2
    need(1)
    split(mm(act, ws[1][...]) + mm(rank2, b2[...]), out)


def mlp_backward_kernel(ws, ins, outs, need):
    g_refs, x_refs, (act,), (slope,), (rank1,), (rank2,), (a1,), (b1,), (a2,), (b2,) = ins
    out, (t_b1,), (t_a2,), (t_b2,), (t_a1,) = outs
    grad = join(g_refs)
    low2 = mm_t(grad, b2[...]).astype(BF)
    t_b2[...] = t_mm(rank2[...], grad)
    t_a2[...] = t_mm(low2, act[...])
    need(1)
    grad_act = mm_t(grad, ws[1][...]) + mm(low2, a2[...])
    gh = (grad_act * slope[...].astype(F32)).astype(BF)
    low1 = mm_t(gh, b1[...]).astype(BF)
    t_b1[...] = t_mm(rank1[...], gh)
    t_a1[...] = t_mm(low1, join(x_refs))
    need(0)
    split(mm_t(gh, ws[0][...]) + mm(low1, a1[...]), out)


def project(kernel, offs, matrices, ins, outs, first):
    arrays, specs, counts = [], [], []
    for group in ins:
        counts.append(len(group))
        for item in group:
            if isinstance(item, tuple):
                array, row, rows = item
                arrays.append(array)
                specs.append(pl.BlockSpec((rows, array.shape[1]), lambda i, at=row // rows: (at, 0)))
            else:
                arrays.append(item)
                specs.append(pl.BlockSpec(item.shape, lambda i: (0, 0)))
    sources, plan = [], []
    order = [first] + [m for m in range(len(matrices)) if m != first]
    for m in order:
        base = len(sources)
        sources += matrices[m].sources
        plan += [(base + p[0],) + p[1:4] + (m,) + p[4:] for p in matrices[m].plan]
    shapes = [jax.ShapeDtypeStruct(*o) for group in outs for o in group]
    n_in, n_src, n_out, n_mat = len(arrays), len(sources), len(shapes), len(matrices)

    def groups(refs, sizes):
        result, i = [], 0
        for n in sizes:
            result.append(list(refs[i : i + n]))
            i += n
        return result

    def body(offs_ref, *refs):
        in_refs, refs = refs[:n_in], refs[n_in:]
        src_refs, refs = refs[:n_src], refs[n_src:]
        out_refs, refs = refs[:n_out], refs[n_out:]
        w_refs, sems = refs[:n_mat], refs[n_mat]
        start, wait = copies(offs_ref, plan, src_refs, w_refs, sems)
        start()
        kernel(w_refs, groups(in_refs, counts), groups(out_refs, [len(g) for g in outs]), lambda m: wait([m]))

    flops = sum(4 * outs[0][0][0][0] * len(outs[0]) * m.shape[0] * m.shape[1] for m in matrices)
    moved = sum(2 * m.shape[0] * m.shape[1] for m in matrices) + sum(2 * s.size for s in shapes)
    results = pl.pallas_call(
        body,
        grid=(1,),
        in_specs=[SCALARS] + specs + [ANY] * n_src,
        out_specs=[pl.BlockSpec(s.shape, lambda i: (0, 0)) for s in shapes],
        out_shape=shapes,
        scratch_shapes=[pltpu.VMEM(m.shape, BF) for m in matrices] + [pltpu.SemaphoreType.DMA((len(plan),))],
        compiler_params=pltpu.CompilerParams(vmem_limit_bytes=56 * 1024 * 1024),
        cost_estimate=pl.CostEstimate(flops=flops, transcendentals=0, bytes_accessed=moved),
    )(offs, *arrays, *sources)
    return groups(results, [len(g) for g in outs])


class Stream:
    pass


def powers(size):
    bits, bit = [], 1
    while bit < size:
        bits.append(bit)
        bit *= 2
    return bits


def body(
    mesh_shape,
    image_input,
    text_input,
    cond,
    image_cotangent,
    text_cotangent,
    live,
    slot_adapter_index,
    modulation_weight,
    query_key_value_weight,
    output_weight,
    first_feed_weight,
    second_feed_weight,
    adapter_down_table,
    adapter_up_table,
    modulation_up_factor,
    query_key_value_up,
    first_feed_up,
    output_down_factor,
    second_feed_down,
):
    R, F, T = mesh_shape
    H = T // CORES
    X = R // CORES
    W = image_input.shape[-1]
    wq = W // T
    Rf = modulation_up_factor.shape[1]
    Rq = adapter_down_table.shape[2]
    ffq = first_feed_weight.shape[-1]
    r = lax.axis_index("rep")
    f = lax.axis_index("fsdp")
    z = lax.axis_index("tp")
    core = lax.rem(r, CORES)
    xi = lax.div(r, CORES)
    high = lax.div(z, H)
    native = core == high

    def xz(v, bit):
        return lax.ppermute(v, "tp", [(i, i ^ bit) for i in range(T)])

    def xf(v, bit):
        return lax.ppermute(v, "fsdp", [(i, i ^ bit) for i in range(F)])

    def xr(v, bit):
        return lax.ppermute(v, "rep", [(i, i ^ bit) for i in range(R)])

    swap_pairs, across_pairs = [], []
    for a in range(R):
        for b in range(T):
            if a % CORES != b // H:
                swap_pairs.append((a * T + b, (a ^ 1) * T + (b ^ H)))
                across_pairs.append((a * T + b, (a ^ 2) * T + b))

    def swap(v):
        return lax.ppermute(v, ("rep", "tp"), swap_pairs)

    def swap_across(v):
        return lax.ppermute(v, ("rep", "tp"), across_pairs)

    def exchange(v):
        return jnp.where(native, v, swap(v))

    lanes = {}

    def queue(lane, step, value, *more):
        if lane in lanes:
            _, value = lax.optimization_barrier((lanes[lane], value))
        lanes[lane] = step(value, *more)
        return lanes[lane]

    LX, LY, LZ = range(3)

    def due(value, *arrived):
        return lax.optimization_barrier((value, arrived))[0]

    def gather_by(v, step, bits):
        return gather_by_more(v[None], step, bits)

    def gather_by_more(blocks, step, bits):
        for bit in bits:
            blocks = jnp.concatenate([blocks, step(blocks, bit)], axis=0)
        return blocks

    x_bits = [b for b in powers(R) if b > 1]
    h_bits = powers(H)
    t_bits = powers(T)
    f_bits = powers(F)
    arange_t = jnp.arange(T, dtype=jnp.int32)

    def gather_group(v):
        blocks = [v]
        for bit in h_bits:
            blocks = blocks + [xz(b, bit) for b in blocks]
        return blocks + [xr(b, 1) for b in blocks]

    def fold_cores(blocks):
        return [blocks[i].astype(F32) + xr(blocks[H + i], 1).astype(F32) for i in range(H)]

    def fold_chips(keep):
        sent = None
        for bit in reversed(h_bits):
            out = [k.astype(BF) for k in keep[bit:]]
            sent = out if sent is None else sent
            keep = [keep[i] + xz(out[i], bit).astype(F32) for i in range(bit)]
        return keep[0], sent

    def gather_texts(pair):
        rows = pair[0].shape[0]
        blocks = gather_by(jnp.concatenate(pair, axis=0), xz, t_bits)
        blocks = jnp.take(blocks, jnp.bitwise_xor(z, arange_t), axis=0)
        return [blocks[:, i * rows : (i + 1) * rows].reshape(T * rows, W) for i in range(2)]

    def bit_of(index, bit):
        return lax.rem(lax.div(index, bit), 2)

    def sum_text(v):
        for bit in t_bits:
            v = v + xz(v, bit)
        return v

    def own_rows_of(v):
        rows = v.shape[0] // T
        return lax.dynamic_slice_in_dim(v, z * rows, rows, axis=0)

    def scatter_rows(v):
        for bit in reversed(t_bits):
            half = v.shape[0] // 2
            mine = bit_of(z, bit) == 0
            low, high_part = v[:half], v[half:]
            out = jnp.where(mine, high_part, low).astype(BF)
            v = jnp.where(mine, low, high_part).astype(F32) + xz(out, bit).astype(F32)
        return v

    def scatter_columns(rows, steps):
        for step, bit, mine in steps:
            half = rows.shape[1] // 2
            low, high_part = rows[:, :half], rows[:, half:]
            rows = jnp.where(mine == 0, low, high_part) + step(jnp.where(mine == 0, high_part, low), bit)
        return rows

    img_steps = [(xr, 1, core)] + [(xz, bit, bit_of(z, bit)) for bit in reversed(h_bits)]
    txt_steps = [(xz, bit, bit_of(z, bit)) for bit in reversed(t_bits)]

    silu = jax.nn.silu(cond).astype(BF)
    info = jnp.concatenate(
        [
            silu.astype(F32),
            jnp.broadcast_to(slot_adapter_index.astype(F32)[:, None], (1, 64)),
            jnp.broadcast_to(live.astype(F32)[:, None], (1, 64)),
        ],
        axis=1,
    )
    info_f = gather_by(info[0], xf, f_bits)
    silu_f = info_f[:, :W].astype(BF)
    ids_f = info_f[:, W].astype(jnp.int32)

    row_ids = f * Rf + jnp.arange(Rf, dtype=jnp.int32)
    row_adapter = lax.div(row_ids, RANK)
    rows_d = modulation_weight.shape[1]

    def condition_ranks(silu_rows):
        held = jnp.einsum("fd,kid->fki", silu_rows, adapter_down_table[0], preferred_element_type=F32)
        spread = jnp.take(gather_by(held, xz, t_bits), jnp.bitwise_xor(z, arange_t), axis=0)
        return jnp.moveaxis(spread, 0, 2).reshape(silu_rows.shape[0], 2, Rf)

    def partial_modulation(ranks):
        own_rows = (row_adapter[None] == ids_f[:, None])[:, None, :]
        rank_rows = jnp.where(own_rows, ranks, 0.0).astype(BF)
        silu_rows = lax.dynamic_slice_in_dim(silu_f, f * rows_d, rows_d, axis=1)
        parts = []
        for k in range(2):
            parts.append(
                jnp.einsum("fd,dcj->fcj", silu_rows, modulation_weight[k], preferred_element_type=F32)
                + jnp.einsum(
                    "fr,rcj->fcj", rank_rows[:, k], modulation_up_factor[k], preferred_element_type=F32
                )
            )
        return jnp.stack(parts, axis=1)

    def modulation_shard(partial_mod):
        total_mod = partial_mod[0]
        for d in range(1, F):
            total_mod = total_mod + xf(partial_mod[d], d)
        return total_mod

    def modulation(mod_shard):
        mod_rel = gather_by(mod_shard, xz, t_bits)
        mod_abs = jnp.take(mod_rel, jnp.bitwise_xor(z, arange_t), axis=0)
        return jnp.moveaxis(mod_abs, 0, 2).reshape(2, 6, W)

    def both_modulations(mod_all):
        mine = jnp.concatenate([mod_all[0], jnp.broadcast_to(text.live, (1, W))], axis=0)
        both = jnp.where(native, mine, xr(mine, 1))
        image.live = both[6:7]
        return both[:6], mod_all[1]

    base_row = f * Rf + z * Rq

    def own_table_rows(ident, kinds):
        table = jnp.concatenate(kinds, axis=2)
        wanted = ident * RANK + jnp.arange(RANK, dtype=jnp.int32)
        held = base_row + jnp.arange(Rq, dtype=jnp.int32)
        if Rq == RANK:
            return jnp.where(ident * RANK == base_row, table, jnp.zeros_like(table))
        match = (wanted[:, None] == held[None, :]).astype(BF)
        return jnp.einsum("ir,srw->siw", match, table, preferred_element_type=F32).astype(BF)

    def own_columns(ident, kinds):
        start = ident * RANK - f * Rf
        inside = (start >= 0) & (start <= Rf - RANK)
        first = jnp.clip(start, 0, Rf - RANK)
        taken = jnp.concatenate(
            [lax.dynamic_slice_in_dim(k, first, RANK, axis=1) for k in kinds], axis=2
        )
        return jnp.where(inside, taken, jnp.zeros_like(taken))

    def fetch_adapters(tables, columns, after):
        tables, columns = due((tables, columns), after)
        both = [
            jnp.concatenate([own_table_rows(ids_f[d], tables), own_columns(ids_f[d], columns)], axis=2)
            for d in range(F)
        ]
        rows = both[0]
        for d in range(1, F):
            rows = rows + queue(LY, xf, both[d], d)
        yield rows
        cut = len(tables) * W
        table_rows, column_rows = rows[:, :, :cut], rows[:, :, cut:]
        for bit in t_bits:
            if bit < H:
                table_rows = table_rows + xz(table_rows, bit)
            else:
                table_rows = table_rows + queue(LZ, xz, table_rows, bit)
        rows_img = jnp.where(native, table_rows[0], xr(table_rows[0], 1))
        cols_img = jnp.where(native, column_rows[0], queue(LZ, swap, column_rows[0]))

        def pieces(array, widths):
            result, at = [], 0
            for n in widths:
                result.append(array[:, at : at + n])
                at += n
            return result

        table_widths = [t.shape[2] for t in tables]
        column_widths = [c.shape[2] for c in columns]
        yield (
            pieces(rows_img, table_widths) + pieces(cols_img, column_widths),
            pieces(table_rows[1], table_widths) + pieces(column_rows[1], column_widths),
        )

    image, text = Stream(), Stream()
    text.live = live.astype(F32)[0]
    qkv_planes = lax.optimization_barrier(jnp.moveaxis(query_key_value_weight, 2, 1))
    sub, ffh, wh = rows_d // 2, ffq // 2, wq // 2
    xb, cb = lax.rem(xi, 2), core
    entries = [native.astype(jnp.int32)]

    def slot(value):
        entries.append(value)
        return Slot(len(entries) - 1)

    def fetch_first(after):
        return fetch_adapters(
            [adapter_down_table[1], adapter_up_table[0], adapter_down_table[2], adapter_up_table[1]],
            [query_key_value_up.reshape(2, Rf, 3 * wq), output_down_factor, first_feed_up, second_feed_down],
            after,
        )

    def norm_first():
        for s, mod, tokens in ((image, mods[0], img), (text, mods[1], text_tokens)):
            s.xf = tokens.astype(F32)
            s.hat1, s.inv1 = norm_rows(s.xf)
            s.normed = (s.hat1 * (1.0 + mod[1:2]) + mod[0:1]).astype(BF)

    if F == 2 and X == 2 and rows_d % 128 == 0 and wh % 16 == 0 and sub % 16 == 0:
        own, other = slot(f * rows_d), slot((1 - f) * rows_d)
        own_x, own_y = slot(f * rows_d + xb * sub), slot(f * rows_d + (1 - xb) * sub)
        other_x, other_y = slot((1 - f) * rows_d + xb * sub), slot((1 - f) * rows_d + (1 - xb) * sub)
        other_c, other_d = slot((1 - f) * rows_d + cb * sub), slot((1 - f) * rows_d + (1 - cb) * sub)
        half_x, half_y = slot(xb * ffh), slot((1 - xb) * ffh)
        half_c, half_d = slot(cb * ffh), slot((1 - cb) * ffh)
        att_c, att_d = slot(cb * wh), slot((1 - cb) * wh)

        def piece(weight, k, which, rows):
            start = (k,) + (0,) * (weight.ndim - 3) + (which * rows, 0)
            return lax.dynamic_slice(weight, start, (1,) + weight.shape[1:-2] + (rows, weight.shape[-1]))[0]

        def planes(weight, plan, k):
            if weight.ndim == 3:
                return plan
            n = weight.shape[-1]
            return [
                (p[0], c if p[1] is None else (k, c)) + p[2:5] + (c * n,) + p[6:]
                for p in plan
                for c in range(weight.shape[1])
            ]

        def width(weight):
            return weight.shape[-1] * (1 if weight.ndim == 3 else weight.shape[1])

        def image_pieces(weight, rows):
            mine = piece(weight, 0, xb, rows)
            a0 = queue(LZ, swap, mine)
            after = yield a0
            if after is not None:
                a0 = due(a0, after)
            a1 = queue(LX, swap_across, a0)
            b0 = queue(LY, xf, jnp.where(native, mine, a0), 1)
            after = yield a1, b0
            if after is not None:
                b0 = due(b0, after)
            yield [weight, a0, a1, b0, queue(LX, xr, b0, 2)]

        def image_in(weight, sources):
            n = weight.shape[-1]
            plan = [
                (0, 0, rows_d, n, own, 0, 1),
                (1, None, sub, n, own_x, 0, 0),
                (2, None, sub, n, own_y, 0, 0),
                (3, None, sub, n, other_x, 0, None),
                (4, None, sub, n, other_y, 0, None),
            ]
            return Matrix((W, width(weight)), sources, planes(weight, plan, 0))

        def image_out(sources):
            plan = [
                (0, 0, ffq, rows_d, 0, own, 1),
                (1, None, ffh, rows_d, half_x, own, 0),
                (2, None, ffh, rows_d, half_y, own, 0),
                (3, None, ffh, rows_d, half_x, other, None),
                (4, None, ffh, rows_d, half_y, other, None),
            ]
            return Matrix((ffq, W), sources, plan)

        def text_piece(weight, rows):
            b0 = queue(LY, xf, piece(weight, 1, cb, rows), 1)
            return [weight, b0, xr(b0, 1)]

        def text_in(weight):
            n = weight.shape[-1]
            plan = [
                (0, 1, rows_d, n, own, 0, None),
                (1, None, sub, n, other_c, 0, None),
                (2, None, sub, n, other_d, 0, None),
            ]
            return Matrix((W, width(weight)), text_piece(weight, sub), planes(weight, plan, 1))

        def text_out(weight, rows, slot_c, slot_d):
            plan = [
                (0, 1, 2 * rows, rows_d, 0, own, None),
                (1, None, rows, rows_d, slot_c, other, None),
                (2, None, rows, rows_d, slot_d, other, None),
            ]
            return Matrix((2 * rows, W), text_piece(weight, rows), plan)

        get_qkv = image_pieces(qkv_planes, sub)
        a0_qkv = next(get_qkv)
        text.w_qkv = text_in(due(qkv_planes, info_f))
        ranks = due(condition_ranks(silu_f), a0_qkv)
        img_swap = queue(LZ, swap, due(image_input[0], ranks))
        img = jnp.where(native, image_input[0], img_swap)
        shard = modulation_shard(due(partial_modulation(ranks), text.w_qkv.sources[1]))
        text_tokens, text.cot = gather_texts(due((text_input[0], text_cotangent[0]), shard))
        get_first = fetch_first(shard)
        next(get_first)
        a1_qkv, b0_qkv = get_qkv.send(shard)
        mods = both_modulations(due(modulation(shard), img_swap))
        norm_first()
        first_img, first_txt = next(get_first)
        image.w_qkv = image_in(qkv_planes, next(get_qkv))
        image.n1 = gather_group(image.normed)
        image.n1[1] = due(image.n1[1], a1_qkv, b0_qkv)
        rest = (output_weight, first_feed_weight, second_feed_weight, image_cotangent)
        _, rest = lax.optimization_barrier((image.normed, rest))
        text.w_out = text_out(rest[0], wh, att_c, att_d)
        text.w_fc1 = text_in(rest[1])
        text.w_fc2 = text_out(rest[2], ffh, half_c, half_d)
        rest = due(rest, image.n1[1])
        output_weight, first_feed_weight, second_feed_weight, image_cotangent = rest
        flight = Stream()

        def bulk(stage, value):
            if stage == 0:
                flight.out = output_weight[0]
                flight.a_out = queue(LZ, swap, flight.out)
                flight.get_fc1 = image_pieces(first_feed_weight, sub)
                flight.a0_fc1 = next(flight.get_fc1)
            elif stage == 1:
                flight.a_out, flight.a0_fc1 = due((flight.a_out, flight.a0_fc1), value)
                b_out = queue(LY, xf, jnp.where(native, flight.out, flight.a_out), 1)
                image.w_out = Matrix(
                    (wq, W),
                    [output_weight, flight.a_out, b_out],
                    [
                        (0, 0, wq, rows_d, 0, own, 1),
                        (1, None, wq, rows_d, 0, own, 0),
                        (2, None, wq, rows_d, 0, other, None),
                    ],
                )
                flight.part_fc1 = flight.get_fc1.send(value)
                flight.get_fc2 = image_pieces(due(second_feed_weight, value), ffh)
                flight.a0_fc2 = next(flight.get_fc2)
                return [flight.a_out]
            elif stage == 2:
                image.w_fc1 = image_in(first_feed_weight, flight.get_fc1.send(value))
                return [flight.part_fc1[0]]
            elif stage == 3:
                flight.part_fc2 = flight.get_fc2.send(value)
                return [flight.part_fc1[1], flight.a0_fc2]
            else:
                image.w_fc2 = image_out(flight.get_fc2.send(value))
                image.cot = jnp.where(
                    native, image_cotangent[0], queue(LZ, swap, due(image_cotangent[0], value))
                )
                return list(flight.part_fc2) + [image.w_fc1.sources[4]]
            return []

    else:

        def bulk(stage, value):
            return []

        def place(shape, pieces, axis):
            full = jnp.zeros(shape, BF)
            for piece, offset in pieces:
                full = lax.dynamic_update_slice_in_dim(full, piece, offset, axis=axis)
            return full

        def fetch_image(weight, axis):
            rows, cols = weight.shape
            part = rows // X
            mine = lax.dynamic_slice_in_dim(weight, xi * part, part, axis=0)
            moved = gather_by(exchange(mine), xr, x_bits)
            held = place((rows, cols), [(moved[e], (xi ^ e) * part) for e in range(X)], 0)
            held = jnp.where(native, weight, held)
            full_shape = (rows * F, cols) if axis == 0 else (rows, cols * F)
            size = weight.shape[axis]
            full = place(full_shape, [(held, f * size)], axis)
            for d in range(1, F):
                full = lax.dynamic_update_slice_in_dim(full, xf(held, d), (f ^ d) * size, axis=axis)
            return full

        def fetch_text(weight, axis):
            rows, cols = weight.shape
            part = rows // R
            mine = lax.dynamic_slice_in_dim(weight, r * part, part, axis=0)
            full_shape = (rows * F, cols) if axis == 0 else (rows, cols * F)
            size = weight.shape[axis]
            full = place(full_shape, [(weight, f * size)], axis)
            for d in range(1, F):
                pieces = gather_by(xf(mine, d), xr, x_bits + [1])
                order = [0]
                for bit in x_bits + [1]:
                    order = order + [o ^ bit for o in order]
                for e in range(R):
                    start = [0, 0]
                    start[axis] = (f ^ d) * size
                    start[0] = start[0] + (r ^ order[e]) * part
                    full = lax.dynamic_update_slice(full, pieces[e], start)
            return full

        def whole(full):
            rows, cols = full.shape
            return Matrix(full.shape, [full], [(0, None, rows, cols, 0, 0, None)])

        qkv_native = query_key_value_weight.reshape(2, rows_d, 3 * wq)
        img = exchange(image_input[0])
        image.cot = exchange(image_cotangent[0])
        shard = modulation_shard(partial_modulation(condition_ranks(silu_f)))
        text_tokens, text.cot = gather_texts((text_input[0], text_cotangent[0]))
        mods = both_modulations(modulation(shard))
        _, (first_img, first_txt) = fetch_first(shard)
        norm_first()
        image.n1 = gather_group(image.normed)
        for s, k, fetch in ((image, 0, fetch_image), (text, 1, fetch_text)):
            s.w_qkv = whole(fetch(qkv_native[k], 0))
            s.w_out = whole(fetch(output_weight[k], 1))
            s.w_fc1 = whole(fetch(first_feed_weight[k], 0))
            s.w_fc2 = whole(fetch(second_feed_weight[k], 1))
    offs = jnp.stack(entries).astype(jnp.int32)
    streams = (image, text)
    for s, mod, tokens, first in (
        (image, mods[0], img, first_img),
        (text, mods[1], text_tokens, first_txt),
    ):
        s.mod, s.x = mod, tokens
        s.a_qkv, s.b_out, s.a_fc1, s.b_fc2, s.b_qkv, s.a_out, s.b_fc1, s.a_fc2 = first

    near = [0, H]
    far = [i for i in range(T) if i not in near]
    flow = near + far
    image.size, text.size = image.x.shape[0], text.x.shape[0]
    image.once, image.twice = [flow], [near, far]
    text.once = text.twice = [[0]]
    img_len = T * image.size

    def scatter_image(blocks, parts):
        placed = [None] * T
        for i, v in zip([i for part in parts for i in part], blocks):
            placed[i] = v
        return fold_chips(fold_cores(placed))

    def windows(s, array, parts):
        result, row = [], 0
        for part in parts:
            rows = len(part) * s.size
            result.append((array, row, rows))
            row += rows
        return result

    def own_part(s, v):
        return own_rows_of(v) if s is text else v

    def total(results):
        value = results[0]
        for more in results[1:]:
            value = value + more
        return value

    def blocks_out(s, part):
        return [((s.size, W), BF)] * len(part)

    def qkv_forward(s):
        s.joint, s.rank_qkv = [], []
        for part in s.twice:
            rows = len(part) * s.size
            (out,), (rank,) = project(
                qkv_forward_kernel, offs, [s.w_qkv],
                [[s.n1[i] for i in part], [s.a_qkv], [s.b_qkv]],
                [[((rows, 3 * wq), BF)], [((rows, RANK), BF)]], 0,
            )
            s.joint.append(out)
            s.rank_qkv.append(rank)

    def out_forward(s):
        rows = len(s.once[0]) * s.size
        partial, (s.rank_out,) = project(
            out_forward_kernel, offs, [s.w_out], [windows(s, s.att, s.once), [s.a_out], [s.b_out]],
            [blocks_out(s, s.once[0]), [((rows, RANK), BF)]], 0,
        )
        return partial

    def second_norm(s, branch):
        mod = s.mod
        s.br_attn = branch
        s.after = s.xf + mod[2:3] * branch
        s.hat2, s.inv2 = norm_rows(s.after)
        return (s.hat2 * (1.0 + mod[4:5]) + mod[3:4]).astype(BF)

    def mlp_forward(s):
        s.saved, partial = [], []
        for part in s.twice:
            rows = len(part) * s.size
            out, *saved = project(
                mlp_forward_kernel, offs, [s.w_fc1, s.w_fc2],
                [[s.n2[i] for i in part], [s.a_fc1], [s.b_fc1], [s.a_fc2], [s.b_fc2]],
                [
                    blocks_out(s, part), [((rows, ffq), BF)], [((rows, ffq), BF)],
                    [((rows, RANK), BF)], [((rows, RANK), BF)],
                ],
                0,
            )
            partial += out
            s.saved.append([v[0] for v in saved])
        return partial

    def mlp_backward(s):
        partial, sums = [], []
        for part, (act, slope, rank1, rank2) in zip(s.twice, s.saved):
            out, *more = project(
                mlp_backward_kernel, offs, [s.w_fc1, s.w_fc2],
                [
                    [s.gb_mlp[i] for i in part], [s.n2[i] for i in part], [act], [slope], [rank1], [rank2],
                    [s.a_fc1], [s.b_fc1], [s.a_fc2], [s.b_fc2],
                ],
                [blocks_out(s, part)] + [[((RANK, n), F32)] for n in (ffq, ffq, W, W)],
                1,
            )
            partial += out
            sums.append([m[0] for m in more])
        s.t_b_fc1, s.t_a_fc2, s.t_back1, s.t_in2 = [total(t) for t in zip(*sums)]
        return partial

    def second_norm_back(s, gn2):
        mod = s.mod
        s.gs_mlp = jnp.sum(own_part(s, gn2), axis=0)
        s.gc_mlp = jnp.sum(own_part(s, gn2 * s.hat2), axis=0)
        s.g_after = s.g2 + norm_back(gn2 * (1.0 + mod[4:5]), s.hat2, s.inv2)
        s.gg_attn = jnp.sum(own_part(s, s.g_after * s.br_attn), axis=0)
        return (mod[2:3] * s.g_after).astype(BF)

    def out_backward(s, gb):
        s.g_att, sums = [], []
        atts, ranks = windows(s, s.att, s.twice), windows(s, s.rank_out, s.twice)
        for part, att, rank in zip(s.twice, atts, ranks):
            rows = len(part) * s.size
            (out,), *more = project(
                out_backward_kernel, offs, [s.w_out],
                [[gb[i] for i in part], [att], [rank], [s.a_out], [s.b_out]],
                [[((rows, wq), BF)], [((RANK, W), F32)], [((RANK, wq), F32)]], 0,
            )
            s.g_att.append(out)
            sums.append([m[0] for m in more])
        s.t_back0, s.t_a_out = [total(t) for t in zip(*sums)]

    def qkv_backward(s):
        partial, (s.t_b_qkv,), (s.t_in1,) = project(
            qkv_backward_kernel, offs, [s.w_qkv],
            [windows(s, s.g_joint, s.once), [s.n1[i] for i in s.once[0]], s.rank_qkv, [s.a_qkv], [s.b_qkv]],
            [blocks_out(s, s.once[0]), [((RANK, 3 * wq), F32)], [((RANK, W), F32)]], 0,
        )
        return partial

    text.n1 = [due(text.normed, image.normed)]
    qkv_forward(text)
    bulk(0, image.n1[1])
    qkv_forward(image)
    arrived = bulk(1, image.joint[0])
    joints = [(j, None) for j in image.joint] + [(text.joint[0], 1), (swap(text.joint[0]), 0)]
    joints[0] = (due(joints[0][0], *arrived), None)
    attended, lse = attend_forward(offs, joints)
    attended = due(attended, *bulk(2, attended))
    image.att = attended
    img_partial = out_forward(image)
    arrived = bulk(3, img_partial[0])
    text.att = exchange(attended[img_len:])
    txt_partial = out_forward(text)
    branch, sent = scatter_image(img_partial, image.once)
    branch = due(branch, *arrived)
    txt_branch = sum_text(txt_partial[0]).astype(F32)
    normed = second_norm(image, branch)
    image.n2 = gather_group(normed)
    arrived = bulk(4, normed)
    late = image.w_fc2.sources[-1]
    image.g2 = image.cot.astype(F32) * image.live
    image.gb_mlp = gather_group(due((image.mod[5:6] * image.g2).astype(BF), image.n2[1]))
    text.n2 = [second_norm(text, txt_branch)]
    text.g2 = text.cot.astype(F32) * text.live
    text.gb_mlp = [(text.mod[5:6] * text.g2).astype(BF)]
    txt_done = mlp_forward(text)
    txt_partial = mlp_backward(text)
    txt_gn2 = sum_text(txt_partial[0]).astype(F32)
    image.n2[0] = due(image.n2[0], txt_partial)
    image.n2[1] = due(image.n2[1], *arrived)

    info_f = due(info_f, normed, late)
    info_all = gather_by(info_f, xr, [1] + x_bits)
    ids_all = info_all[:, :, W].astype(jnp.int32)
    silu_all = info_all[:, :, :W].astype(BF)
    rank_all = condition_ranks(silu_all.reshape(R * F, W))

    img_done = mlp_forward(image)
    out_backward(text, [second_norm_back(text, txt_gn2)])
    txt_grad = swap(text.g_att[0])
    image.gb_mlp[0] = due(image.gb_mlp[0], txt_grad)
    img_partial = mlp_backward(image)
    gn2, sent = scatter_image(img_partial, image.twice)

    gb = second_norm_back(image, gn2)
    gb_img = gather_group(gb)
    out_backward(image, gb_img)
    img_done, txt_done = due((img_done, txt_done), image.g_att)
    image.br_mlp, _ = scatter_image(img_done, image.twice)
    text.br_mlp = lax.psum_scatter(txt_done[0], "tp", scatter_dimension=0, tiled=True).astype(F32)
    for s in streams:
        s.out = ((own_part(s, s.after) + s.mod[5:6] * s.br_mlp) * s.live).astype(BF)
        s.gg_mlp = jnp.sum(own_part(s, s.g2) * s.br_mlp, axis=0)

    def combine_input(img_cols, txt_cols, rows):
        kinds = rows[0].shape[0] // RANK
        img_cols = exchange(jnp.concatenate(img_cols, axis=1).astype(BF))
        return jnp.concatenate(
            [img_cols] + [c.astype(BF) for c in txt_cols]
            + [r[i * RANK : (i + 1) * RANK] for r in rows for i in range(kinds)],
            axis=1,
        )

    def gather_all(pieces):
        return gather_by(gather_by(pieces, xf, f_bits), xr, [1] + x_bits)

    def combine(blocks, idents):
        flat = blocks.reshape(R * F * RANK, blocks.shape[-1])
        slots = (idents.reshape(R * F, 1) * RANK + jnp.arange(RANK, dtype=jnp.int32)).reshape(1, -1)
        place_rows = (row_ids[:, None] == slots).astype(BF)
        return mm(place_rows, flat)

    def reduce_rows(img_rows, txt_rows):
        return exchange(scatter_columns(img_rows, img_steps)), scatter_columns(txt_rows, txt_steps)

    def rows_home(rows):
        kinds = rows.shape[1]
        blocks = rows.astype(BF).reshape(T, Rq, kinds, wq)
        blocks = jnp.take(blocks, jnp.bitwise_xor(z, arange_t), axis=0)
        got = jnp.stack([blocks[0]] + [xz(blocks[d], d) for d in range(1, T)])
        got = jnp.take(got, jnp.bitwise_xor(z, arange_t), axis=0)
        return jnp.moveaxis(got, 0, 2).reshape(Rq, kinds, W).astype(F32)

    ids_in_order = jnp.take(
        jnp.take(ids_all, jnp.bitwise_xor(r, jnp.arange(R, dtype=jnp.int32)), axis=0),
        jnp.bitwise_xor(f, jnp.arange(F, dtype=jnp.int32)),
        axis=1,
    )
    early_blocks = lax.all_gather(
        combine_input(
            [image.t_b_fc1, image.t_a_fc2, image.t_a_out],
            [text.t_b_fc1, text.t_a_fc2, text.t_a_out],
            reduce_rows(
                *[jnp.concatenate([s.t_back1, s.t_in2, s.t_back0], axis=0).astype(BF) for s in streams]
            ),
        ),
        ("rep", "fsdp"),
    )

    grads = [(g, None) for g in image.g_att] + [(text.g_att[0], 1), (txt_grad, 0)]
    g_joint = attend_backward(offs, joints, grads, lse)
    g_joint = due(g_joint, image.br_mlp)
    out_swap = swap(image.out)
    image.g_joint = g_joint
    text.g_joint = exchange(g_joint[img_len:])
    img_partial = qkv_backward(image)
    keep = fold_cores([img_partial[flow.index(i)] for i in range(T)])
    gn1_img, sent = fold_chips(keep)
    text.g_joint = due(text.g_joint, sent)
    txt_partial = qkv_backward(text)
    late_in = combine_input(
        [image.t_b_qkv], [text.t_b_qkv], reduce_rows(image.t_in1.astype(BF), text.t_in1.astype(BF))
    )
    late_blocks = gather_all(late_in)
    gn1_img = due(gn1_img, out_swap)
    for s, gn1 in ((image, gn1_img), (text, scatter_rows(txt_partial[0]))):
        hat1, inv1, g_after = [own_part(s, v) for v in (s.hat1, s.inv1, s.g_after)]
        s.gs_attn = jnp.sum(gn1, axis=0)
        s.gc_attn = jnp.sum(gn1 * hat1, axis=0)
        dx = g_after + norm_back(gn1 * (1.0 + s.mod[1:2]), hat1, inv1)
        s.dx = dx.astype(BF)
    gm = jnp.stack(
        reduce_rows(
            *[
                jnp.stack([s.gs_attn, s.gc_attn, s.gg_attn, s.gs_mlp, s.gc_mlp, s.gg_mlp])
                for s in streams
            ]
        )
    ).astype(BF)
    gm_f = gather_by(gm, xf, f_bits)
    gm_all = gather_by(gm_f, xr, [1] + x_bits)
    early, late = combine(early_blocks, ids_in_order), combine(late_blocks, ids_all)
    span = 2 * ffq + wq
    grad_b_fc1 = jnp.stack([early[:, 0:ffq], early[:, span : span + ffq]])
    grad_a_fc2 = jnp.stack([early[:, ffq : 2 * ffq], early[:, span + ffq : span + 2 * ffq]])
    grad_a_out = jnp.stack([early[:, 2 * ffq : span], early[:, span + 2 * ffq : 2 * span]])
    grad_b_qkv = jnp.stack([late[:, : 3 * wq], late[:, 3 * wq : 6 * wq]]).reshape(2, Rf, 3, wq)
    home = rows_home(
        jnp.concatenate([early[:, 2 * span :], late[:, 6 * wq : 8 * wq]], axis=1).reshape(Rf, 8, wq)
    )

    seqs = R * F
    match = (row_adapter[None, :] == ids_all.reshape(seqs)[:, None]).astype(F32)
    gm_seq = gm_all.reshape(seqs, 2, 6, wq)
    rank_seq = (rank_all * match[:, None, :]).astype(BF)
    grad_b_ada, gcr = [], []
    for k in range(2):
        grad_b_ada.append(
            jnp.einsum("sr,scj->rcj", rank_seq[:, k], gm_seq[:, k], preferred_element_type=F32)
        )
        gcr.append(
            jnp.einsum(
                "scj,rcj->sr", gm_seq[:, k], modulation_up_factor[k], preferred_element_type=F32
            )
            * match
        )
    grad_b_ada = jnp.stack(grad_b_ada)
    gcr = jnp.stack(gcr, axis=1)
    gcr_rel = jnp.take(
        jnp.moveaxis(gcr.reshape(seqs, 2, T, Rq), 2, 0), jnp.bitwise_xor(z, arange_t), axis=0
    )
    gcr_own = gcr_rel[0]
    for d in range(1, T):
        gcr_own = gcr_own + xz(gcr_rel[d], d)
    grad_in0 = jnp.einsum(
        "ski,sd->kid",
        gcr_own,
        silu_all.reshape(seqs, W).astype(F32),
        precision=lax.Precision.HIGHEST,
    )
    gm_pair = gm_f
    dpart = jnp.zeros((F, rows_d), F32)
    for k in range(2):
        dpart = dpart + jnp.einsum(
            "fcj,dcj->fd", gm_pair[:, k], modulation_weight[k], preferred_element_type=F32
        )
    dfull = lax.dynamic_update_slice_in_dim(jnp.zeros((F, W), F32), dpart, f * rows_d, axis=1)
    dfull = dfull + jnp.einsum(
        "fki,kid->fd",
        gcr_own.reshape(R, F, 2, Rq)[0],
        adapter_down_table[0].astype(F32),
        precision=lax.Precision.HIGHEST,
    )
    dsum = dfull[0]
    for d in range(1, F):
        dsum = dsum + xf(dfull[d], d)
    for bit in t_bits:
        dsum = dsum + xz(dsum, bit)
    sigmoid = jax.nn.sigmoid(cond)
    dcond = dsum[None] * sigmoid * (1.0 + cond * (1.0 - sigmoid))

    grad_in = jnp.stack(
        [
            grad_in0,
            jnp.stack([home[:, 6], home[:, 7]]),
            jnp.stack([home[:, 1], home[:, 4]]),
        ]
    )
    grad_back = jnp.stack(
        [jnp.stack([home[:, 2], home[:, 5]]), jnp.stack([home[:, 0], home[:, 3]])]
    )
    return (
        jnp.where(native, image.out, out_swap)[None],
        text.out[None],
        exchange(image.dx)[None],
        text.dx[None],
        dcond,
        grad_in,
        grad_back,
        grad_b_ada,
        grad_b_qkv,
        grad_b_fc1,
        grad_a_out,
        grad_a_fc2,
    )


def solution(mesh):
    tokens = P(("rep", "fsdp"), "tp", None)
    table = P(None, None, ("fsdp", "tp"), None)
    columns4 = P(None, "fsdp", None, "tp")
    columns3 = P(None, "fsdp", "tp")
    rows3 = P(None, "tp", "fsdp")
    slot = P(("rep", "fsdp"))
    in_specs = (
        tokens, tokens, P(("rep", "fsdp"), None), tokens, tokens, slot, slot,
        columns4, columns4, rows3, columns3, rows3, table, table,
        columns4, columns4, columns3, columns3, columns3,
    )
    out_specs = (
        tokens, tokens, tokens, tokens, P(("rep", "fsdp"), None),
        table, table, columns4, columns4, columns3, columns3, columns3,
    )
    sizes = (mesh.shape["rep"], mesh.shape["fsdp"], mesh.shape["tp"])
    return jax.shard_map(
        functools.partial(body, sizes), mesh=mesh, in_specs=in_specs, out_specs=out_specs, check_vma=False
    )
```

```python
import functools

import jax
import jax.numpy as jnp
from jax import lax
from jax.experimental import pallas as pl
from jax.experimental.pallas import tpu as pltpu
from jax.sharding import PartitionSpec as P

HD = 64
RANK = 16
EPSILON = 1e-06
BF = jnp.bfloat16
F32 = jnp.float32
CORES = 2


def dot(left, right, dims):
    return lax.dot_general(left, right, (dims, ((), ())), preferred_element_type=F32)


def mm(left, right):
    return dot(left, right, ((left.ndim - 1,), (0,)))


def mm_t(left, right):
    return dot(left, right, ((left.ndim - 1,), (right.ndim - 1,)))


def t_mm(left, right):
    return dot(left, right, ((0,), (0,)))


def norm_rows(values):
    centred = values - jnp.mean(values, axis=-1, keepdims=True)
    inverse = lax.rsqrt(jnp.mean(centred * centred, axis=-1, keepdims=True) + EPSILON)
    return centred * inverse, inverse


def norm_back(grad_hat, hat, inverse):
    first = jnp.mean(grad_hat, axis=-1, keepdims=True)
    second = jnp.mean(grad_hat * hat, axis=-1, keepdims=True)
    return inverse * (grad_hat - first - hat * second)


def gelu_tanh(values):
    return jax.nn.gelu(values, approximate=True)


class Slot(int):
    pass


def spot(offs, where, step):
    if isinstance(where, Slot):
        return pl.multiple_of(offs[int(where)], step)
    return where


def copies(offs, plan, sources, targets, sems):
    def make(i):
        source, lead, rows, cols, target, row, col, _ = plan[i]
        ref = sources[source] if lead is None else sources[source].at[lead]
        dst = targets[target].at[pl.ds(spot(offs, row, 16), rows), pl.ds(spot(offs, col, 128), cols)]
        return pltpu.make_async_copy(ref, dst, sems.at[i])

    def each(action, chosen):
        for i in range(len(plan)):
            if chosen is not None and plan[i][4] not in chosen:
                continue
            case = plan[i][7]
            if case is None:
                action(make(i))
            else:

                @pl.when(offs[0] == case)
                def _(i=i):
                    action(make(i))

    return (
        lambda chosen=None: each(lambda c: c.start(), chosen),
        lambda chosen=None: each(lambda c: c.wait(), chosen),
    )


ANY = pl.BlockSpec(memory_space=pl.ANY)
SCALARS = pl.BlockSpec(memory_space=pltpu.SMEM)


def head_tiles(width):
    if width % 128 == 0:
        return [(p * 128, 128, 2) for p in range(width // 128)]
    return [(h * HD, HD, 1) for h in range(width // HD)]


def head_masks(rows, count):
    if count == 1:
        return [None]
    lane = lax.broadcasted_iota(jnp.int32, (rows, 128), 1)
    return [lane < HD, lane >= HD]


def pick(mask, values):
    return values if mask is None else jnp.where(mask, values, jnp.zeros_like(values))


def attend_forward_kernel(width, plan, offs, *refs):
    *sources, out_ref, lse_ref, kv_ref, sems = refs
    start_all, wait_all = copies(offs, plan, sources, [kv_ref], sems)
    step = pl.program_id(0)

    @pl.when(step == 0)
    def _():
        start_all()
        wait_all()

    rows = out_ref.shape[0]
    here = pl.ds(pl.multiple_of(step * rows, rows), rows)
    lses = []
    for start, size, count in head_tiles(width):
        queries = kv_ref[here, start : start + size] * jnp.asarray(HD ** (-0.5), BF)
        keys = kv_ref[:, width + start : width + start + size]
        values = kv_ref[:, 2 * width + start : 2 * width + start + size]
        total = None
        for mask in head_masks(rows, count):
            scores = mm_t(pick(mask, queries), keys)
            top = jnp.max(scores, axis=-1, keepdims=True)
            weights = jnp.exp(scores - top)
            norm = jnp.sum(weights, axis=-1, keepdims=True)
            part = mm(weights.astype(BF), values) * (1.0 / norm)
            part = pick(mask, part)
            total = part if total is None else total + part
            lses.append(top + jnp.log(norm))
        out_ref[:, start : start + size] = total.astype(BF)
    lse_ref[...] = jnp.concatenate(lses, axis=1)


def attend_backward_kernel(width, blocks, plan, offs, lse_ref, *refs):
    *sources, out_ref, kv_ref, grad_ref, dk_ref, dv_ref, sems = refs
    start_all, wait_all = copies(offs, plan, sources, [kv_ref, grad_ref], sems)
    step = pl.program_id(0)

    @pl.when(step == 0)
    def _():
        start_all()
        dk_ref[...] = jnp.zeros_like(dk_ref)
        dv_ref[...] = jnp.zeros_like(dv_ref)
        wait_all()

    rows = lse_ref.shape[0]
    here = pl.ds(pl.multiple_of(step * rows, rows), rows)
    head = 0
    for start, size, count in head_tiles(width):
        queries = kv_ref[here, start : start + size] * jnp.asarray(HD ** (-0.5), BF)
        keys = kv_ref[:, width + start : width + start + size]
        values = kv_ref[:, 2 * width + start : 2 * width + start + size]
        grads = grad_ref[here, start : start + size]
        grad_q = None
        for mask in head_masks(rows, count):
            queries_m = pick(mask, queries)
            grads_m = pick(mask, grads)
            scores = mm_t(queries_m, keys)
            probs = jnp.exp(scores - lse_ref[:, head : head + 1])
            grad_probs = mm_t(grads_m, values)
            product = probs * grad_probs
            inner = jnp.sum(product, axis=-1, keepdims=True)
            grad_scores = (product - probs * inner).astype(BF)
            part = pick(mask, mm(grad_scores, keys))
            grad_q = part if grad_q is None else grad_q + part
            dk_ref[:, start : start + size] += t_mm(grad_scores, queries_m)
            dv_ref[:, start : start + size] += t_mm(probs.astype(BF), grads_m)
            head += 1
        out_ref[here, start : start + size] = (grad_q * HD ** (-0.5)).astype(BF)

    @pl.when(step == blocks - 1)
    def _():
        out_ref[:, width : 2 * width] = dk_ref[...].astype(BF)
        out_ref[:, 2 * width :] = dv_ref[...].astype(BF)


def query_block(length):
    for rows in (256, 128, 64, 32, 16):
        if length % rows == 0:
            return rows
    return length


def stack_plan(arrays, target, first):
    plan, row = [], 0
    for i, (array, case) in enumerate(arrays):
        plan.append((first + i, None, array.shape[0], array.shape[1], target, row, 0, case))
        if case != 1:
            row += array.shape[0]
    return plan, row


def attend_forward(offs, joints):
    plan, length = stack_plan(joints, 0, 0)
    width3 = joints[0][0].shape[1]
    width = width3 // 3
    heads = width // HD
    rows = query_block(length)
    return pl.pallas_call(
        functools.partial(attend_forward_kernel, width, plan),
        grid=(length // rows,),
        in_specs=[SCALARS] + [ANY] * len(joints),
        out_specs=[
            pl.BlockSpec((rows, width), lambda i: (i, 0)),
            pl.BlockSpec((rows, heads), lambda i: (i, 0)),
        ],
        out_shape=[
            jax.ShapeDtypeStruct((length, width), BF),
            jax.ShapeDtypeStruct((length, heads), F32),
        ],
        scratch_shapes=[pltpu.VMEM((length, width3), BF), pltpu.SemaphoreType.DMA((len(plan),))],
        compiler_params=pltpu.CompilerParams(vmem_limit_bytes=40 * 1024 * 1024),
        cost_estimate=pl.CostEstimate(
            flops= 64 * 2 * length * length * width,
            transcendentals=length * length * heads,
            bytes_accessed=length * width3 * 4,
        ),
        name="attend_forward",
    )(offs, *[a for a, _ in joints])


def attend_backward(offs, joints, grads, lse):
    plan, length = stack_plan(joints, 0, 0)
    more, _ = stack_plan(grads, 1, len(joints))
    plan = plan + more
    width3 = joints[0][0].shape[1]
    width = width3 // 3
    heads = width // HD
    rows = query_block(length)
    blocks = length // rows
    return pl.pallas_call(
        functools.partial(attend_backward_kernel, width, blocks, plan),
        grid=(blocks,),
        in_specs=[SCALARS, pl.BlockSpec((rows, heads), lambda i: (i, 0))] + [ANY] * len(plan),
        out_specs=pl.BlockSpec((length, width3), lambda i: (0, 0)),
        out_shape=jax.ShapeDtypeStruct((length, width3), BF),
        scratch_shapes=[
            pltpu.VMEM((length, width3), BF),
            pltpu.VMEM((length, width), BF),
            pltpu.VMEM((length, width), F32),
            pltpu.VMEM((length, width), F32),
            pltpu.SemaphoreType.DMA((len(plan),)),
        ],
        compiler_params=pltpu.CompilerParams(vmem_limit_bytes=48 * 1024 * 1024),
        cost_estimate=pl.CostEstimate(
            flops= 128 * 2 * length * length * width,
            transcendentals=length * length * heads,
            bytes_accessed=length * width3 * 8,
        ),
        name="attend_backward",
    )(offs, lse, *[a for a, _ in joints], *[a for a, _ in grads])


class Matrix:
    def __init__(self, shape, sources, plan):
        self.shape, self.sources, self.plan = shape, sources, plan


def join(refs):
    if len(refs) == 1:
        return refs[0][...]
    return jnp.concatenate([r[...] for r in refs], axis=0)


def split(value, refs):
    row = 0
    for ref in refs:
        ref[...] = value[row : row + ref.shape[0]].astype(ref.dtype)
        row += ref.shape[0]


def qkv_forward_kernel(ws, ins, outs, need):
    (x_refs, (a,), (b,)), ((out,), (rank_out,)) = ins, outs
    x = join(x_refs)
    rank = mm_t(x, a[...]).astype(BF)
    rank_out[...] = rank
    low = mm(rank, b[...])
    need(0)
    out[...] = (mm(x, ws[0][...]) + low).astype(BF)


def qkv_backward_kernel(ws, ins, outs, need):
    ((g,), x_refs, ranks, (a,), (b,)), (out, (t_b,), (t_a,)) = ins, outs
    grad = g[...]
    low = mm_t(grad, b[...]).astype(BF)
    t_b[...] = t_mm(join(ranks), grad)
    t_a[...] = t_mm(low, join(x_refs))
    need(0)
    split(mm_t(grad, ws[0][...]) + mm(low, a[...]), out)


def out_forward_kernel(ws, ins, outs, need):
    ((att,), (a,), (b,)), (out, (rank_out,)) = ins, outs
    act = att[...]
    rank = mm_t(act, a[...]).astype(BF)
    rank_out[...] = rank
    need(0)
    split(mm(act, ws[0][...]) + mm(rank, b[...]), out)


def out_backward_kernel(ws, ins, outs, need):
    (g_refs, (att,), (rank,), (a,), (b,)), ((out,), (t_b,), (t_a,)) = ins, outs
    grad = join(g_refs)
    low = mm_t(grad, b[...]).astype(BF)
    t_b[...] = t_mm(rank[...], grad)
    t_a[...] = t_mm(low, att[...])
    need(0)
    out[...] = (mm_t(grad, ws[0][...]) + mm(low, a[...])).astype(BF)


def row_tile(rows):
    for tile in (224, 128, 112, 64, 32, 16):
        if rows % tile == 0:
            return tile
    return rows


def column_tiles(cols):
    tile = 512 if cols % 512 == 0 else cols
    return [(c, tile) for c in range(0, cols, tile)]


def by_rows(rows, step):
    tile = row_tile(rows)

    def run(i, carry):
        step(pl.ds(pl.multiple_of(i * tile, 16), tile))
        return carry

    lax.fori_loop(0, rows // tile, run, 0)


def mlp_forward_kernel(ws, ins, outs, need, gathered):
    (a1,), (b1,), (a2,), (b2,) = ins
    out, (act_out,), (slope_out,), (rank1_out,), (rank2_out,), (spill,) = outs
    (xs,) = gathered
    need(len(ws))
    need(0)

    def first(here):
        x = xs[here, :]
        rank1 = mm_t(x, a1[...]).astype(BF)
        rank1_out[here, :] = rank1
        for c, tile in column_tiles(act_out.shape[1]):
            hidden = mm(x, ws[0][:, c : c + tile]) + mm(rank1, b1[:, c : c + tile])
            square = hidden * hidden
            bend = jnp.tanh(hidden * (0.7978845608028654 + 0.035677408136300125 * square))
            half = 0.5 + 0.5 * bend
            act_out[here, c : c + tile] = (hidden * half).astype(BF)
            slope = half + (half * (1.0 - bend)) * hidden * (
                0.7978845608028654 + 0.10703222440890037 * square
            )
            slope_out[here, c : c + tile] = slope.astype(BF)

    by_rows(xs.shape[0], first)
    need(1)

    def second(here):
        act = act_out[here, :]
        rank2 = mm_t(act, a2[...]).astype(BF)
        rank2_out[here, :] = rank2
        for c, tile in column_tiles(spill.shape[1]):
            spill[here, c : c + tile] = (mm(act, ws[1][:, c : c + tile]) + mm(rank2, b2[:, c : c + tile])).astype(BF)

    by_rows(xs.shape[0], second)
    split(spill, out)


def mlp_backward_kernel(ws, ins, outs, need, gathered):
    (act,), (slope,), (rank1,), (rank2,), (a1,), (b1,), (a2,), (b2,) = ins
    out, (t_b1,), (t_a2,), (t_b2,), (t_a1,), (spill,) = outs
    gs, xs = gathered
    need(len(ws))
    need(1)
    t_b1[...] = jnp.zeros_like(t_b1)
    t_a2[...] = jnp.zeros_like(t_a2)
    t_b2[...] = jnp.zeros_like(t_b2)
    t_a1[...] = jnp.zeros_like(t_a1)

    def first(here):
        grad = gs[here, :]
        low2 = mm_t(grad, b2[...]).astype(BF)
        t_b2[...] += t_mm(rank2[here, :], grad)
        t_a2[...] += t_mm(low2, act[here, :])
        for c, tile in column_tiles(spill.shape[1]):
            part = mm_t(grad, ws[1][c : c + tile, :]) + mm(low2, a2[:, c : c + tile])
            spill[here, c : c + tile] = (part * slope[here, c : c + tile].astype(F32)).astype(BF)

    by_rows(gs.shape[0], first)
    need(len(ws) + 1)
    need(0)

    def second(here):
        gh = spill[here, :]
        low1 = mm_t(gh, b1[...]).astype(BF)
        t_b1[...] += t_mm(rank1[here, :], gh)
        t_a1[...] += t_mm(low1, xs[here, :])
        for c, tile in column_tiles(gs.shape[1]):
            gs[here, c : c + tile] = (mm_t(gh, ws[0][c : c + tile, :]) + mm(low1, a1[:, c : c + tile])).astype(BF)

    by_rows(gs.shape[0], second)
    split(gs, out)


def project(kernel, offs, matrices, ins, outs, first, blocks=(), spill=None):
    arrays, specs, counts = [], [], []
    for group in ins:
        counts.append(len(group))
        for item in group:
            if isinstance(item, tuple):
                array, row, rows = item
                arrays.append(array)
                specs.append(pl.BlockSpec((rows, array.shape[1]), lambda i, at=row // rows: (at, 0)))
            else:
                arrays.append(item)
                specs.append(pl.BlockSpec(item.shape, lambda i: (0, 0)))
    sources, plan = [], []
    order = [first] + [m for m in range(len(matrices)) if m != first]
    for m in order:
        base = len(sources)
        sources += matrices[m].sources
        plan += [(base + p[0],) + p[1:4] + (m,) + p[4:] for p in matrices[m].plan]
    scratch = []
    for i, group in enumerate(blocks):
        rows, cols = sum(g.shape[0] for g in group), group[0].shape[1]
        more, row = [], 0
        for g in group:
            more.append((len(sources), None, g.shape[0], cols, len(matrices) + i, row, 0, None))
            sources.append(g)
            row += g.shape[0]
        plan = more + plan if i == 0 else plan + more
        scratch.append(pltpu.VMEM((rows, cols), BF))
    n_blocks = len(scratch)
    if spill is not None:
        scratch.append(pltpu.VMEM(spill, BF))
    shapes = [jax.ShapeDtypeStruct(*o) for group in outs for o in group]
    n_in, n_src, n_out, n_mat = len(arrays), len(sources), len(shapes), len(matrices)

    def groups(refs, sizes):
        result, i = [], 0
        for n in sizes:
            result.append(list(refs[i : i + n]))
            i += n
        return result

    def body(offs_ref, *refs):
        in_refs, refs = refs[:n_in], refs[n_in:]
        src_refs, refs = refs[:n_src], refs[n_src:]
        out_refs, refs = refs[:n_out], refs[n_out:]
        *targets, sems = refs
        w_refs, gathered = targets[:n_mat], targets[n_mat : n_mat + n_blocks]
        start, wait = copies(offs_ref, plan, src_refs, targets[: n_mat + n_blocks], sems)
        start()
        results = groups(out_refs, [len(g) for g in outs])
        if n_blocks:
            results.append(targets[n_mat + n_blocks :])
            kernel(w_refs, groups(in_refs, counts), results, lambda m: wait([m]), gathered)
        else:
            kernel(w_refs, groups(in_refs, counts), results, lambda m: wait([m]))

    flops = sum(16 * outs[0][0][0][0] * len(outs[0]) * m.shape[0] * m.shape[1] for m in matrices)
    moved = sum(2 * m.shape[0] * m.shape[1] for m in matrices) + sum(2 * s.size for s in shapes)
    results = pl.pallas_call(
        body,
        grid=(1,),
        in_specs=[SCALARS] + specs + [ANY] * n_src,
        out_specs=[pl.BlockSpec(s.shape, lambda i: (0, 0)) for s in shapes],
        out_shape=shapes,
        scratch_shapes=[pltpu.VMEM(m.shape, BF) for m in matrices] + scratch + [pltpu.SemaphoreType.DMA((len(plan),))],
        compiler_params=pltpu.CompilerParams(vmem_limit_bytes=56 * 1024 * 1024),
        cost_estimate=pl.CostEstimate(flops=flops, transcendentals=0, bytes_accessed=moved),
    )(offs, *arrays, *sources)
    return groups(results, [len(g) for g in outs])


class Stream:
    pass


def powers(size):
    bits, bit = [], 1
    while bit < size:
        bits.append(bit)
        bit *= 2
    return bits


def body(
    mesh_shape,
    image_input,
    text_input,
    cond,
    image_cotangent,
    text_cotangent,
    live,
    slot_adapter_index,
    modulation_weight,
    query_key_value_weight,
    output_weight,
    first_feed_weight,
    second_feed_weight,
    adapter_down_table,
    adapter_up_table,
    modulation_up_factor,
    query_key_value_up,
    first_feed_up,
    output_down_factor,
    second_feed_down,
):
    R, F, T = mesh_shape
    H = T // CORES
    X = R // CORES
    W = image_input.shape[-1]
    wq = W // T
    Rf = modulation_up_factor.shape[1]
    Rq = adapter_down_table.shape[2]
    ffq = first_feed_weight.shape[-1]
    r = lax.axis_index("rep")
    f = lax.axis_index("fsdp")
    z = lax.axis_index("tp")
    core = lax.rem(r, CORES)
    xi = lax.div(r, CORES)
    high = lax.div(z, H)
    native = core == high

    def xz(v, bit):
        return lax.ppermute(v, "tp", [(i, i ^ bit) for i in range(T)])

    def xf(v, bit):
        return lax.ppermute(v, "fsdp", [(i, i ^ bit) for i in range(F)])

    def xr(v, bit):
        return lax.ppermute(v, "rep", [(i, i ^ bit) for i in range(R)])

    swap_pairs, across_pairs = [], []
    for a in range(R):
        for b in range(T):
            if a % CORES != b // H:
                swap_pairs.append((a * T + b, (a ^ 1) * T + (b ^ H)))
                across_pairs.append((a * T + b, (a ^ 2) * T + b))

    def swap(v):
        return lax.ppermute(v, ("rep", "tp"), swap_pairs)

    def swap_across(v):
        return lax.ppermute(v, ("rep", "tp"), across_pairs)

    def exchange(v):
        return jnp.where(native, v, swap(v))

    lanes = {}

    def queue(lane, step, value, *more):
        if lane in lanes:
            _, value = lax.optimization_barrier((lanes[lane], value))
        lanes[lane] = step(value, *more)
        return lanes[lane]

    LX, LY, LZ = range(3)

    def due(value, *arrived):
        return lax.optimization_barrier((value, arrived))[0]

    def gather_by(v, step, bits):
        return gather_by_more(v[None], step, bits)

    def gather_by_more(blocks, step, bits):
        for bit in bits:
            blocks = jnp.concatenate([blocks, step(blocks, bit)], axis=0)
        return blocks

    x_bits = [b for b in powers(R) if b > 1]
    h_bits = powers(H)
    t_bits = powers(T)
    f_bits = powers(F)
    arange_t = jnp.arange(T, dtype=jnp.int32)

    def gather_group(v):
        blocks = [v]
        for bit in h_bits:
            blocks = blocks + [xz(b, bit) for b in blocks]
        return blocks + [xr(b, 1) for b in blocks]

    def fold_cores(blocks):
        return [blocks[i].astype(F32) + xr(blocks[H + i], 1).astype(F32) for i in range(H)]

    def fold_chips(keep):
        sent = None
        for bit in reversed(h_bits):
            out = [k.astype(BF) for k in keep[bit:]]
            sent = out if sent is None else sent
            keep = [keep[i] + xz(out[i], bit).astype(F32) for i in range(bit)]
        return keep[0], sent

    def gather_texts(pair):
        rows = pair[0].shape[0]
        blocks = gather_by(jnp.concatenate(pair, axis=0), xz, t_bits)
        blocks = jnp.take(blocks, jnp.bitwise_xor(z, arange_t), axis=0)
        return [blocks[:, i * rows : (i + 1) * rows].reshape(T * rows, W) for i in range(2)]

    def bit_of(index, bit):
        return lax.rem(lax.div(index, bit), 2)

    def sum_text(v):
        for bit in t_bits:
            v = v + xz(v, bit)
        return v

    def own_rows_of(v):
        rows = v.shape[0] // T
        return lax.dynamic_slice_in_dim(v, z * rows, rows, axis=0)

    def scatter_rows(v):
        for bit in reversed(t_bits):
            half = v.shape[0] // 2
            mine = bit_of(z, bit) == 0
            low, high_part = v[:half], v[half:]
            out = jnp.where(mine, high_part, low).astype(BF)
            v = jnp.where(mine, low, high_part).astype(F32) + xz(out, bit).astype(F32)
        return v

    def scatter_columns(rows, steps):
        for step, bit, mine in steps:
            half = rows.shape[1] // 2
            low, high_part = rows[:, :half], rows[:, half:]
            rows = jnp.where(mine == 0, low, high_part) + step(jnp.where(mine == 0, high_part, low), bit)
        return rows

    img_steps = [(xr, 1, core)] + [(xz, bit, bit_of(z, bit)) for bit in reversed(h_bits)]
    txt_steps = [(xz, bit, bit_of(z, bit)) for bit in reversed(t_bits)]

    silu = jax.nn.silu(cond).astype(BF)
    info = jnp.concatenate(
        [
            silu.astype(F32),
            jnp.broadcast_to(slot_adapter_index.astype(F32)[:, None], (1, 64)),
            jnp.broadcast_to(live.astype(F32)[:, None], (1, 64)),
        ],
        axis=1,
    )
    info_f = gather_by(info[0], xf, f_bits)
    silu_f = info_f[:, :W].astype(BF)
    ids_f = info_f[:, W].astype(jnp.int32)

    row_ids = f * Rf + jnp.arange(Rf, dtype=jnp.int32)
    row_adapter = lax.div(row_ids, RANK)
    rows_d = modulation_weight.shape[1]

    def condition_ranks(silu_rows):
        held = jnp.einsum("fd,kid->fki", silu_rows, adapter_down_table[0], preferred_element_type=F32)
        spread = jnp.take(gather_by(held, xz, t_bits), jnp.bitwise_xor(z, arange_t), axis=0)
        return jnp.moveaxis(spread, 0, 2).reshape(silu_rows.shape[0], 2, Rf)

    def partial_modulation(ranks):
        own_rows = (row_adapter[None] == ids_f[:, None])[:, None, :]
        rank_rows = jnp.where(own_rows, ranks, 0.0).astype(BF)
        silu_rows = lax.dynamic_slice_in_dim(silu_f, f * rows_d, rows_d, axis=1)
        parts = []
        for k in range(2):
            parts.append(
                jnp.einsum("fd,dcj->fcj", silu_rows, modulation_weight[k], preferred_element_type=F32)
                + jnp.einsum(
                    "fr,rcj->fcj", rank_rows[:, k], modulation_up_factor[k], preferred_element_type=F32
                )
            )
        return jnp.stack(parts, axis=1)

    def modulation_shard(partial_mod):
        total_mod = partial_mod[0]
        for d in range(1, F):
            total_mod = total_mod + xf(partial_mod[d], d)
        return total_mod

    def modulation(mod_shard):
        mod_rel = gather_by(mod_shard, xz, t_bits)
        mod_abs = jnp.take(mod_rel, jnp.bitwise_xor(z, arange_t), axis=0)
        return jnp.moveaxis(mod_abs, 0, 2).reshape(2, 6, W)

    def both_modulations(mod_all):
        mine = jnp.concatenate([mod_all[0], jnp.broadcast_to(text.live, (1, W))], axis=0)
        both = jnp.where(native, mine, xr(mine, 1))
        image.live = both[6:7]
        return both[:6], mod_all[1]

    base_row = f * Rf + z * Rq

    def own_table_rows(ident, kinds):
        table = jnp.concatenate(kinds, axis=2)
        wanted = ident * RANK + jnp.arange(RANK, dtype=jnp.int32)
        held = base_row + jnp.arange(Rq, dtype=jnp.int32)
        if Rq == RANK:
            return jnp.where(ident * RANK == base_row, table, jnp.zeros_like(table))
        match = (wanted[:, None] == held[None, :]).astype(BF)
        return jnp.einsum("ir,srw->siw", match, table, preferred_element_type=F32).astype(BF)

    def own_columns(ident, kinds):
        start = ident * RANK - f * Rf
        inside = (start >= 0) & (start <= Rf - RANK)
        first = jnp.clip(start, 0, Rf - RANK)
        taken = jnp.concatenate(
            [lax.dynamic_slice_in_dim(k, first, RANK, axis=1) for k in kinds], axis=2
        )
        return jnp.where(inside, taken, jnp.zeros_like(taken))

    def fetch_adapters(tables, columns, after):
        tables, columns = due((tables, columns), after)
        both = [
            jnp.concatenate([own_table_rows(ids_f[d], tables), own_columns(ids_f[d], columns)], axis=2)
            for d in range(F)
        ]
        rows = both[0]
        for d in range(1, F):
            rows = rows + queue(LY, xf, both[d], d)
        yield rows
        cut = len(tables) * W
        table_rows, column_rows = rows[:, :, :cut], rows[:, :, cut:]
        for bit in t_bits:
            if bit < H:
                table_rows = table_rows + xz(table_rows, bit)
            else:
                table_rows = table_rows + queue(LZ, xz, table_rows, bit)
        rows_img = jnp.where(native, table_rows[0], xr(table_rows[0], 1))
        cols_img = jnp.where(native, column_rows[0], queue(LZ, swap, column_rows[0]))

        def pieces(array, widths):
            result, at = [], 0
            for n in widths:
                result.append(array[:, at : at + n])
                at += n
            return result

        table_widths = [t.shape[2] for t in tables]
        column_widths = [c.shape[2] for c in columns]
        yield (
            pieces(rows_img, table_widths) + pieces(cols_img, column_widths),
            pieces(table_rows[1], table_widths) + pieces(column_rows[1], column_widths),
        )

    image, text = Stream(), Stream()
    text.live = live.astype(F32)[0]
    qkv_planes = lax.optimization_barrier(jnp.moveaxis(query_key_value_weight, 2, 1))
    sub, ffh, wh = rows_d // 2, ffq // 2, wq // 2
    xb, cb = lax.rem(xi, 2), core
    entries = [native.astype(jnp.int32)]

    def slot(value):
        entries.append(value)
        return Slot(len(entries) - 1)

    def fetch_first(after):
        return fetch_adapters(
            [adapter_down_table[1], adapter_up_table[0], adapter_down_table[2], adapter_up_table[1]],
            [query_key_value_up.reshape(2, Rf, 3 * wq), output_down_factor, first_feed_up, second_feed_down],
            after,
        )

    def norm_first():
        for s, mod, tokens in ((image, mods[0], img), (text, mods[1], text_tokens)):
            s.xf = tokens.astype(F32)
            s.hat1, s.inv1 = norm_rows(s.xf)
            s.normed = (s.hat1 * (1.0 + mod[1:2]) + mod[0:1]).astype(BF)

    if F == 2 and X == 2 and rows_d % 128 == 0 and wh % 16 == 0 and sub % 16 == 0:
        own, other = slot(f * rows_d), slot((1 - f) * rows_d)
        own_x, own_y = slot(f * rows_d + xb * sub), slot(f * rows_d + (1 - xb) * sub)
        other_x, other_y = slot((1 - f) * rows_d + xb * sub), slot((1 - f) * rows_d + (1 - xb) * sub)
        other_c, other_d = slot((1 - f) * rows_d + cb * sub), slot((1 - f) * rows_d + (1 - cb) * sub)
        half_x, half_y = slot(xb * ffh), slot((1 - xb) * ffh)
        half_c, half_d = slot(cb * ffh), slot((1 - cb) * ffh)
        att_c, att_d = slot(cb * wh), slot((1 - cb) * wh)

        def piece(weight, k, which, rows):
            start = (k,) + (0,) * (weight.ndim - 3) + (which * rows, 0)
            return lax.dynamic_slice(weight, start, (1,) + weight.shape[1:-2] + (rows, weight.shape[-1]))[0]

        def planes(weight, plan, k):
            if weight.ndim == 3:
                return plan
            n = weight.shape[-1]
            return [
                (p[0], c if p[1] is None else (k, c)) + p[2:5] + (c * n,) + p[6:]
                for p in plan
                for c in range(weight.shape[1])
            ]

        def width(weight):
            return weight.shape[-1] * (1 if weight.ndim == 3 else weight.shape[1])

        def image_pieces(weight, rows):
            mine = piece(weight, 0, xb, rows)
            a0 = queue(LZ, swap, mine)
            after = yield a0
            if after is not None:
                a0 = due(a0, after)
            a1 = queue(LX, swap_across, a0)
            b0 = queue(LY, xf, jnp.where(native, mine, a0), 1)
            after = yield a1, b0
            if after is not None:
                b0 = due(b0, after)
            yield [weight, a0, a1, b0, queue(LX, xr, b0, 2)]

        def image_in(weight, sources):
            n = weight.shape[-1]
            plan = [
                (0, 0, rows_d, n, own, 0, 1),
                (1, None, sub, n, own_x, 0, 0),
                (2, None, sub, n, own_y, 0, 0),
                (3, None, sub, n, other_x, 0, None),
                (4, None, sub, n, other_y, 0, None),
            ]
            return Matrix((W, width(weight)), sources, planes(weight, plan, 0))

        def image_out(sources):
            plan = [
                (0, 0, ffq, rows_d, 0, own, 1),
                (1, None, ffh, rows_d, half_x, own, 0),
                (2, None, ffh, rows_d, half_y, own, 0),
                (3, None, ffh, rows_d, half_x, other, None),
                (4, None, ffh, rows_d, half_y, other, None),
            ]
            return Matrix((ffq, W), sources, plan)

        def text_piece(weight, rows):
            b0 = queue(LY, xf, piece(weight, 1, cb, rows), 1)
            return [weight, b0, xr(b0, 1)]

        def text_in(weight):
            n = weight.shape[-1]
            plan = [
                (0, 1, rows_d, n, own, 0, None),
                (1, None, sub, n, other_c, 0, None),
                (2, None, sub, n, other_d, 0, None),
            ]
            return Matrix((W, width(weight)), text_piece(weight, sub), planes(weight, plan, 1))

        def text_out(weight, rows, slot_c, slot_d):
            plan = [
                (0, 1, 2 * rows, rows_d, 0, own, None),
                (1, None, rows, rows_d, slot_c, other, None),
                (2, None, rows, rows_d, slot_d, other, None),
            ]
            return Matrix((2 * rows, W), text_piece(weight, rows), plan)

        get_qkv = image_pieces(qkv_planes, sub)
        a0_qkv = next(get_qkv)
        text.w_qkv = text_in(due(qkv_planes, info_f))
        ranks = due(condition_ranks(silu_f), a0_qkv)
        img_swap = queue(LZ, swap, due(image_input[0], ranks))
        img = jnp.where(native, image_input[0], img_swap)
        shard = modulation_shard(due(partial_modulation(ranks), text.w_qkv.sources[1]))
        text_tokens, text.cot = gather_texts(due((text_input[0], text_cotangent[0]), shard))
        get_first = fetch_first(shard)
        next(get_first)
        a1_qkv, b0_qkv = get_qkv.send(shard)
        mods = both_modulations(due(modulation(shard), img_swap))
        norm_first()
        first_img, first_txt = next(get_first)
        image.w_qkv = image_in(qkv_planes, next(get_qkv))
        image.n1 = gather_group(image.normed)
        image.n1[1] = due(image.n1[1], a1_qkv, b0_qkv)
        rest = (output_weight, first_feed_weight, second_feed_weight, image_cotangent)
        _, rest = lax.optimization_barrier((image.normed, rest))
        text.w_out = Matrix(
            (wq, W),
            [output_weight, queue(LY, xf, rest[0][1], 1)],
            [(0, 1, wq, rows_d, 0, own, None), (1, None, wq, rows_d, 0, other, None)],
        )
        text.w_fc1 = text_in(rest[1])
        text.w_fc2 = text_out(rest[2], ffh, half_c, half_d)
        rest = due(rest, image.n1[1])
        output_weight, first_feed_weight, second_feed_weight, image_cotangent = rest
        flight = Stream()

        def bulk(stage, value):
            if stage == 0:
                flight.out = output_weight[0]
                flight.a_out = queue(LZ, swap, flight.out)
                flight.get_fc1 = image_pieces(first_feed_weight, sub)
                flight.a0_fc1 = next(flight.get_fc1)
            elif stage == 1:
                flight.a_out, flight.a0_fc1 = due((flight.a_out, flight.a0_fc1), value)
                b_out = queue(LY, xf, jnp.where(native, flight.out, flight.a_out), 1)
                image.w_out = Matrix(
                    (wq, W),
                    [output_weight, flight.a_out, b_out],
                    [
                        (0, 0, wq, rows_d, 0, own, 1),
                        (1, None, wq, rows_d, 0, own, 0),
                        (2, None, wq, rows_d, 0, other, None),
                    ],
                )
                flight.part_fc1 = flight.get_fc1.send(value)
                flight.get_fc2 = image_pieces(due(second_feed_weight, value), ffh)
                flight.a0_fc2 = next(flight.get_fc2)
                return [flight.a_out]
            elif stage == 2:
                image.w_fc1 = image_in(first_feed_weight, flight.get_fc1.send(value))
                return [flight.part_fc1[0]]
            elif stage == 3:
                flight.part_fc2 = flight.get_fc2.send(value)
                return [flight.part_fc1[1], flight.a0_fc2]
            else:
                image.w_fc2 = image_out(flight.get_fc2.send(value))
                image.cot = jnp.where(
                    native, image_cotangent[0], queue(LZ, swap, due(image_cotangent[0], value))
                )
                return list(flight.part_fc2) + [image.w_fc1.sources[4]]
            return []

    else:

        def bulk(stage, value):
            return []

        def place(shape, pieces, axis):
            full = jnp.zeros(shape, BF)
            for piece, offset in pieces:
                full = lax.dynamic_update_slice_in_dim(full, piece, offset, axis=axis)
            return full

        def fetch_image(weight, axis):
            rows, cols = weight.shape
            part = rows // X
            mine = lax.dynamic_slice_in_dim(weight, xi * part, part, axis=0)
            moved = gather_by(exchange(mine), xr, x_bits)
            held = place((rows, cols), [(moved[e], (xi ^ e) * part) for e in range(X)], 0)
            held = jnp.where(native, weight, held)
            full_shape = (rows * F, cols) if axis == 0 else (rows, cols * F)
            size = weight.shape[axis]
            full = place(full_shape, [(held, f * size)], axis)
            for d in range(1, F):
                full = lax.dynamic_update_slice_in_dim(full, xf(held, d), (f ^ d) * size, axis=axis)
            return full

        def fetch_text(weight, axis):
            rows, cols = weight.shape
            part = rows // R
            mine = lax.dynamic_slice_in_dim(weight, r * part, part, axis=0)
            full_shape = (rows * F, cols) if axis == 0 else (rows, cols * F)
            size = weight.shape[axis]
            full = place(full_shape, [(weight, f * size)], axis)
            for d in range(1, F):
                pieces = gather_by(xf(mine, d), xr, x_bits + [1])
                order = [0]
                for bit in x_bits + [1]:
                    order = order + [o ^ bit for o in order]
                for e in range(R):
                    start = [0, 0]
                    start[axis] = (f ^ d) * size
                    start[0] = start[0] + (r ^ order[e]) * part
                    full = lax.dynamic_update_slice(full, pieces[e], start)
            return full

        def whole(full):
            rows, cols = full.shape
            return Matrix(full.shape, [full], [(0, None, rows, cols, 0, 0, None)])

        qkv_native = query_key_value_weight.reshape(2, rows_d, 3 * wq)
        img = exchange(image_input[0])
        image.cot = exchange(image_cotangent[0])
        shard = modulation_shard(partial_modulation(condition_ranks(silu_f)))
        text_tokens, text.cot = gather_texts((text_input[0], text_cotangent[0]))
        mods = both_modulations(modulation(shard))
        _, (first_img, first_txt) = fetch_first(shard)
        norm_first()
        image.n1 = gather_group(image.normed)
        for s, k, fetch in ((image, 0, fetch_image), (text, 1, fetch_text)):
            s.w_qkv = whole(fetch(qkv_native[k], 0))
            s.w_out = whole(fetch(output_weight[k], 1))
            s.w_fc1 = whole(fetch(first_feed_weight[k], 0))
            s.w_fc2 = whole(fetch(second_feed_weight[k], 1))
    offs = jnp.stack(entries).astype(jnp.int32)
    streams = (image, text)
    for s, mod, tokens, first in (
        (image, mods[0], img, first_img),
        (text, mods[1], text_tokens, first_txt),
    ):
        s.mod, s.x = mod, tokens
        s.a_qkv, s.b_out, s.a_fc1, s.b_fc2, s.b_qkv, s.a_out, s.b_fc1, s.a_fc2 = first

    near = [0, H]
    far = [i for i in range(T) if i not in near]
    flow = near + far
    image.size, text.size = image.x.shape[0], text.x.shape[0]
    image.once, image.twice = [flow], [near, far]
    text.once = text.twice = [[0]]
    img_len = T * image.size

    def scatter_image(blocks, parts):
        placed = [None] * T
        for i, v in zip([i for part in parts for i in part], blocks):
            placed[i] = v
        return fold_chips(fold_cores(placed))

    def windows(s, array, parts):
        result, row = [], 0
        for part in parts:
            rows = len(part) * s.size
            result.append((array, row, rows))
            row += rows
        return result

    def own_part(s, v):
        return own_rows_of(v) if s is text else v

    def total(results):
        value = results[0]
        for more in results[1:]:
            value = value + more
        return value

    def blocks_out(s, part):
        return [((s.size, W), BF)] * len(part)

    def qkv_forward(s):
        s.joint, s.rank_qkv = [], []
        for part in s.twice:
            rows = len(part) * s.size
            (out,), (rank,) = project(
                qkv_forward_kernel, offs, [s.w_qkv],
                [[s.n1[i] for i in part], [s.a_qkv], [s.b_qkv]],
                [[((rows, 3 * wq), BF)], [((rows, RANK), BF)]], 0,
            )
            s.joint.append(out)
            s.rank_qkv.append(rank)

    def out_forward(s):
        rows = len(s.once[0]) * s.size
        partial, (s.rank_out,) = project(
            out_forward_kernel, offs, [s.w_out], [windows(s, s.att, s.once), [s.a_out], [s.b_out]],
            [blocks_out(s, s.once[0]), [((rows, RANK), BF)]], 0,
        )
        return partial

    def second_norm(s, branch):
        mod = s.mod
        s.br_attn = branch
        s.after = s.xf + mod[2:3] * branch
        s.hat2, s.inv2 = norm_rows(s.after)
        return (s.hat2 * (1.0 + mod[4:5]) + mod[3:4]).astype(BF)

    def mlp_forward(s):
        s.saved, partial = [], []
        for part in s.once:
            rows = len(part) * s.size
            out, *saved = project(
                mlp_forward_kernel, offs, [s.w_fc1, s.w_fc2],
                [[s.a_fc1], [s.b_fc1], [s.a_fc2], [s.b_fc2]],
                [
                    blocks_out(s, part), [((rows, ffq), BF)], [((rows, ffq), BF)],
                    [((rows, RANK), BF)], [((rows, RANK), BF)],
                ],
                0, [[s.n2[i] for i in part]], (rows, W),
            )
            partial += out
            s.saved.append([v[0] for v in saved])
        return partial

    def mlp_backward(s):
        partial, sums = [], []
        for part, (act, slope, rank1, rank2) in zip(s.once, s.saved):
            out, *more = project(
                mlp_backward_kernel, offs, [s.w_fc1, s.w_fc2],
                [
                    [act], [slope], [rank1], [rank2],
                    [s.a_fc1], [s.b_fc1], [s.a_fc2], [s.b_fc2],
                ],
                [blocks_out(s, part)] + [[((RANK, n), F32)] for n in (ffq, ffq, W, W)],
                1, [[s.gb_mlp[i] for i in part], [s.n2[i] for i in part]], (len(part) * s.size, ffq),
            )
            partial += out
            sums.append([m[0] for m in more])
        s.t_b_fc1, s.t_a_fc2, s.t_back1, s.t_in2 = [total(t) for t in zip(*sums)]
        return partial

    def second_norm_back(s, gn2):
        mod = s.mod
        s.gs_mlp = jnp.sum(own_part(s, gn2), axis=0)
        s.gc_mlp = jnp.sum(own_part(s, gn2 * s.hat2), axis=0)
        s.g_after = s.g2 + norm_back(gn2 * (1.0 + mod[4:5]), s.hat2, s.inv2)
        s.gg_attn = jnp.sum(own_part(s, s.g_after * s.br_attn), axis=0)
        return (mod[2:3] * s.g_after).astype(BF)

    def out_backward(s, gb):
        s.g_att, sums = [], []
        atts, ranks = windows(s, s.att, s.twice), windows(s, s.rank_out, s.twice)
        for part, att, rank in zip(s.twice, atts, ranks):
            rows = len(part) * s.size
            (out,), *more = project(
                out_backward_kernel, offs, [s.w_out],
                [[gb[i] for i in part], [att], [rank], [s.a_out], [s.b_out]],
                [[((rows, wq), BF)], [((RANK, W), F32)], [((RANK, wq), F32)]], 0,
            )
            s.g_att.append(out)
            sums.append([m[0] for m in more])
        s.t_back0, s.t_a_out = [total(t) for t in zip(*sums)]

    def qkv_backward(s):
        partial, (s.t_b_qkv,), (s.t_in1,) = project(
            qkv_backward_kernel, offs, [s.w_qkv],
            [windows(s, s.g_joint, s.once), [s.n1[i] for i in s.once[0]], s.rank_qkv, [s.a_qkv], [s.b_qkv]],
            [blocks_out(s, s.once[0]), [((RANK, 3 * wq), F32)], [((RANK, W), F32)]], 0,
        )
        return partial

    text.n1 = [due(text.normed, image.normed)]
    bulk(0, image.n1[1])
    qkv_forward(image)
    text.n1[0] = due(text.n1[0], image.joint[0])
    qkv_forward(text)
    arrived = bulk(1, image.joint[0])
    joints = [(j, None) for j in image.joint] + [(text.joint[0], 1), (swap(text.joint[0]), 0)]
    joints[0] = (due(joints[0][0], *arrived), None)
    attended, lse = attend_forward(offs, joints)
    attended = due(attended, *bulk(2, attended))
    image.att = attended
    img_partial = out_forward(image)
    arrived = bulk(3, img_partial[0])
    text.att = exchange(attended[img_len:])
    txt_partial = out_forward(text)
    branch, sent = scatter_image(img_partial, image.once)
    branch = due(branch, *arrived)
    txt_branch = sum_text(txt_partial[0]).astype(F32)
    normed = second_norm(image, branch)
    image.n2 = gather_group(normed)
    arrived = bulk(4, normed)
    late = image.w_fc2.sources[-1]
    image.g2 = image.cot.astype(F32) * image.live
    image.gb_mlp = gather_group(due((image.mod[5:6] * image.g2).astype(BF), image.n2[1]))
    text.n2 = [second_norm(text, txt_branch)]
    text.g2 = text.cot.astype(F32) * text.live
    text.gb_mlp = [(text.mod[5:6] * text.g2).astype(BF)]
    txt_done = mlp_forward(text)
    txt_partial = mlp_backward(text)
    txt_gn2 = sum_text(txt_partial[0]).astype(F32)
    image.n2[0] = due(image.n2[0], txt_partial)
    image.n2[1] = due(image.n2[1], *arrived)

    info_f = due(info_f, normed, late)
    info_all = gather_by(info_f, xr, [1] + x_bits)
    ids_all = info_all[:, :, W].astype(jnp.int32)
    silu_all = info_all[:, :, :W].astype(BF)
    rank_all = condition_ranks(silu_all.reshape(R * F, W))

    img_done = mlp_forward(image)
    out_backward(text, [second_norm_back(text, txt_gn2)])
    txt_grad = swap(text.g_att[0])
    image.gb_mlp[0] = due(image.gb_mlp[0], txt_grad)
    img_partial = mlp_backward(image)
    gn2, sent = scatter_image(img_partial, image.once)

    gb = second_norm_back(image, gn2)
    gb_img = gather_group(gb)
    out_backward(image, gb_img)
    img_done, txt_done = due((img_done, txt_done), gb_img[0])
    image.br_mlp, _ = scatter_image(img_done, image.once)
    text.br_mlp = lax.psum_scatter(txt_done[0], "tp", scatter_dimension=0, tiled=True).astype(F32)
    for s in streams:
        s.out = ((own_part(s, s.after) + s.mod[5:6] * s.br_mlp) * s.live).astype(BF)
        s.gg_mlp = jnp.sum(own_part(s, s.g2) * s.br_mlp, axis=0)

    def combine_input(img_cols, txt_cols, rows):
        kinds = rows[0].shape[0] // RANK
        img_cols = exchange(jnp.concatenate(img_cols, axis=1).astype(BF))
        return jnp.concatenate(
            [img_cols] + [c.astype(BF) for c in txt_cols]
            + [r[i * RANK : (i + 1) * RANK] for r in rows for i in range(kinds)],
            axis=1,
        )

    def gather_all(pieces):
        return gather_by(gather_by(pieces, xf, f_bits), xr, [1] + x_bits)

    def combine(blocks, idents):
        flat = blocks.reshape(R * F * RANK, blocks.shape[-1])
        slots = (idents.reshape(R * F, 1) * RANK + jnp.arange(RANK, dtype=jnp.int32)).reshape(1, -1)
        place_rows = (row_ids[:, None] == slots).astype(BF)
        return mm(place_rows, flat)

    def reduce_rows(img_rows, txt_rows):
        return exchange(scatter_columns(img_rows, img_steps)), scatter_columns(txt_rows, txt_steps)

    def rows_home(rows):
        kinds = rows.shape[1]
        blocks = rows.astype(BF).reshape(T, Rq, kinds, wq)
        blocks = jnp.take(blocks, jnp.bitwise_xor(z, arange_t), axis=0)
        got = jnp.stack([blocks[0]] + [xz(blocks[d], d) for d in range(1, T)])
        got = jnp.take(got, jnp.bitwise_xor(z, arange_t), axis=0)
        return jnp.moveaxis(got, 0, 2).reshape(Rq, kinds, W).astype(F32)

    ids_in_order = jnp.take(
        jnp.take(ids_all, jnp.bitwise_xor(r, jnp.arange(R, dtype=jnp.int32)), axis=0),
        jnp.bitwise_xor(f, jnp.arange(F, dtype=jnp.int32)),
        axis=1,
    )
    early_blocks = lax.all_gather(
        combine_input(
            [image.t_b_fc1, image.t_a_fc2, image.t_a_out],
            [text.t_b_fc1, text.t_a_fc2, text.t_a_out],
            reduce_rows(
                *[jnp.concatenate([s.t_back1, s.t_in2, s.t_back0], axis=0).astype(BF) for s in streams]
            ),
        ),
        ("rep", "fsdp"),
    )

    grads = [(g, None) for g in image.g_att] + [(text.g_att[0], 1), (txt_grad, 0)]
    g_joint = attend_backward(offs, joints, grads, lse)
    g_joint = due(g_joint, image.br_mlp)
    out_swap = swap(image.out)
    image.g_joint = g_joint
    text.g_joint = exchange(g_joint[img_len:])
    img_partial = qkv_backward(image)
    keep = fold_cores([img_partial[flow.index(i)] for i in range(T)])
    gn1_img, sent = fold_chips(keep)
    text.g_joint = due(text.g_joint, sent)
    txt_partial = qkv_backward(text)
    late_in = combine_input(
        [image.t_b_qkv], [text.t_b_qkv], reduce_rows(image.t_in1.astype(BF), text.t_in1.astype(BF))
    )
    late_blocks = gather_all(late_in)
    gn1_img = due(gn1_img, out_swap)
    for s, gn1 in ((image, gn1_img), (text, scatter_rows(txt_partial[0]))):
        hat1, inv1, g_after = [own_part(s, v) for v in (s.hat1, s.inv1, s.g_after)]
        s.gs_attn = jnp.sum(gn1, axis=0)
        s.gc_attn = jnp.sum(gn1 * hat1, axis=0)
        dx = g_after + norm_back(gn1 * (1.0 + s.mod[1:2]), hat1, inv1)
        s.dx = dx.astype(BF)
    gm = jnp.stack(
        reduce_rows(
            *[
                jnp.stack([s.gs_attn, s.gc_attn, s.gg_attn, s.gs_mlp, s.gc_mlp, s.gg_mlp])
                for s in streams
            ]
        )
    ).astype(BF)
    gm_f = gather_by(gm, xf, f_bits)
    gm_all = gather_by(gm_f, xr, [1] + x_bits)
    early, late = combine(early_blocks, ids_in_order), combine(late_blocks, ids_all)
    span = 2 * ffq + wq
    grad_b_fc1 = jnp.stack([early[:, 0:ffq], early[:, span : span + ffq]])
    grad_a_fc2 = jnp.stack([early[:, ffq : 2 * ffq], early[:, span + ffq : span + 2 * ffq]])
    grad_a_out = jnp.stack([early[:, 2 * ffq : span], early[:, span + 2 * ffq : 2 * span]])
    grad_b_qkv = jnp.stack([late[:, : 3 * wq], late[:, 3 * wq : 6 * wq]]).reshape(2, Rf, 3, wq)
    home = rows_home(
        jnp.concatenate([early[:, 2 * span :], late[:, 6 * wq : 8 * wq]], axis=1).reshape(Rf, 8, wq)
    )

    seqs = R * F
    match = (row_adapter[None, :] == ids_all.reshape(seqs)[:, None]).astype(F32)
    gm_seq = gm_all.reshape(seqs, 2, 6, wq)
    rank_seq = (rank_all * match[:, None, :]).astype(BF)
    grad_b_ada, gcr = [], []
    for k in range(2):
        grad_b_ada.append(
            jnp.einsum("sr,scj->rcj", rank_seq[:, k], gm_seq[:, k], preferred_element_type=F32)
        )
        gcr.append(
            jnp.einsum(
                "scj,rcj->sr", gm_seq[:, k], modulation_up_factor[k], preferred_element_type=F32
            )
            * match
        )
    grad_b_ada = jnp.stack(grad_b_ada)
    gcr = jnp.stack(gcr, axis=1)
    gcr_rel = jnp.take(
        jnp.moveaxis(gcr.reshape(seqs, 2, T, Rq), 2, 0), jnp.bitwise_xor(z, arange_t), axis=0
    )
    gcr_own = gcr_rel[0]
    for d in range(1, T):
        gcr_own = gcr_own + xz(gcr_rel[d], d)
    grad_in0 = jnp.einsum(
        "ski,sd->kid",
        gcr_own,
        silu_all.reshape(seqs, W).astype(F32),
        precision=lax.Precision.HIGHEST,
    )
    gm_pair = gm_f
    dpart = jnp.zeros((F, rows_d), F32)
    for k in range(2):
        dpart = dpart + jnp.einsum(
            "fcj,dcj->fd", gm_pair[:, k], modulation_weight[k], preferred_element_type=F32
        )
    dfull = lax.dynamic_update_slice_in_dim(jnp.zeros((F, W), F32), dpart, f * rows_d, axis=1)
    dfull = dfull + jnp.einsum(
        "fki,kid->fd",
        gcr_own.reshape(R, F, 2, Rq)[0],
        adapter_down_table[0].astype(F32),
        precision=lax.Precision.HIGHEST,
    )
    dsum = dfull[0]
    for d in range(1, F):
        dsum = dsum + xf(dfull[d], d)
    for bit in t_bits:
        dsum = dsum + xz(dsum, bit)
    sigmoid = jax.nn.sigmoid(cond)
    dcond = dsum[None] * sigmoid * (1.0 + cond * (1.0 - sigmoid))

    grad_in = jnp.stack(
        [
            grad_in0,
            jnp.stack([home[:, 6], home[:, 7]]),
            jnp.stack([home[:, 1], home[:, 4]]),
        ]
    )
    grad_back = jnp.stack(
        [jnp.stack([home[:, 2], home[:, 5]]), jnp.stack([home[:, 0], home[:, 3]])]
    )
    return (
        jnp.where(native, image.out, out_swap)[None],
        text.out[None],
        exchange(image.dx)[None],
        text.dx[None],
        dcond,
        grad_in,
        grad_back,
        grad_b_ada,
        grad_b_qkv,
        grad_b_fc1,
        grad_a_out,
        grad_a_fc2,
    )


def solution(mesh):
    tokens = P(("rep", "fsdp"), "tp", None)
    table = P(None, None, ("fsdp", "tp"), None)
    columns4 = P(None, "fsdp", None, "tp")
    columns3 = P(None, "fsdp", "tp")
    rows3 = P(None, "tp", "fsdp")
    slot = P(("rep", "fsdp"))
    in_specs = (
        tokens, tokens, P(("rep", "fsdp"), None), tokens, tokens, slot, slot,
        columns4, columns4, rows3, columns3, rows3, table, table,
        columns4, columns4, columns3, columns3, columns3,
    )
    out_specs = (
        tokens, tokens, tokens, tokens, P(("rep", "fsdp"), None),
        table, table, columns4, columns4, columns3, columns3, columns3,
    )
    sizes = (mesh.shape["rep"], mesh.shape["fsdp"], mesh.shape["tp"])
    return jax.shard_map(
        functools.partial(body, sizes), mesh=mesh, in_specs=in_specs, out_specs=out_specs, check_vma=False
    )
```

```python
import functools

import jax
import jax.numpy as jnp
from jax import lax
from jax.experimental import pallas as pl
from jax.experimental.pallas import tpu as pltpu
from jax.sharding import PartitionSpec as P

HD = 64
RANK = 16
EPSILON = 1e-06
BF = jnp.bfloat16
F32 = jnp.float32
CORES = 2


def dot(left, right, dims):
    return lax.dot_general(left, right, (dims, ((), ())), preferred_element_type=F32)


def mm(left, right):
    return dot(left, right, ((left.ndim - 1,), (0,)))


def mm_t(left, right):
    return dot(left, right, ((left.ndim - 1,), (right.ndim - 1,)))


def t_mm(left, right):
    return dot(left, right, ((0,), (0,)))


def norm_rows(values):
    centred = values - jnp.mean(values, axis=-1, keepdims=True)
    inverse = lax.rsqrt(jnp.mean(centred * centred, axis=-1, keepdims=True) + EPSILON)
    return centred * inverse, inverse


def norm_back(grad_hat, hat, inverse):
    first = jnp.mean(grad_hat, axis=-1, keepdims=True)
    second = jnp.mean(grad_hat * hat, axis=-1, keepdims=True)
    return inverse * (grad_hat - first - hat * second)


def gelu_tanh(values):
    return jax.nn.gelu(values, approximate=True)


class Slot(int):
    pass


def spot(offs, where, step):
    if isinstance(where, Slot):
        return pl.multiple_of(offs[int(where)], step)
    return where


def copies(offs, plan, sources, targets, sems):
    def make(i):
        source, lead, rows, cols, target, row, col, _ = plan[i]
        ref = sources[source] if lead is None else sources[source].at[lead]
        dst = targets[target].at[pl.ds(spot(offs, row, 16), rows), pl.ds(spot(offs, col, 128), cols)]
        return pltpu.make_async_copy(ref, dst, sems.at[i])

    def each(action, chosen):
        for i in range(len(plan)):
            if chosen is not None and plan[i][4] not in chosen:
                continue
            case = plan[i][7]
            if case is None:
                action(make(i))
            else:

                @pl.when(offs[0] == case)
                def _(i=i):
                    action(make(i))

    return (
        lambda chosen=None: each(lambda c: c.start(), chosen),
        lambda chosen=None: each(lambda c: c.wait(), chosen),
    )


ANY = pl.BlockSpec(memory_space=pl.ANY)
SCALARS = pl.BlockSpec(memory_space=pltpu.SMEM)


def head_tiles(width):
    if width % 128 == 0:
        return [(p * 128, 128, 2) for p in range(width // 128)]
    return [(h * HD, HD, 1) for h in range(width // HD)]


def head_masks(rows, count):
    if count == 1:
        return [None]
    lane = lax.broadcasted_iota(jnp.int32, (rows, 128), 1)
    return [lane < HD, lane >= HD]


def pick(mask, values):
    return values if mask is None else jnp.where(mask, values, jnp.zeros_like(values))


def attend_forward_kernel(width, plan, offs, *refs):
    *sources, out_ref, lse_ref, kv_ref, sems = refs
    start_all, wait_all = copies(offs, plan, sources, [kv_ref], sems)
    step = pl.program_id(0)

    @pl.when(step == 0)
    def _():
        start_all()
        wait_all()

    rows = out_ref.shape[0]
    here = pl.ds(pl.multiple_of(step * rows, rows), rows)
    lses = []
    for start, size, count in head_tiles(width):
        queries = kv_ref[here, start : start + size] * jnp.asarray(HD ** (-0.5), BF)
        keys = kv_ref[:, width + start : width + start + size]
        values = kv_ref[:, 2 * width + start : 2 * width + start + size]
        total = None
        for mask in head_masks(rows, count):
            scores = mm_t(pick(mask, queries), keys)
            top = jnp.max(scores, axis=-1, keepdims=True)
            weights = jnp.exp(scores - top)
            norm = jnp.sum(weights, axis=-1, keepdims=True)
            part = mm(weights.astype(BF), values) * (1.0 / norm)
            part = pick(mask, part)
            total = part if total is None else total + part
            lses.append(top + jnp.log(norm))
        out_ref[:, start : start + size] = total.astype(BF)
    lse_ref[...] = jnp.concatenate(lses, axis=1)


def attend_backward_kernel(width, blocks, plan, offs, lse_ref, *refs):
    *sources, out_ref, kv_ref, grad_ref, dk_ref, dv_ref, sems = refs
    start_all, wait_all = copies(offs, plan, sources, [kv_ref, grad_ref], sems)
    step = pl.program_id(0)

    @pl.when(step == 0)
    def _():
        start_all()
        dk_ref[...] = jnp.zeros_like(dk_ref)
        dv_ref[...] = jnp.zeros_like(dv_ref)
        wait_all()

    rows = lse_ref.shape[0]
    here = pl.ds(pl.multiple_of(step * rows, rows), rows)
    head = 0
    for start, size, count in head_tiles(width):
        queries = kv_ref[here, start : start + size] * jnp.asarray(HD ** (-0.5), BF)
        keys = kv_ref[:, width + start : width + start + size]
        values = kv_ref[:, 2 * width + start : 2 * width + start + size]
        grads = grad_ref[here, start : start + size]
        grad_q = None
        for mask in head_masks(rows, count):
            queries_m = pick(mask, queries)
            grads_m = pick(mask, grads)
            scores = mm_t(queries_m, keys)
            probs = jnp.exp(scores - lse_ref[:, head : head + 1])
            grad_probs = mm_t(grads_m, values)
            product = probs * grad_probs
            inner = jnp.sum(product, axis=-1, keepdims=True)
            grad_scores = (product - probs * inner).astype(BF)
            part = pick(mask, mm(grad_scores, keys))
            grad_q = part if grad_q is None else grad_q + part
            dk_ref[:, start : start + size] += t_mm(grad_scores, queries_m)
            dv_ref[:, start : start + size] += t_mm(probs.astype(BF), grads_m)
            head += 1
        out_ref[here, start : start + size] = (grad_q * HD ** (-0.5)).astype(BF)

    @pl.when(step == blocks - 1)
    def _():
        out_ref[:, width : 2 * width] = dk_ref[...].astype(BF)
        out_ref[:, 2 * width :] = dv_ref[...].astype(BF)


def query_block(length):
    for rows in (512, 256, 128, 64, 32, 16):
        if length % rows == 0:
            return rows
    return length


def stack_plan(arrays, target, first):
    plan, row = [], 0
    for i, (array, case) in enumerate(arrays):
        plan.append((first + i, None, array.shape[0], array.shape[1], target, row, 0, case))
        if case != 1:
            row += array.shape[0]
    return plan, row


def attend_forward(offs, joints):
    plan, length = stack_plan(joints, 0, 0)
    width3 = joints[0][0].shape[1]
    width = width3 // 3
    heads = width // HD
    rows = query_block(length)
    return pl.pallas_call(
        functools.partial(attend_forward_kernel, width, plan),
        grid=(length // rows,),
        in_specs=[SCALARS] + [ANY] * len(joints),
        out_specs=[
            pl.BlockSpec((rows, width), lambda i: (i, 0)),
            pl.BlockSpec((rows, heads), lambda i: (i, 0)),
        ],
        out_shape=[
            jax.ShapeDtypeStruct((length, width), BF),
            jax.ShapeDtypeStruct((length, heads), F32),
        ],
        scratch_shapes=[pltpu.VMEM((length, width3), BF), pltpu.SemaphoreType.DMA((len(plan),))],
        compiler_params=pltpu.CompilerParams(vmem_limit_bytes=40 * 1024 * 1024),
        cost_estimate=pl.CostEstimate(
            flops= 64 * 2 * length * length * width,
            transcendentals=length * length * heads,
            bytes_accessed=length * width3 * 4,
        ),
        name="attend_forward",
    )(offs, *[a for a, _ in joints])


def attend_backward(offs, joints, grads, lse):
    plan, length = stack_plan(joints, 0, 0)
    more, _ = stack_plan(grads, 1, len(joints))
    plan = plan + more
    width3 = joints[0][0].shape[1]
    width = width3 // 3
    heads = width // HD
    rows = query_block(length)
    blocks = length // rows
    return pl.pallas_call(
        functools.partial(attend_backward_kernel, width, blocks, plan),
        grid=(blocks,),
        in_specs=[SCALARS, pl.BlockSpec((rows, heads), lambda i: (i, 0))] + [ANY] * len(plan),
        out_specs=pl.BlockSpec((length, width3), lambda i: (0, 0)),
        out_shape=jax.ShapeDtypeStruct((length, width3), BF),
        scratch_shapes=[
            pltpu.VMEM((length, width3), BF),
            pltpu.VMEM((length, width), BF),
            pltpu.VMEM((length, width), F32),
            pltpu.VMEM((length, width), F32),
            pltpu.SemaphoreType.DMA((len(plan),)),
        ],
        compiler_params=pltpu.CompilerParams(vmem_limit_bytes=48 * 1024 * 1024),
        cost_estimate=pl.CostEstimate(
            flops= 128 * 2 * length * length * width,
            transcendentals=length * length * heads,
            bytes_accessed=length * width3 * 8,
        ),
        name="attend_backward",
    )(offs, lse, *[a for a, _ in joints], *[a for a, _ in grads])


class Matrix:
    def __init__(self, shape, sources, plan):
        self.shape, self.sources, self.plan = shape, sources, plan


def join(refs):
    if len(refs) == 1:
        return refs[0][...]
    return jnp.concatenate([r[...] for r in refs], axis=0)


def split(value, refs):
    row = 0
    for ref in refs:
        ref[...] = value[row : row + ref.shape[0]].astype(ref.dtype)
        row += ref.shape[0]


def qkv_forward_kernel(ws, ins, outs, need):
    (x_refs, (a,), (b,)), ((out,), (rank_out,)) = ins, outs
    x = join(x_refs)
    rank = mm_t(x, a[...]).astype(BF)
    rank_out[...] = rank
    low = mm(rank, b[...])
    need(0)
    out[...] = (mm(x, ws[0][...]) + low).astype(BF)


def qkv_backward_kernel(ws, ins, outs, need):
    ((g,), x_refs, ranks, (a,), (b,)), (out, (t_b,), (t_a,)) = ins, outs
    grad = g[...]
    low = mm_t(grad, b[...]).astype(BF)
    t_b[...] = t_mm(join(ranks), grad)
    t_a[...] = t_mm(low, join(x_refs))
    need(0)
    split(mm_t(grad, ws[0][...]) + mm(low, a[...]), out)


def out_forward_kernel(ws, ins, outs, need):
    ((att,), (a,), (b,)), (out, (rank_out,)) = ins, outs
    act = att[...]
    rank = mm_t(act, a[...]).astype(BF)
    rank_out[...] = rank
    need(0)
    split(mm(act, ws[0][...]) + mm(rank, b[...]), out)


def out_backward_kernel(ws, ins, outs, need):
    (g_refs, (att,), (rank,), (a,), (b,)), ((out,), (t_b,), (t_a,)) = ins, outs
    grad = join(g_refs)
    low = mm_t(grad, b[...]).astype(BF)
    t_b[...] = t_mm(rank[...], grad)
    t_a[...] = t_mm(low, att[...])
    need(0)
    out[...] = (mm_t(grad, ws[0][...]) + mm(low, a[...])).astype(BF)


def row_tile(rows):
    for tile in (448, 224, 128, 112, 64, 32, 16):
        if rows % tile == 0:
            return tile
    return rows


def column_tiles(cols):
    tile = 512 if cols % 512 == 0 else cols
    return [(c, tile) for c in range(0, cols, tile)]


def by_rows(rows, step):
    tile = row_tile(rows)

    def run(i, carry):
        step(pl.ds(pl.multiple_of(i * tile, 16), tile))
        return carry

    lax.fori_loop(0, rows // tile, run, 0)


def mlp_forward_kernel(ws, ins, outs, need, gathered):
    (a1,), (b1,), (a2,), (b2,) = ins
    out, (act_out,), (slope_out,), (rank1_out,), (rank2_out,), (spill,) = outs
    (xs,) = gathered
    need(len(ws))
    need(0)

    def first(here):
        x = xs[here, :]
        rank1 = mm_t(x, a1[...]).astype(BF)
        rank1_out[here, :] = rank1
        for c, tile in column_tiles(act_out.shape[1]):
            hidden = mm(x, ws[0][:, c : c + tile]) + mm(rank1, b1[:, c : c + tile])
            square = hidden * hidden
            bend = jnp.tanh(hidden * (0.7978845608028654 + 0.035677408136300125 * square))
            half = 0.5 + 0.5 * bend
            act_out[here, c : c + tile] = (hidden * half).astype(BF)
            slope = half + (half * (1.0 - bend)) * hidden * (
                0.7978845608028654 + 0.10703222440890037 * square
            )
            slope_out[here, c : c + tile] = slope.astype(BF)

    by_rows(xs.shape[0], first)
    need(1)

    def second(here):
        act = act_out[here, :]
        rank2 = mm_t(act, a2[...]).astype(BF)
        rank2_out[here, :] = rank2
        for c, tile in column_tiles(spill.shape[1]):
            spill[here, c : c + tile] = (mm(act, ws[1][:, c : c + tile]) + mm(rank2, b2[:, c : c + tile])).astype(BF)

    by_rows(xs.shape[0], second)
    split(spill, out)


def mlp_backward_kernel(ws, ins, outs, need, gathered):
    (act,), (slope,), (rank1,), (rank2,), (a1,), (b1,), (a2,), (b2,) = ins
    out, (t_b1,), (t_a2,), (t_b2,), (t_a1,), (spill,) = outs
    gs, xs = gathered
    need(len(ws))
    need(1)
    t_b1[...] = jnp.zeros_like(t_b1)
    t_a2[...] = jnp.zeros_like(t_a2)
    t_b2[...] = jnp.zeros_like(t_b2)
    t_a1[...] = jnp.zeros_like(t_a1)

    def first(here):
        grad = gs[here, :]
        low2 = mm_t(grad, b2[...]).astype(BF)
        t_b2[...] += t_mm(rank2[here, :], grad)
        t_a2[...] += t_mm(low2, act[here, :])
        for c, tile in column_tiles(spill.shape[1]):
            part = mm_t(grad, ws[1][c : c + tile, :]) + mm(low2, a2[:, c : c + tile])
            spill[here, c : c + tile] = (part * slope[here, c : c + tile].astype(F32)).astype(BF)

    by_rows(gs.shape[0], first)
    need(len(ws) + 1)
    need(0)

    def second(here):
        gh = spill[here, :]
        low1 = mm_t(gh, b1[...]).astype(BF)
        t_b1[...] += t_mm(rank1[here, :], gh)
        t_a1[...] += t_mm(low1, xs[here, :])
        for c, tile in column_tiles(gs.shape[1]):
            gs[here, c : c + tile] = (mm_t(gh, ws[0][c : c + tile, :]) + mm(low1, a1[:, c : c + tile])).astype(BF)

    by_rows(gs.shape[0], second)
    split(gs, out)


def project(kernel, offs, matrices, ins, outs, first, blocks=(), spill=None):
    arrays, specs, counts = [], [], []
    for group in ins:
        counts.append(len(group))
        for item in group:
            if isinstance(item, tuple):
                array, row, rows = item
                arrays.append(array)
                specs.append(pl.BlockSpec((rows, array.shape[1]), lambda i, at=row // rows: (at, 0)))
            else:
                arrays.append(item)
                specs.append(pl.BlockSpec(item.shape, lambda i: (0, 0)))
    sources, plan = [], []
    order = [first] + [m for m in range(len(matrices)) if m != first]
    for m in order:
        base = len(sources)
        sources += matrices[m].sources
        plan += [(base + p[0],) + p[1:4] + (m,) + p[4:] for p in matrices[m].plan]
    scratch = []
    for i, group in enumerate(blocks):
        rows, cols = sum(g.shape[0] for g in group), group[0].shape[1]
        more, row = [], 0
        for g in group:
            more.append((len(sources), None, g.shape[0], cols, len(matrices) + i, row, 0, None))
            sources.append(g)
            row += g.shape[0]
        plan = more + plan if i == 0 else plan + more
        scratch.append(pltpu.VMEM((rows, cols), BF))
    n_blocks = len(scratch)
    if spill is not None:
        scratch.append(pltpu.VMEM(spill, BF))
    shapes = [jax.ShapeDtypeStruct(*o) for group in outs for o in group]
    n_in, n_src, n_out, n_mat = len(arrays), len(sources), len(shapes), len(matrices)

    def groups(refs, sizes):
        result, i = [], 0
        for n in sizes:
            result.append(list(refs[i : i + n]))
            i += n
        return result

    def body(offs_ref, *refs):
        in_refs, refs = refs[:n_in], refs[n_in:]
        src_refs, refs = refs[:n_src], refs[n_src:]
        out_refs, refs = refs[:n_out], refs[n_out:]
        *targets, sems = refs
        w_refs, gathered = targets[:n_mat], targets[n_mat : n_mat + n_blocks]
        start, wait = copies(offs_ref, plan, src_refs, targets[: n_mat + n_blocks], sems)
        start()
        results = groups(out_refs, [len(g) for g in outs])
        if n_blocks:
            results.append(targets[n_mat + n_blocks :])
            kernel(w_refs, groups(in_refs, counts), results, lambda m: wait([m]), gathered)
        else:
            kernel(w_refs, groups(in_refs, counts), results, lambda m: wait([m]))

    flops = sum(16 * outs[0][0][0][0] * len(outs[0]) * m.shape[0] * m.shape[1] for m in matrices)
    moved = sum(2 * m.shape[0] * m.shape[1] for m in matrices) + sum(2 * s.size for s in shapes)
    results = pl.pallas_call(
        body,
        grid=(1,),
        in_specs=[SCALARS] + specs + [ANY] * n_src,
        out_specs=[pl.BlockSpec(s.shape, lambda i: (0, 0)) for s in shapes],
        out_shape=shapes,
        scratch_shapes=[pltpu.VMEM(m.shape, BF) for m in matrices] + scratch + [pltpu.SemaphoreType.DMA((len(plan),))],
        compiler_params=pltpu.CompilerParams(vmem_limit_bytes=56 * 1024 * 1024),
        cost_estimate=pl.CostEstimate(flops=flops, transcendentals=0, bytes_accessed=moved),
    )(offs, *arrays, *sources)
    return groups(results, [len(g) for g in outs])


class Stream:
    pass


def powers(size):
    bits, bit = [], 1
    while bit < size:
        bits.append(bit)
        bit *= 2
    return bits


def body(
    mesh_shape,
    image_input,
    text_input,
    cond,
    image_cotangent,
    text_cotangent,
    live,
    slot_adapter_index,
    modulation_weight,
    query_key_value_weight,
    output_weight,
    first_feed_weight,
    second_feed_weight,
    adapter_down_table,
    adapter_up_table,
    modulation_up_factor,
    query_key_value_up,
    first_feed_up,
    output_down_factor,
    second_feed_down,
):
    R, F, T = mesh_shape
    H = T // CORES
    X = R // CORES
    W = image_input.shape[-1]
    wq = W // T
    Rf = modulation_up_factor.shape[1]
    Rq = adapter_down_table.shape[2]
    ffq = first_feed_weight.shape[-1]
    r = lax.axis_index("rep")
    f = lax.axis_index("fsdp")
    z = lax.axis_index("tp")
    core = lax.rem(r, CORES)
    xi = lax.div(r, CORES)
    high = lax.div(z, H)
    native = core == high

    def xz(v, bit):
        return lax.ppermute(v, "tp", [(i, i ^ bit) for i in range(T)])

    def xf(v, bit):
        return lax.ppermute(v, "fsdp", [(i, i ^ bit) for i in range(F)])

    def xr(v, bit):
        return lax.ppermute(v, "rep", [(i, i ^ bit) for i in range(R)])

    swap_pairs, across_pairs = [], []
    for a in range(R):
        for b in range(T):
            if a % CORES != b // H:
                swap_pairs.append((a * T + b, (a ^ 1) * T + (b ^ H)))
                across_pairs.append((a * T + b, (a ^ 2) * T + b))

    def swap(v):
        return lax.ppermute(v, ("rep", "tp"), swap_pairs)

    def swap_across(v):
        return lax.ppermute(v, ("rep", "tp"), across_pairs)

    def exchange(v):
        return jnp.where(native, v, swap(v))

    lanes = {}

    def queue(lane, step, value, *more):
        if lane in lanes:
            _, value = lax.optimization_barrier((lanes[lane], value))
        lanes[lane] = step(value, *more)
        return lanes[lane]

    LX, LY, LZ = range(3)

    def due(value, *arrived):
        return lax.optimization_barrier((value, arrived))[0]

    def gather_by(v, step, bits):
        return gather_by_more(v[None], step, bits)

    def gather_by_more(blocks, step, bits):
        for bit in bits:
            blocks = jnp.concatenate([blocks, step(blocks, bit)], axis=0)
        return blocks

    x_bits = [b for b in powers(R) if b > 1]
    h_bits = powers(H)
    t_bits = powers(T)
    f_bits = powers(F)
    arange_t = jnp.arange(T, dtype=jnp.int32)

    def gather_group(v):
        blocks = [v]
        for bit in h_bits:
            blocks = blocks + [xz(b, bit) for b in blocks]
        return blocks + [xr(b, 1) for b in blocks]

    def fold_cores(blocks):
        return [blocks[i].astype(F32) + xr(blocks[H + i], 1).astype(F32) for i in range(H)]

    def fold_chips(keep):
        sent = None
        for bit in reversed(h_bits):
            out = [k.astype(BF) for k in keep[bit:]]
            sent = out if sent is None else sent
            keep = [keep[i] + xz(out[i], bit).astype(F32) for i in range(bit)]
        return keep[0], sent

    def gather_texts(pair):
        rows = pair[0].shape[0]
        blocks = gather_by(jnp.concatenate(pair, axis=0), xz, t_bits)
        blocks = jnp.take(blocks, jnp.bitwise_xor(z, arange_t), axis=0)
        return [blocks[:, i * rows : (i + 1) * rows].reshape(T * rows, W) for i in range(2)]

    def bit_of(index, bit):
        return lax.rem(lax.div(index, bit), 2)

    def sum_text(v):
        for bit in t_bits:
            v = v + xz(v, bit)
        return v

    def own_rows_of(v):
        rows = v.shape[0] // T
        return lax.dynamic_slice_in_dim(v, z * rows, rows, axis=0)

    def scatter_rows(v):
        for bit in reversed(t_bits):
            half = v.shape[0] // 2
            mine = bit_of(z, bit) == 0
            low, high_part = v[:half], v[half:]
            out = jnp.where(mine, high_part, low).astype(BF)
            v = jnp.where(mine, low, high_part).astype(F32) + xz(out, bit).astype(F32)
        return v

    def scatter_columns(rows, steps):
        for step, bit, mine in steps:
            half = rows.shape[1] // 2
            low, high_part = rows[:, :half], rows[:, half:]
            rows = jnp.where(mine == 0, low, high_part) + step(jnp.where(mine == 0, high_part, low), bit)
        return rows

    img_steps = [(xr, 1, core)] + [(xz, bit, bit_of(z, bit)) for bit in reversed(h_bits)]
    txt_steps = [(xz, bit, bit_of(z, bit)) for bit in reversed(t_bits)]

    silu = jax.nn.silu(cond).astype(BF)
    info = jnp.concatenate(
        [
            silu.astype(F32),
            jnp.broadcast_to(slot_adapter_index.astype(F32)[:, None], (1, 64)),
            jnp.broadcast_to(live.astype(F32)[:, None], (1, 64)),
        ],
        axis=1,
    )
    info_f = gather_by(info[0], xf, f_bits)
    silu_f = info_f[:, :W].astype(BF)
    ids_f = info_f[:, W].astype(jnp.int32)

    row_ids = f * Rf + jnp.arange(Rf, dtype=jnp.int32)
    row_adapter = lax.div(row_ids, RANK)
    rows_d = modulation_weight.shape[1]

    def condition_ranks(silu_rows):
        held = jnp.einsum("fd,kid->fki", silu_rows, adapter_down_table[0], preferred_element_type=F32)
        spread = jnp.take(gather_by(held, xz, t_bits), jnp.bitwise_xor(z, arange_t), axis=0)
        return jnp.moveaxis(spread, 0, 2).reshape(silu_rows.shape[0], 2, Rf)

    def partial_modulation(ranks):
        own_rows = (row_adapter[None] == ids_f[:, None])[:, None, :]
        rank_rows = jnp.where(own_rows, ranks, 0.0).astype(BF)
        silu_rows = lax.dynamic_slice_in_dim(silu_f, f * rows_d, rows_d, axis=1)
        parts = []
        for k in range(2):
            parts.append(
                jnp.einsum("fd,dcj->fcj", silu_rows, modulation_weight[k], preferred_element_type=F32)
                + jnp.einsum(
                    "fr,rcj->fcj", rank_rows[:, k], modulation_up_factor[k], preferred_element_type=F32
                )
            )
        return jnp.stack(parts, axis=1)

    def modulation_shard(partial_mod):
        total_mod = partial_mod[0]
        for d in range(1, F):
            total_mod = total_mod + xf(partial_mod[d], d)
        return total_mod

    def modulation(mod_shard):
        mod_rel = gather_by(mod_shard, xz, t_bits)
        mod_abs = jnp.take(mod_rel, jnp.bitwise_xor(z, arange_t), axis=0)
        return jnp.moveaxis(mod_abs, 0, 2).reshape(2, 6, W)

    def both_modulations(mod_all):
        mine = jnp.concatenate([mod_all[0], jnp.broadcast_to(text.live, (1, W))], axis=0)
        both = jnp.where(native, mine, xr(mine, 1))
        image.live = both[6:7]
        return both[:6], mod_all[1]

    base_row = f * Rf + z * Rq

    def own_table_rows(ident, kinds):
        table = jnp.concatenate(kinds, axis=2)
        wanted = ident * RANK + jnp.arange(RANK, dtype=jnp.int32)
        held = base_row + jnp.arange(Rq, dtype=jnp.int32)
        if Rq == RANK:
            return jnp.where(ident * RANK == base_row, table, jnp.zeros_like(table))
        match = (wanted[:, None] == held[None, :]).astype(BF)
        return jnp.einsum("ir,srw->siw", match, table, preferred_element_type=F32).astype(BF)

    def own_columns(ident, kinds):
        start = ident * RANK - f * Rf
        inside = (start >= 0) & (start <= Rf - RANK)
        first = jnp.clip(start, 0, Rf - RANK)
        taken = jnp.concatenate(
            [lax.dynamic_slice_in_dim(k, first, RANK, axis=1) for k in kinds], axis=2
        )
        return jnp.where(inside, taken, jnp.zeros_like(taken))

    def fetch_adapters(tables, columns, after):
        tables, columns = due((tables, columns), after)
        both = [
            jnp.concatenate([own_table_rows(ids_f[d], tables), own_columns(ids_f[d], columns)], axis=2)
            for d in range(F)
        ]
        rows = both[0]
        for d in range(1, F):
            rows = rows + queue(LY, xf, both[d], d)
        yield rows
        cut = len(tables) * W
        table_rows, column_rows = rows[:, :, :cut], rows[:, :, cut:]
        for bit in t_bits:
            if bit < H:
                table_rows = table_rows + xz(table_rows, bit)
            else:
                table_rows = table_rows + queue(LZ, xz, table_rows, bit)
        rows_img = jnp.where(native, table_rows[0], xr(table_rows[0], 1))
        cols_img = jnp.where(native, column_rows[0], queue(LZ, swap, column_rows[0]))

        def pieces(array, widths):
            result, at = [], 0
            for n in widths:
                result.append(array[:, at : at + n])
                at += n
            return result

        table_widths = [t.shape[2] for t in tables]
        column_widths = [c.shape[2] for c in columns]
        yield (
            pieces(rows_img, table_widths) + pieces(cols_img, column_widths),
            pieces(table_rows[1], table_widths) + pieces(column_rows[1], column_widths),
        )

    image, text = Stream(), Stream()
    text.live = live.astype(F32)[0]
    qkv_planes = lax.optimization_barrier(jnp.moveaxis(query_key_value_weight, 2, 1))
    sub, ffh, wh = rows_d // 2, ffq // 2, wq // 2
    xb, cb = lax.rem(xi, 2), core
    entries = [native.astype(jnp.int32)]

    def slot(value):
        entries.append(value)
        return Slot(len(entries) - 1)

    def fetch_first(after):
        return fetch_adapters(
            [adapter_down_table[1], adapter_up_table[0], adapter_down_table[2], adapter_up_table[1]],
            [query_key_value_up.reshape(2, Rf, 3 * wq), output_down_factor, first_feed_up, second_feed_down],
            after,
        )

    def norm_first():
        for s, mod, tokens in ((image, mods[0], img), (text, mods[1], text_tokens)):
            s.xf = tokens.astype(F32)
            s.hat1, s.inv1 = norm_rows(s.xf)
            s.normed = (s.hat1 * (1.0 + mod[1:2]) + mod[0:1]).astype(BF)

    if F == 2 and X == 2 and rows_d % 128 == 0 and wh % 16 == 0 and sub % 16 == 0:
        own, other = slot(f * rows_d), slot((1 - f) * rows_d)
        own_x, own_y = slot(f * rows_d + xb * sub), slot(f * rows_d + (1 - xb) * sub)
        other_x, other_y = slot((1 - f) * rows_d + xb * sub), slot((1 - f) * rows_d + (1 - xb) * sub)
        other_c, other_d = slot((1 - f) * rows_d + cb * sub), slot((1 - f) * rows_d + (1 - cb) * sub)
        half_x, half_y = slot(xb * ffh), slot((1 - xb) * ffh)
        half_c, half_d = slot(cb * ffh), slot((1 - cb) * ffh)
        att_c, att_d = slot(cb * wh), slot((1 - cb) * wh)

        def piece(weight, k, which, rows):
            start = (k,) + (0,) * (weight.ndim - 3) + (which * rows, 0)
            return lax.dynamic_slice(weight, start, (1,) + weight.shape[1:-2] + (rows, weight.shape[-1]))[0]

        def planes(weight, plan, k):
            if weight.ndim == 3:
                return plan
            n = weight.shape[-1]
            return [
                (p[0], c if p[1] is None else (k, c)) + p[2:5] + (c * n,) + p[6:]
                for p in plan
                for c in range(weight.shape[1])
            ]

        def width(weight):
            return weight.shape[-1] * (1 if weight.ndim == 3 else weight.shape[1])

        def image_pieces(weight, rows):
            mine = piece(weight, 0, xb, rows)
            a0 = queue(LZ, swap, mine)
            after = yield a0
            if after is not None:
                a0 = due(a0, after)
            a1 = queue(LX, swap_across, a0)
            b0 = queue(LY, xf, jnp.where(native, mine, a0), 1)
            after = yield a1, b0
            if after is not None:
                b0 = due(b0, after)
            yield [weight, a0, a1, b0, queue(LX, xr, b0, 2)]

        def image_in(weight, sources):
            n = weight.shape[-1]
            plan = [
                (0, 0, rows_d, n, own, 0, 1),
                (1, None, sub, n, own_x, 0, 0),
                (2, None, sub, n, own_y, 0, 0),
                (3, None, sub, n, other_x, 0, None),
                (4, None, sub, n, other_y, 0, None),
            ]
            return Matrix((W, width(weight)), sources, planes(weight, plan, 0))

        def image_out(sources):
            plan = [
                (0, 0, ffq, rows_d, 0, own, 1),
                (1, None, ffh, rows_d, half_x, own, 0),
                (2, None, ffh, rows_d, half_y, own, 0),
                (3, None, ffh, rows_d, half_x, other, None),
                (4, None, ffh, rows_d, half_y, other, None),
            ]
            return Matrix((ffq, W), sources, plan)

        def text_piece(weight, rows):
            b0 = queue(LY, xf, piece(weight, 1, cb, rows), 1)
            return [weight, b0, xr(b0, 1)]

        def text_in(weight):
            n = weight.shape[-1]
            plan = [
                (0, 1, rows_d, n, own, 0, None),
                (1, None, sub, n, other_c, 0, None),
                (2, None, sub, n, other_d, 0, None),
            ]
            return Matrix((W, width(weight)), text_piece(weight, sub), planes(weight, plan, 1))

        def text_out(weight, rows, slot_c, slot_d):
            plan = [
                (0, 1, 2 * rows, rows_d, 0, own, None),
                (1, None, rows, rows_d, slot_c, other, None),
                (2, None, rows, rows_d, slot_d, other, None),
            ]
            return Matrix((2 * rows, W), text_piece(weight, rows), plan)

        get_qkv = image_pieces(qkv_planes, sub)
        a0_qkv = next(get_qkv)
        text.w_qkv = text_in(due(qkv_planes, info_f))
        ranks = due(condition_ranks(silu_f), a0_qkv)
        img_swap = queue(LZ, swap, due(image_input[0], ranks))
        img = jnp.where(native, image_input[0], img_swap)
        shard = modulation_shard(due(partial_modulation(ranks), text.w_qkv.sources[1]))
        text_tokens, text.cot = gather_texts(due((text_input[0], text_cotangent[0]), shard))
        get_first = fetch_first(ranks)
        next(get_first)
        a1_qkv, b0_qkv = get_qkv.send(shard)
        mods = both_modulations(due(modulation(shard), img_swap))
        norm_first()
        first_img, first_txt = next(get_first)
        image.w_qkv = image_in(qkv_planes, next(get_qkv))
        image.n1 = gather_group(image.normed)
        image.n1[1] = due(image.n1[1], a1_qkv, b0_qkv)
        rest = (output_weight, first_feed_weight, second_feed_weight, image_cotangent)
        _, rest = lax.optimization_barrier((image.normed, rest))
        text.w_out = Matrix(
            (wq, W),
            [output_weight, queue(LY, xf, rest[0][1], 1)],
            [(0, 1, wq, rows_d, 0, own, None), (1, None, wq, rows_d, 0, other, None)],
        )
        text.w_fc1 = text_in(rest[1])
        text.w_fc2 = text_out(rest[2], ffh, half_c, half_d)
        rest = due(rest, image.n1[1])
        output_weight, first_feed_weight, second_feed_weight, image_cotangent = rest
        flight = Stream()

        def bulk(stage, value):
            if stage == 0:
                flight.out = output_weight[0]
                flight.a_out = queue(LZ, swap, flight.out)
                flight.get_fc1 = image_pieces(first_feed_weight, sub)
                flight.a0_fc1 = next(flight.get_fc1)
            elif stage == 1:
                flight.a_out, flight.a0_fc1 = due((flight.a_out, flight.a0_fc1), value)
                b_out = queue(LY, xf, jnp.where(native, flight.out, flight.a_out), 1)
                image.w_out = Matrix(
                    (wq, W),
                    [output_weight, flight.a_out, b_out],
                    [
                        (0, 0, wq, rows_d, 0, own, 1),
                        (1, None, wq, rows_d, 0, own, 0),
                        (2, None, wq, rows_d, 0, other, None),
                    ],
                )
                flight.part_fc1 = flight.get_fc1.send(value)
                flight.get_fc2 = image_pieces(due(second_feed_weight, value), ffh)
                flight.a0_fc2 = next(flight.get_fc2)
                return [flight.a_out]
            elif stage == 2:
                image.w_fc1 = image_in(first_feed_weight, flight.get_fc1.send(value))
                return [flight.part_fc1[0]]
            elif stage == 3:
                flight.part_fc2 = flight.get_fc2.send(value)
                return [flight.part_fc1[1], flight.a0_fc2]
            else:
                image.w_fc2 = image_out(flight.get_fc2.send(value))
                image.cot = jnp.where(
                    native, image_cotangent[0], queue(LZ, swap, due(image_cotangent[0], value))
                )
                return list(flight.part_fc2) + [image.w_fc1.sources[4]]
            return []

    else:

        def bulk(stage, value):
            return []

        def place(shape, pieces, axis):
            full = jnp.zeros(shape, BF)
            for piece, offset in pieces:
                full = lax.dynamic_update_slice_in_dim(full, piece, offset, axis=axis)
            return full

        def fetch_image(weight, axis):
            rows, cols = weight.shape
            part = rows // X
            mine = lax.dynamic_slice_in_dim(weight, xi * part, part, axis=0)
            moved = gather_by(exchange(mine), xr, x_bits)
            held = place((rows, cols), [(moved[e], (xi ^ e) * part) for e in range(X)], 0)
            held = jnp.where(native, weight, held)
            full_shape = (rows * F, cols) if axis == 0 else (rows, cols * F)
            size = weight.shape[axis]
            full = place(full_shape, [(held, f * size)], axis)
            for d in range(1, F):
                full = lax.dynamic_update_slice_in_dim(full, xf(held, d), (f ^ d) * size, axis=axis)
            return full

        def fetch_text(weight, axis):
            rows, cols = weight.shape
            part = rows // R
            mine = lax.dynamic_slice_in_dim(weight, r * part, part, axis=0)
            full_shape = (rows * F, cols) if axis == 0 else (rows, cols * F)
            size = weight.shape[axis]
            full = place(full_shape, [(weight, f * size)], axis)
            for d in range(1, F):
                pieces = gather_by(xf(mine, d), xr, x_bits + [1])
                order = [0]
                for bit in x_bits + [1]:
                    order = order + [o ^ bit for o in order]
                for e in range(R):
                    start = [0, 0]
                    start[axis] = (f ^ d) * size
                    start[0] = start[0] + (r ^ order[e]) * part
                    full = lax.dynamic_update_slice(full, pieces[e], start)
            return full

        def whole(full):
            rows, cols = full.shape
            return Matrix(full.shape, [full], [(0, None, rows, cols, 0, 0, None)])

        qkv_native = query_key_value_weight.reshape(2, rows_d, 3 * wq)
        img = exchange(image_input[0])
        image.cot = exchange(image_cotangent[0])
        shard = modulation_shard(partial_modulation(condition_ranks(silu_f)))
        text_tokens, text.cot = gather_texts((text_input[0], text_cotangent[0]))
        mods = both_modulations(modulation(shard))
        _, (first_img, first_txt) = fetch_first(shard)
        norm_first()
        image.n1 = gather_group(image.normed)
        for s, k, fetch in ((image, 0, fetch_image), (text, 1, fetch_text)):
            s.w_qkv = whole(fetch(qkv_native[k], 0))
            s.w_out = whole(fetch(output_weight[k], 1))
            s.w_fc1 = whole(fetch(first_feed_weight[k], 0))
            s.w_fc2 = whole(fetch(second_feed_weight[k], 1))
    offs = jnp.stack(entries).astype(jnp.int32)
    streams = (image, text)
    for s, mod, tokens, first in (
        (image, mods[0], img, first_img),
        (text, mods[1], text_tokens, first_txt),
    ):
        s.mod, s.x = mod, tokens
        s.a_qkv, s.b_out, s.a_fc1, s.b_fc2, s.b_qkv, s.a_out, s.b_fc1, s.a_fc2 = first

    near = [0, H]
    far = [i for i in range(T) if i not in near]
    flow = near + far
    image.size, text.size = image.x.shape[0], text.x.shape[0]
    image.once, image.twice = [flow], [near, far]
    text.once = text.twice = [[0]]
    img_len = T * image.size

    def scatter_image(blocks, parts):
        placed = [None] * T
        for i, v in zip([i for part in parts for i in part], blocks):
            placed[i] = v
        return fold_chips(fold_cores(placed))

    def windows(s, array, parts):
        result, row = [], 0
        for part in parts:
            rows = len(part) * s.size
            result.append((array, row, rows))
            row += rows
        return result

    def own_part(s, v):
        return own_rows_of(v) if s is text else v

    def total(results):
        value = results[0]
        for more in results[1:]:
            value = value + more
        return value

    def blocks_out(s, part):
        return [((s.size, W), BF)] * len(part)

    def qkv_forward(s):
        s.joint, s.rank_qkv = [], []
        for part in s.twice:
            rows = len(part) * s.size
            (out,), (rank,) = project(
                qkv_forward_kernel, offs, [s.w_qkv],
                [[s.n1[i] for i in part], [s.a_qkv], [s.b_qkv]],
                [[((rows, 3 * wq), BF)], [((rows, RANK), BF)]], 0,
            )
            s.joint.append(out)
            s.rank_qkv.append(rank)

    def out_forward(s):
        rows = len(s.once[0]) * s.size
        partial, (s.rank_out,) = project(
            out_forward_kernel, offs, [s.w_out], [windows(s, s.att, s.once), [s.a_out], [s.b_out]],
            [blocks_out(s, s.once[0]), [((rows, RANK), BF)]], 0,
        )
        return partial

    def second_norm(s, branch):
        mod = s.mod
        s.br_attn = branch
        s.after = s.xf + mod[2:3] * branch
        s.hat2, s.inv2 = norm_rows(s.after)
        return (s.hat2 * (1.0 + mod[4:5]) + mod[3:4]).astype(BF)

    def mlp_forward(s):
        s.saved, partial = [], []
        for part in s.once:
            rows = len(part) * s.size
            out, *saved = project(
                mlp_forward_kernel, offs, [s.w_fc1, s.w_fc2],
                [[s.a_fc1], [s.b_fc1], [s.a_fc2], [s.b_fc2]],
                [
                    blocks_out(s, part), [((rows, ffq), BF)], [((rows, ffq), BF)],
                    [((rows, RANK), BF)], [((rows, RANK), BF)],
                ],
                0, [[s.n2[i] for i in part]], (rows, W),
            )
            partial += out
            s.saved.append([v[0] for v in saved])
        return partial

    def mlp_backward(s):
        partial, sums = [], []
        for part, (act, slope, rank1, rank2) in zip(s.once, s.saved):
            out, *more = project(
                mlp_backward_kernel, offs, [s.w_fc1, s.w_fc2],
                [
                    [act], [slope], [rank1], [rank2],
                    [s.a_fc1], [s.b_fc1], [s.a_fc2], [s.b_fc2],
                ],
                [blocks_out(s, part)] + [[((RANK, n), F32)] for n in (ffq, ffq, W, W)],
                1, [[s.gb_mlp[i] for i in part], [s.n2[i] for i in part]], (len(part) * s.size, ffq),
            )
            partial += out
            sums.append([m[0] for m in more])
        s.t_b_fc1, s.t_a_fc2, s.t_back1, s.t_in2 = [total(t) for t in zip(*sums)]
        return partial

    def second_norm_back(s, gn2):
        mod = s.mod
        s.gs_mlp = jnp.sum(own_part(s, gn2), axis=0)
        s.gc_mlp = jnp.sum(own_part(s, gn2 * s.hat2), axis=0)
        s.g_after = s.g2 + norm_back(gn2 * (1.0 + mod[4:5]), s.hat2, s.inv2)
        s.gg_attn = jnp.sum(own_part(s, s.g_after * s.br_attn), axis=0)
        return (mod[2:3] * s.g_after).astype(BF)

    def out_backward(s, gb):
        s.g_att, sums = [], []
        atts, ranks = windows(s, s.att, s.twice), windows(s, s.rank_out, s.twice)
        for part, att, rank in zip(s.twice, atts, ranks):
            rows = len(part) * s.size
            (out,), *more = project(
                out_backward_kernel, offs, [s.w_out],
                [[gb[i] for i in part], [att], [rank], [s.a_out], [s.b_out]],
                [[((rows, wq), BF)], [((RANK, W), F32)], [((RANK, wq), F32)]], 0,
            )
            s.g_att.append(out)
            sums.append([m[0] for m in more])
        s.t_back0, s.t_a_out = [total(t) for t in zip(*sums)]

    def qkv_backward(s):
        partial, (s.t_b_qkv,), (s.t_in1,) = project(
            qkv_backward_kernel, offs, [s.w_qkv],
            [windows(s, s.g_joint, s.once), [s.n1[i] for i in s.once[0]], s.rank_qkv, [s.a_qkv], [s.b_qkv]],
            [blocks_out(s, s.once[0]), [((RANK, 3 * wq), F32)], [((RANK, W), F32)]], 0,
        )
        return partial

    text.n1 = [due(text.normed, image.normed)]
    bulk(0, image.n1[1])
    qkv_forward(image)
    text.n1[0] = due(text.n1[0], image.joint[0])
    qkv_forward(text)
    arrived = bulk(1, image.joint[0])
    joints = [(j, None) for j in image.joint] + [(text.joint[0], 1), (swap(text.joint[0]), 0)]
    joints[0] = (due(joints[0][0], *arrived), None)
    attended, lse = attend_forward(offs, joints)
    attended = due(attended, *bulk(2, attended))
    image.att = attended
    img_partial = out_forward(image)
    arrived = bulk(3, img_partial[0])
    text.att = exchange(attended[img_len:])
    txt_partial = out_forward(text)
    branch, sent = scatter_image(img_partial, image.once)
    branch = due(branch, *arrived)
    txt_branch = sum_text(txt_partial[0]).astype(F32)
    normed = second_norm(image, branch)
    image.n2 = gather_group(normed)
    arrived = bulk(4, normed)
    late = image.w_fc2.sources[-1]
    image.g2 = image.cot.astype(F32) * image.live
    image.gb_mlp = gather_group(due((image.mod[5:6] * image.g2).astype(BF), image.n2[1]))
    text.n2 = [second_norm(text, txt_branch)]
    text.g2 = text.cot.astype(F32) * text.live
    text.gb_mlp = [(text.mod[5:6] * text.g2).astype(BF)]
    txt_done = mlp_forward(text)
    txt_partial = mlp_backward(text)
    txt_gn2 = sum_text(txt_partial[0]).astype(F32)
    image.n2[0] = due(image.n2[0], txt_partial)
    image.n2[1] = due(image.n2[1], *arrived)

    info_f = due(info_f, normed, late)
    info_all = gather_by(info_f, xr, [1] + x_bits)
    ids_all = info_all[:, :, W].astype(jnp.int32)
    silu_all = info_all[:, :, :W].astype(BF)
    rank_all = condition_ranks(silu_all.reshape(R * F, W))

    img_done = mlp_forward(image)
    out_backward(text, [second_norm_back(text, txt_gn2)])
    txt_grad = swap(text.g_att[0])
    image.gb_mlp[0] = due(image.gb_mlp[0], txt_grad)
    img_partial = mlp_backward(image)
    gn2, sent = scatter_image(img_partial, image.once)

    gb = second_norm_back(image, gn2)
    gb_img = gather_group(gb)
    out_backward(image, gb_img)
    img_done, txt_done = due((img_done, txt_done), gb_img[0])
    image.br_mlp, _ = scatter_image(img_done, image.once)
    text.br_mlp = lax.psum_scatter(txt_done[0], "tp", scatter_dimension=0, tiled=True).astype(F32)
    for s in streams:
        s.out = ((own_part(s, s.after) + s.mod[5:6] * s.br_mlp) * s.live).astype(BF)
        s.gg_mlp = jnp.sum(own_part(s, s.g2) * s.br_mlp, axis=0)

    def combine_input(img_cols, txt_cols, rows):
        kinds = rows[0].shape[0] // RANK
        img_cols = exchange(jnp.concatenate(img_cols, axis=1).astype(BF))
        return jnp.concatenate(
            [img_cols] + [c.astype(BF) for c in txt_cols]
            + [r[i * RANK : (i + 1) * RANK] for r in rows for i in range(kinds)],
            axis=1,
        )

    def gather_all(pieces):
        return gather_by(gather_by(pieces, xf, f_bits), xr, [1] + x_bits)

    def combine(blocks, idents):
        flat = blocks.reshape(R * F * RANK, blocks.shape[-1])
        slots = (idents.reshape(R * F, 1) * RANK + jnp.arange(RANK, dtype=jnp.int32)).reshape(1, -1)
        place_rows = (row_ids[:, None] == slots).astype(BF)
        return mm(place_rows, flat)

    def reduce_rows(img_rows, txt_rows):
        return exchange(scatter_columns(img_rows, img_steps)), scatter_columns(txt_rows, txt_steps)

    def rows_home(rows):
        kinds = rows.shape[1]
        blocks = rows.astype(BF).reshape(T, Rq, kinds, wq)
        blocks = jnp.take(blocks, jnp.bitwise_xor(z, arange_t), axis=0)
        got = jnp.stack([blocks[0]] + [xz(blocks[d], d) for d in range(1, T)])
        got = jnp.take(got, jnp.bitwise_xor(z, arange_t), axis=0)
        return jnp.moveaxis(got, 0, 2).reshape(Rq, kinds, W).astype(F32)

    ids_in_order = jnp.take(
        jnp.take(ids_all, jnp.bitwise_xor(r, jnp.arange(R, dtype=jnp.int32)), axis=0),
        jnp.bitwise_xor(f, jnp.arange(F, dtype=jnp.int32)),
        axis=1,
    )
    early_blocks = lax.all_gather(
        combine_input(
            [image.t_b_fc1, image.t_a_fc2, image.t_a_out],
            [text.t_b_fc1, text.t_a_fc2, text.t_a_out],
            reduce_rows(
                *[jnp.concatenate([s.t_back1, s.t_in2, s.t_back0], axis=0).astype(BF) for s in streams]
            ),
        ),
        ("rep", "fsdp"),
    )

    grads = [(g, None) for g in image.g_att] + [(text.g_att[0], 1), (txt_grad, 0)]
    g_joint = attend_backward(offs, joints, grads, lse)
    g_joint = due(g_joint, image.br_mlp)
    out_swap = swap(image.out)
    image.g_joint = g_joint
    text.g_joint = exchange(g_joint[img_len:])
    img_partial = qkv_backward(image)
    keep = fold_cores([img_partial[flow.index(i)] for i in range(T)])
    gn1_img, sent = fold_chips(keep)
    text.g_joint = due(text.g_joint, sent)
    txt_partial = qkv_backward(text)
    late_in = combine_input(
        [image.t_b_qkv], [text.t_b_qkv], reduce_rows(image.t_in1.astype(BF), text.t_in1.astype(BF))
    )
    late_blocks = gather_all(late_in)
    gn1_img = due(gn1_img, out_swap)
    for s, gn1 in ((image, gn1_img), (text, scatter_rows(txt_partial[0]))):
        hat1, inv1, g_after = [own_part(s, v) for v in (s.hat1, s.inv1, s.g_after)]
        s.gs_attn = jnp.sum(gn1, axis=0)
        s.gc_attn = jnp.sum(gn1 * hat1, axis=0)
        dx = g_after + norm_back(gn1 * (1.0 + s.mod[1:2]), hat1, inv1)
        s.dx = dx.astype(BF)
    gm = jnp.stack(
        reduce_rows(
            *[
                jnp.stack([s.gs_attn, s.gc_attn, s.gg_attn, s.gs_mlp, s.gc_mlp, s.gg_mlp])
                for s in streams
            ]
        )
    ).astype(BF)
    gm_f = gather_by(gm, xf, f_bits)
    gm_all = gather_by(gm_f, xr, [1] + x_bits)
    early, late = combine(early_blocks, ids_in_order), combine(late_blocks, ids_all)
    span = 2 * ffq + wq
    grad_b_fc1 = jnp.stack([early[:, 0:ffq], early[:, span : span + ffq]])
    grad_a_fc2 = jnp.stack([early[:, ffq : 2 * ffq], early[:, span + ffq : span + 2 * ffq]])
    grad_a_out = jnp.stack([early[:, 2 * ffq : span], early[:, span + 2 * ffq : 2 * span]])
    grad_b_qkv = jnp.stack([late[:, : 3 * wq], late[:, 3 * wq : 6 * wq]]).reshape(2, Rf, 3, wq)
    home = rows_home(
        jnp.concatenate([early[:, 2 * span :], late[:, 6 * wq : 8 * wq]], axis=1).reshape(Rf, 8, wq)
    )

    seqs = R * F
    match = (row_adapter[None, :] == ids_all.reshape(seqs)[:, None]).astype(F32)
    gm_seq = gm_all.reshape(seqs, 2, 6, wq)
    rank_seq = (rank_all * match[:, None, :]).astype(BF)
    grad_b_ada, gcr = [], []
    for k in range(2):
        grad_b_ada.append(
            jnp.einsum("sr,scj->rcj", rank_seq[:, k], gm_seq[:, k], preferred_element_type=F32)
        )
        gcr.append(
            jnp.einsum(
                "scj,rcj->sr", gm_seq[:, k], modulation_up_factor[k], preferred_element_type=F32
            )
            * match
        )
    grad_b_ada = jnp.stack(grad_b_ada)
    gcr = jnp.stack(gcr, axis=1)
    gcr_rel = jnp.take(
        jnp.moveaxis(gcr.reshape(seqs, 2, T, Rq), 2, 0), jnp.bitwise_xor(z, arange_t), axis=0
    )
    gcr_own = gcr_rel[0]
    for d in range(1, T):
        gcr_own = gcr_own + xz(gcr_rel[d], d)
    grad_in0 = jnp.einsum(
        "ski,sd->kid",
        gcr_own,
        silu_all.reshape(seqs, W).astype(F32),
        precision=lax.Precision.HIGHEST,
    )
    gm_pair = gm_f
    dpart = jnp.zeros((F, rows_d), F32)
    for k in range(2):
        dpart = dpart + jnp.einsum(
            "fcj,dcj->fd", gm_pair[:, k], modulation_weight[k], preferred_element_type=F32
        )
    dfull = lax.dynamic_update_slice_in_dim(jnp.zeros((F, W), F32), dpart, f * rows_d, axis=1)
    dfull = dfull + jnp.einsum(
        "fki,kid->fd",
        gcr_own.reshape(R, F, 2, Rq)[0],
        adapter_down_table[0].astype(F32),
        precision=lax.Precision.HIGHEST,
    )
    dsum = dfull[0]
    for d in range(1, F):
        dsum = dsum + xf(dfull[d], d)
    for bit in t_bits:
        dsum = dsum + xz(dsum, bit)
    sigmoid = jax.nn.sigmoid(cond)
    dcond = dsum[None] * sigmoid * (1.0 + cond * (1.0 - sigmoid))

    grad_in = jnp.stack(
        [
            grad_in0,
            jnp.stack([home[:, 6], home[:, 7]]),
            jnp.stack([home[:, 1], home[:, 4]]),
        ]
    )
    grad_back = jnp.stack(
        [jnp.stack([home[:, 2], home[:, 5]]), jnp.stack([home[:, 0], home[:, 3]])]
    )
    return (
        jnp.where(native, image.out, out_swap)[None],
        text.out[None],
        exchange(image.dx)[None],
        text.dx[None],
        dcond,
        grad_in,
        grad_back,
        grad_b_ada,
        grad_b_qkv,
        grad_b_fc1,
        grad_a_out,
        grad_a_fc2,
    )


def solution(mesh):
    tokens = P(("rep", "fsdp"), "tp", None)
    table = P(None, None, ("fsdp", "tp"), None)
    columns4 = P(None, "fsdp", None, "tp")
    columns3 = P(None, "fsdp", "tp")
    rows3 = P(None, "tp", "fsdp")
    slot = P(("rep", "fsdp"))
    in_specs = (
        tokens, tokens, P(("rep", "fsdp"), None), tokens, tokens, slot, slot,
        columns4, columns4, rows3, columns3, rows3, table, table,
        columns4, columns4, columns3, columns3, columns3,
    )
    out_specs = (
        tokens, tokens, tokens, tokens, P(("rep", "fsdp"), None),
        table, table, columns4, columns4, columns3, columns3, columns3,
    )
    sizes = (mesh.shape["rep"], mesh.shape["fsdp"], mesh.shape["tp"])
    return jax.shard_map(
        functools.partial(body, sizes), mesh=mesh, in_specs=in_specs, out_specs=out_specs, check_vma=False
    )
```
